32 devices in a mesh: gx: 8 (over z, y), gy: 4 (over x, core).
Axes of the slice: x: 2, y: 2, z: 4, core: 2. Of those that a mesh axis runs over, the one named last changes fastest.
Arguments:
- tokens: bfloat16 [25216, 768], P(('gx', 'gy')), may hold values from -6 to 6
- image_ids: int32 [25216], P(('gx', 'gy')), may hold values from 0 to 1, as said below
- rel_index: int32 [197, 197], replicated, may hold values from 0 to 731
- rel_table: bfloat16 [732, 12], replicated, may hold values from -5 to 5
- ln1_gain: bfloat16 [768], P(('gx', 'gy')), may hold values from 0.25 to 1.75
- ln1_bias: bfloat16 [768], P(('gx', 'gy')), may hold values from -1.75 to 1.75
- w_qkv: bfloat16 [768, 2304], P(('gx', 'gy')), may hold values from -0.21875 to 0.21875
- q_bias: bfloat16 [768], P(('gx', 'gy')), may hold values from -3 to 3
- v_bias: bfloat16 [768], P(('gx', 'gy')), may hold values from -3 to 3
- w_out: bfloat16 [768, 768], P(('gx', 'gy')), may hold values from -3.5 to 3.5
- out_bias: bfloat16 [768], P(('gx', 'gy')), may hold values from -1.75 to 1.75
- gamma1: bfloat16 [768], P(('gx', 'gy')), may hold values from 0.25 to 1.75
- ln2_gain: bfloat16 [768], P(('gx', 'gy')), may hold values from 0.25 to 1.75
- ln2_bias: bfloat16 [768], P(('gx', 'gy')), may hold values from -1.75 to 1.75
- w_fc1: bfloat16 [768, 3072], P(('gx', 'gy')), may hold values from -0.21875 to 0.21875
- fc1_bias: bfloat16 [3072], P(('gx', 'gy')), may hold values from -3 to 3
- w_fc2: bfloat16 [3072, 768], P(('gx', 'gy')), may hold values from -0.109375 to 0.109375
- fc2_bias: bfloat16 [768], P(('gx', 'gy')), may hold values from -1.75 to 1.75
- gamma2: bfloat16 [768], P(('gx', 'gy')), may hold values from 0.25 to 1.75
- out_grad: bfloat16 [25216, 768], P(('gx', 'gy')), may hold values from -6 to 6
Outputs:
- out_tokens: bfloat16 [25216, 768], P(('gx', 'gy'))
- tokens_grad: bfloat16 [25216, 768], P(('gx', 'gy'))
- rel_table_grad: float32 [732, 12], replicated
- ln1_gain_grad: float32 [768], P(('gx', 'gy'))
- ln1_bias_grad: float32 [768], P(('gx', 'gy'))
- w_qkv_grad: float32 [768, 2304], P(('gx', 'gy'))
- q_bias_grad: float32 [768], P(('gx', 'gy'))
- v_bias_grad: float32 [768], P(('gx', 'gy'))
- w_out_grad: float32 [768, 768], P(('gx', 'gy'))
- out_bias_grad: float32 [768], P(('gx', 'gy'))
- gamma1_grad: float32 [768], P(('gx', 'gy'))
- ln2_gain_grad: float32 [768], P(('gx', 'gy'))
- ln2_bias_grad: float32 [768], P(('gx', 'gy'))
- w_fc1_grad: float32 [768, 3072], P(('gx', 'gy'))
- fc1_bias_grad: float32 [3072], P(('gx', 'gy'))
- w_fc2_grad: float32 [3072, 768], P(('gx', 'gy'))
- fc2_bias_grad: float32 [768], P(('gx', 'gy'))
- gamma2_grad: float32 [768], P(('gx', 'gy'))
The draws below stay inside these ranges and needn't reach their ends.
Inputs may be any that keep to these rules, and one draw needn't show every extreme that they name: image_ids is constant over each image's 197 rows; different images of a sequence may carry the same id.
All inputs are finite; a program needn't handle non-finite values.
Results may differ from the reference program's by a relative error of at most 0.012.
Values may be sent and summed in bfloat16 or wider, within the bound.
A program may use at most 256 MiB of HBM per device.

```python
import math
from functools import partial
import jax
import jax.numpy as jnp
from jax import lax

D = 768
HEADS = 12
HEAD = 64
FF = 3072
PATCH = 197
TABLE = 732
IMGS = 2
SEQ_LEN = 394
TOKENS = 25216


def draw_image_ids(key, part):
    seq_total = TOKENS // SEQ_LEN
    drawn = jax.random.randint(key, (seq_total, IMGS), 0, IMGS, dtype=jnp.int32)
    first_row = lax.broadcasted_iota(jnp.int32, (seq_total, IMGS), 1)
    seq_rank = lax.broadcasted_iota(jnp.int32, (seq_total, IMGS), 0)
    chosen = jnp.where(seq_rank == 0, first_row, drawn).astype(jnp.int32)
    return jnp.repeat(chosen.reshape(-1), PATCH).astype(jnp.int32)


def place_ends(values, key, smallest, top_value):
    longest = values.shape.index(max(values.shape))
    spots = []
    for shift in (0, 1):
        where = [jax.random.randint(jax.random.fold_in(key, axis), (), 0, length) for axis, length in enumerate(values.shape)]
        where[longest] = (where[longest] + shift) % values.shape[longest]
        spots.append(tuple(where))
    return values.at[spots[0]].set(smallest).at[spots[1]].set(top_value)


def steps_of(key, shape, cuts, low, high):
    def one(axis_at, shards_of):
        draws = jax.random.uniform(jax.random.fold_in(jax.random.fold_in(key, 6), axis_at), (shards_of,), jnp.float32, low / len(cuts), high / len(cuts))
        return jnp.repeat(jnp.exp(draws), shape[axis_at] // shards_of).reshape((-1,) + (1,) * (len(shape) - axis_at - 1))

    loudness = one(*cuts[0])
    for cut in cuts[1:]:
        loudness = loudness * one(*cut)
    return loudness


def noise(key, shape, scale, reach, split=(), kind=jnp.bfloat16):
    entries = scale * jax.random.normal(key, shape, jnp.float32)
    if split:
        entries = entries * steps_of(key, shape, split, -0.22, 0.18)
    return jnp.clip(entries, -reach, reach).astype(kind)


def setup_inputs(seed: int = 0) -> dict:
    splits = jax.random.split(jax.random.key(seed), 21)
    tokens = noise(splits[0], (TOKENS, D), 1.0, 6.0, ((0, 32),))
    image_ids = draw_image_ids(jax.random.fold_in(splits[20], 71), 0)
    rel_index = place_ends(jax.random.randint(splits[2], (PATCH, PATCH), 0, TABLE), jax.random.fold_in(splits[2], 1), 0, TABLE - 1).astype(jnp.int32)
    rel_table = noise(splits[3], (TABLE, HEADS), 1.0, 5.0)
    ln1_gain = jnp.clip(1.0 + 0.15 * jax.random.normal(splits[4], (D,), jnp.float32), 0.25, 1.75).astype(jnp.bfloat16)
    ln1_bias = noise(splits[5], (D,), 0.3, 1.75, ((0, 32),))
    w_qkv = noise(splits[6], (D, 3 * D), D ** -0.5, 0.21875, ((0, 32),))
    q_bias = noise(splits[7], (D,), 0.5, 3.0, ((0, 32),))
    v_bias = noise(splits[8], (D,), 0.5, 3.0, ((0, 32),))
    w_out = noise(splits[9], (D, D), (max(1, D // PATCH)) ** -0.5, 3.5, ((0, 32),))
    out_bias = noise(splits[10], (D,), 0.3, 1.75, ((0, 32),))
    gamma1 = jnp.clip(1.0 + 0.15 * jax.random.normal(splits[11], (D,), jnp.float32), 0.25, 1.75).astype(jnp.bfloat16)
    ln2_gain = jnp.clip(1.0 + 0.15 * jax.random.normal(splits[12], (D,), jnp.float32), 0.25, 1.75).astype(jnp.bfloat16)
    ln2_bias = noise(splits[13], (D,), 0.3, 1.75, ((0, 32),))
    w_fc1 = noise(splits[14], (D, FF), D ** -0.5, 0.21875, ((0, 32),))
    fc1_bias = noise(splits[15], (FF,), 0.5, 3.0, ((0, 32),))
    w_fc2 = noise(splits[16], (FF, D), FF ** -0.5, 0.109375, ((0, 32),))
    fc2_bias = noise(splits[17], (D,), 0.3, 1.75, ((0, 32),))
    gamma2 = jnp.clip(1.0 + 0.15 * jax.random.normal(splits[18], (D,), jnp.float32), 0.25, 1.75).astype(jnp.bfloat16)
    out_grad = noise(splits[19], (TOKENS, D), 1.0, 6.0, ((0, 32),))
    return dict(tokens=tokens, image_ids=image_ids, rel_index=rel_index, rel_table=rel_table, ln1_gain=ln1_gain, ln1_bias=ln1_bias, w_qkv=w_qkv, q_bias=q_bias, v_bias=v_bias, w_out=w_out, out_bias=out_bias, gamma1=gamma1, ln2_gain=ln2_gain, ln2_bias=ln2_bias, w_fc1=w_fc1, fc1_bias=fc1_bias, w_fc2=w_fc2, fc2_bias=fc2_bias, gamma2=gamma2, out_grad=out_grad)


@jax.custom_vjp
def low(v):
    return lax.optimization_barrier(v.astype(jnp.bfloat16)).astype(jnp.float32)

@jax.custom_vjp
def low_back(v):
    return v

def low_keep(v):
    return (low(v), None)

def low_pass(kept, grad):
    return (grad,)

def back_keep(v):
    return (v, None)

def back_low(kept, grad):
    return (low(grad),)
low.defvjp(low_keep, low_pass)
low_back.defvjp(back_keep, back_low)
eps_norm = 1e-06
neg_fill = -1e+30

def normalize(rows_in, gain_vec, shift_vec):
    row_mean = lax.optimization_barrier(jnp.mean(rows_in, axis=-1, keepdims=True))
    centered = rows_in - row_mean
    variance = lax.optimization_barrier(jnp.mean(centered * centered, axis=-1, keepdims=True))
    return centered * lax.rsqrt(variance + eps_norm) * gain_vec + shift_vec

def block_forward(x_block, id_block, params, bias_seq):
    ln1_g, ln1_b, w_qkv, q_b, v_b, w_out, out_b, gam_one, ln2_g, ln2_b, w_fc1, fc1_b, w_fc2, fc2_b, gam_two = params
    highest = lax.Precision.HIGHEST
    seq_count = x_block.shape[0]
    row_count = seq_count * SEQ_LEN
    x_rows = x_block.reshape(row_count, D)
    act_one = low(normalize(x_rows, ln1_g, ln1_b))
    qkv_rows = low_back(jnp.dot(act_one, w_qkv, precision=highest))
    queries = low((qkv_rows[:, :D] + q_b) * HEAD ** (-0.5)).reshape(seq_count, SEQ_LEN, HEADS, HEAD)
    key_rows = low(qkv_rows[:, D:2 * D]).reshape(seq_count, SEQ_LEN, HEADS, HEAD)
    value_rows = low(qkv_rows[:, 2 * D:] + v_b).reshape(seq_count, SEQ_LEN, HEADS, HEAD)
    raw_scores = low_back(jnp.einsum('sihd,sjhd->shij', queries, key_rows, precision=highest))
    same_id = id_block[:, :, None] == id_block[:, None, :]
    scores = jnp.where(same_id[:, None], raw_scores + bias_seq[None], neg_fill)
    row_max = lax.optimization_barrier(jnp.max(scores, axis=-1, keepdims=True))
    expo_vals = jnp.exp(scores - row_max)
    softmax_w = expo_vals / lax.optimization_barrier(jnp.sum(expo_vals, axis=-1, keepdims=True))
    attended = jnp.einsum('shij,sjhd->sihd', low(softmax_w), value_rows, precision=highest)
    att_rows = low(low_back(attended.reshape(row_count, D)))
    branch = low_back(jnp.dot(att_rows, w_out, precision=highest)) + out_b
    residual = x_rows + gam_one * branch
    act_two = low(normalize(residual, ln2_g, ln2_b))
    pre_act = low_back(jnp.dot(act_two, w_fc1, precision=highest)) + fc1_b
    hidden = low(jax.nn.gelu(pre_act, approximate=False))
    mlp_out = low_back(jnp.dot(hidden, w_fc2, precision=highest)) + fc2_b
    return (residual + gam_two * mlp_out).reshape(seq_count, SEQ_LEN, D)

def reference(tokens, image_ids, rel_index, rel_table, ln1_gain, ln1_bias, w_qkv, q_bias, v_bias, w_out, out_bias, gamma1, ln2_gain, ln2_bias, w_fc1, fc1_bias, w_fc2, fc2_bias, gamma2, out_grad):
    weights = (ln1_gain, ln1_bias, w_qkv, q_bias, v_bias, w_out, out_bias, gamma1, ln2_gain, ln2_bias, w_fc1, fc1_bias, w_fc2, fc2_bias, gamma2)
    weights = tuple((item.astype(jnp.float32) for item in weights))
    seq_total = tokens.shape[0] // SEQ_LEN
    group_size = math.gcd(8, seq_total)
    id_groups = image_ids.reshape(seq_total // group_size, group_size, SEQ_LEN)
    image_eye = jnp.eye(IMGS, dtype=jnp.float32)

    def layer_fn(x_full, table_full, *params):
        bias_img = jnp.transpose(table_full[rel_index], (2, 0, 1))
        bias_seq = jnp.einsum('ac,hij->haicj', image_eye, bias_img).reshape(HEADS, SEQ_LEN, SEQ_LEN)
        blocks = x_full.reshape(seq_total // group_size, group_size, SEQ_LEN, D)
        step_fn = jax.checkpoint(partial(block_forward, params=params, bias_seq=bias_seq))

        def scan_step(carried, inputs):
            return (carried, step_fn(inputs[0], inputs[1]))
        stacked = lax.scan(scan_step, jnp.zeros((), jnp.float32), (blocks, id_groups))[1]
        return stacked.reshape(-1, D)
    outputs, pullback = jax.vjp(layer_fn, tokens.astype(jnp.float32), rel_table.astype(jnp.float32), *weights)
    gradients = pullback(out_grad.astype(jnp.float32))
    return (outputs.astype(jnp.bfloat16), gradients[0].astype(jnp.bfloat16), gradients[1], gradients[2], gradients[3], gradients[4], gradients[5], gradients[6], gradients[7], gradients[8], gradients[9], gradients[10], gradients[11], gradients[12], gradients[13], gradients[14], gradients[15], gradients[16])
```

```python
import functools

import jax
import jax.numpy as jnp
from jax import lax
from jax.experimental import pallas as pl
from jax.experimental.pallas import tpu as pltpu
from jax.sharding import PartitionSpec as P

D=768; HEADS=12; HEAD=64; PATCH=197; IP=208; IL=256
f32=jnp.float32; bf16=jnp.bfloat16
NEG=-1e30
def mm(a,b): return jnp.dot(a,b,preferred_element_type=f32)
def mmt(a,b): return lax.dot_general(a,b,(((1,),(1,)),((),())),preferred_element_type=f32)
def vm(): return pl.BlockSpec(memory_space=pltpu.VMEM)

def ln_parts(x):
    c=x-jnp.mean(x,axis=-1,keepdims=True)
    r=lax.rsqrt(jnp.mean(c*c,axis=-1,keepdims=True)+1e-6)
    return c*r,r

def front_kernel(ni, ids_ref, x_ref, wq_ref, tab_ref, idx_ref, vec_ref, att_ref, q_out, k_out, v_out, p_ref, bias_ref):
    pid=pl.program_id(0)
    R=ni*IP
    @pl.when(pid==0)
    def _():
        for i in range(ni):
            rows=pl.ds(i*IP,IP)
            n,_=ln_parts(x_ref[rows,:].astype(f32))
            a=(n*vec_ref[0:1,:]+vec_ref[1:2,:]).astype(bf16)
            for j in range(3):
                sl=pl.ds(j*D,D)
                o=mm(a,wq_ref[:,sl])
                if j==0: q_out[rows,:]=((o+vec_ref[2:3,:])*0.125).astype(bf16)
                if j==1: k_out[rows,:]=o.astype(bf16)
                if j==2: v_out[rows,:]=(o+vec_ref[3:4,:]).astype(bf16)
    rowi=lax.broadcasted_iota(jnp.int32,(IP,128),0)
    for h in range(2):
        for l in range(2):
            idx=idx_ref[:,pl.ds(l*128,128)]
            lo=jnp.bitwise_and(idx,127); hi=jnp.right_shift(idx,7)
            acc=jnp.zeros((IP,128),f32)
            for k in range(6):
                t=jnp.broadcast_to(tab_ref[0,h,k:k+1,:],(IP,128))
                gth=jnp.take_along_axis(t,lo,axis=1,mode="promise_in_bounds")
                acc=jnp.where(hi==k,gth,acc)
            bias_ref[h,:,pl.ds(l*128,128)]=jnp.where(rowi<PATCH,acc,NEG)
    cols=pl.ds(pl.multiple_of(pid*128,128),128)
    lane=lax.broadcasted_iota(jnp.int32,(1,128),1)
    for s in range(ni//2):
        linked=ids_ref[2*s]==ids_ref[2*s+1]
        mx=jnp.where(jnp.logical_and(lax.broadcasted_iota(jnp.int32,(IP,1),0)<PATCH,linked),0.0,NEG)
        kk=k_out[pl.ds(2*s*IP,2*IP),cols]
        vT=v_out[pl.ds(2*s*IP,2*IP),cols].T
        for a in range(2):
            rows=pl.ds((2*s+a)*IP,IP)
            q=q_out[rows,cols]
            ats=[]
            for h in range(2):
                qm=jnp.where((lane<64) if h==0 else (lane>=64),q,jnp.zeros_like(q))
                st=mmt(kk,qm)
                b=bias_ref[h,:,0:IP]
                if a==0: s0=st[:IP]+b; s1=st[IP:]+mx
                else: s0=st[:IP]+mx; s1=st[IP:]+b
                m=jnp.maximum(jnp.max(s0,axis=0,keepdims=True),jnp.max(s1,axis=0,keepdims=True))
                e0=jnp.exp(s0-m); e1=jnp.exp(s1-m)
                inv=1.0/(jnp.sum(e0,axis=0,keepdims=True)+jnp.sum(e1,axis=0,keepdims=True))
                p0=(e0*inv).astype(bf16); p1=(e1*inv).astype(bf16)
                p_ref[0,s,a,h,0,:,0:IP]=p0
                p_ref[0,s,a,h,1,:,0:IP]=p1
                v_h=vT[h*64:(h+1)*64]
                ats.append(mm(v_h[:,:IP],p0)+mm(v_h[:,IP:],p1))
            att_ref[rows,cols]=jnp.concatenate(ats,axis=0).T.astype(bf16)

def front(ids,x,wq,tab,idx,vec,ni):
    R=ni*IP
    full=lambda *s: pl.BlockSpec(s,lambda p:(0,)*len(s))
    return pl.pallas_call(functools.partial(front_kernel,ni),
        grid=(6,),
        out_shape=[jax.ShapeDtypeStruct((R,D),bf16)]*4+[jax.ShapeDtypeStruct((6,ni//2,2,2,2,IP,IL),bf16)],
        in_specs=[pl.BlockSpec(memory_space=pltpu.SMEM),full(R,D),full(D,3*D),pl.BlockSpec((1,2,6,128),lambda p:(p,0,0,0)),full(IP,IL),full(16,D)],
        out_specs=[full(R,D)]*4+[pl.BlockSpec((1,ni//2,2,2,2,IP,IL),lambda p:(p,0,0,0,0,0,0))],
        scratch_shapes=[pltpu.VMEM((2,IP,IL),f32)],
        compiler_params=pltpu.CompilerParams(vmem_limit_bytes=56<<20),name="front",
    )(ids,x,wq,tab,idx,vec)

def gelu_parts(x):
    z=x*0.7071067811865476
    e=lax.erf(z)
    cdf=0.5+0.5*e
    pdf=jnp.exp(-z*z)*0.3989422804014327
    return cdf, x*pdf

FC=256
def mlp_kernel(ni, nf, x_ref, att_ref, g_ref, wo_ref, vec_ref, w1_ref, w2_ref, b1_ref,
               out_ref, dres_ref, datt_ref, dw1_ref, dw2_ref, dwo_ref, db1_ref, dvec_ref,
               res, n2, r2, branch, act2, act2T, dmlp, mlp, dact):
    pid=pl.program_id(0)
    V=lambda k: vec_ref[k:k+1,:]
    @pl.when(pid==0)
    def _():
        sb=jnp.zeros((1,D),f32)
        for i in range(ni):
            rows=pl.ds(i*IP,IP)
            br=mm(att_ref[rows,:],wo_ref[...])+V(OUTB)
            branch[rows,:]=br
            rs=x_ref[rows,:].astype(f32)+V(GAM1)*br
            res[rows,:]=rs
            n,r=ln_parts(rs)
            n2[rows,:]=n
            r2[rows,:]=jnp.broadcast_to(r,(IP,128))
            act2[rows,:]=(n*V(LN2G)+V(LN2B)).astype(bf16)
            dm=V(GAM2)*g_ref[rows,:].astype(f32)
            sb=sb+jnp.sum(dm,axis=0,keepdims=True)
            dmlp[rows,:]=dm.astype(bf16)
        act2T[...]=act2[...].T
        dvec_ref[0:1,:]=sb
        mlp[...]=jnp.zeros_like(mlp)
        dact[...]=jnp.zeros_like(dact)
    w1=w1_ref[...]; w2=w2_ref[...]
    pre=mm(act2[...],w1)+b1_ref[...]
    cdf,xpdf=gelu_parts(pre)
    hid=(pre*cdf).astype(bf16)
    dh=mmt(dmlp[...],w2)
    dp=dh*(cdf+xpdf)
    db1_ref[...]=jnp.sum(dp,axis=0,keepdims=True)
    dpb=dp.astype(bf16)
    mlp[...]+=mm(hid,w2)
    dact[...]+=mmt(dpb,w1)
    dw1_ref[...]=mm(act2T[...],dpb).astype(bf16)
    dw2_ref[...]=mm(hid.T,dmlp[...]).astype(bf16)
    @pl.when(pid==nf-1)
    def _():
        sums=[jnp.zeros((1,D),f32) for _ in range(5)]
        for i in range(ni):
            rows=pl.ds(i*IP,IP)
            g=g_ref[rows,:].astype(f32)
            ml=mlp[rows,:]+V(FC2B)
            out_ref[rows,:]=(res[rows,:]+V(GAM2)*ml).astype(bf16)
            e=dact[rows,:]; n=n2[rows,:]
            dn=e*V(LN2G)
            dr=g+r2[rows,0:1]*(dn-jnp.mean(dn,axis=-1,keepdims=True)-n*jnp.mean(dn*n,axis=-1,keepdims=True))
            dres_ref[rows,:]=dr
            db=V(GAM1)*dr
            for k,t in enumerate((g*ml,e*n,e,dr*branch[rows,:],db)):
                sums[k]=sums[k]+jnp.sum(t,axis=0,keepdims=True)
            dbb=db.astype(bf16)
            dmlp[rows,:]=dbb
            datt_ref[rows,:]=mmt(dbb,wo_ref[...]).astype(bf16)
        for k in range(5): dvec_ref[k+1:k+2,:]=sums[k]
        dwo_ref[...]=mm(att_ref[...].T,dmlp[...]).astype(bf16)

def mlp(x,att,g,wo,vec,w1,w2,b1,ni):
    R=ni*IP; F=w1.shape[1]; nf=F//FC
    full=lambda *s: pl.BlockSpec(s,lambda p:(0,)*len(s),pipeline_mode=pl.Buffered(1))
    S=jax.ShapeDtypeStruct
    return pl.pallas_call(functools.partial(mlp_kernel,ni,nf),grid=(nf,),
        in_specs=[full(R,D)]*3+[full(D,D),full(16,D),pl.BlockSpec((D,FC),lambda p:(0,p)),pl.BlockSpec((FC,D),lambda p:(p,0)),pl.BlockSpec((1,FC),lambda p:(0,p))],
        out_shape=[S((R,D),bf16),S((R,D),f32),S((R,D),bf16),S((D,F),bf16),S((F,D),bf16),S((D,D),bf16),S((1,F),f32),S((8,D),f32)],
        out_specs=[full(R,D)]*3+[pl.BlockSpec((D,FC),lambda p:(0,p)),pl.BlockSpec((FC,D),lambda p:(p,0)),full(D,D),pl.BlockSpec((1,FC),lambda p:(0,p)),full(8,D)],
        scratch_shapes=[pltpu.VMEM((R,D),f32)]*2+[pltpu.VMEM((R,128),f32),pltpu.VMEM((R,D),f32),pltpu.VMEM((R,D),bf16),pltpu.VMEM((D,R),bf16),pltpu.VMEM((R,D),bf16)]+[pltpu.VMEM((R,D),f32)]*2,
        compiler_params=pltpu.CompilerParams(vmem_limit_bytes=60<<20),name="mlp",
    )(x,att,g,wo,vec,w1,w2,b1)

def attb_kernel(ni, q_ref,k_ref,v_ref,da_ref,p_ref, dq_ref,dk_ref,dv_ref,dimg_ref,dvec_ref):
    lane=lax.broadcasted_iota(jnp.int32,(1,128),1)
    sq=jnp.zeros((1,128),f32); sv=jnp.zeros((1,128),f32)
    for s in range(ni//2):
        srow=pl.ds(2*s*IP,2*IP)
        kk=k_ref[srow,:]; vv=v_ref[srow,:]
        kT=kk.T
        dv=jnp.zeros((2*IP,128),f32); dk=jnp.zeros((2*IP,128),f32)
        for a in range(2):
            rows=pl.ds((2*s+a)*IP,IP)
            q=q_ref[rows,:]; da=da_ref[rows,:]
            dqs=[]
            for h in range(2):
                msk=(lane<64) if h==0 else (lane>=64)
                qm=jnp.where(msk,q,jnp.zeros_like(q)); dam=jnp.where(msk,da,jnp.zeros_like(da))
                pb0=p_ref[0,s,a,h,0,:,0:IP]; pb1=p_ref[0,s,a,h,1,:,0:IP]
                dp=mmt(vv,dam)
                t0=pb0.astype(f32)*dp[:IP]; t1=pb1.astype(f32)*dp[IP:]
                dl=jnp.sum(t0,axis=0,keepdims=True)+jnp.sum(t1,axis=0,keepdims=True)
                d0=t0-pb0.astype(f32)*dl; d1=t1-pb1.astype(f32)*dl
                same=d0 if a==0 else d1
                if s==0 and a==0: dimg_ref[0,h,:,0:IP]=same
                else: dimg_ref[0,h,:,0:IP]+=same
                ds=jnp.concatenate([d0.astype(bf16),d1.astype(bf16)],axis=0)
                pb=jnp.concatenate([pb0,pb1],axis=0)
                dv=dv+mm(pb,dam)
                dk=dk+mm(ds,qm)
                dqs.append(mm(kT[h*64:(h+1)*64],ds))
            dq=jnp.concatenate(dqs,axis=0).T*0.125
            sq=sq+jnp.sum(dq,axis=0,keepdims=True)
            dq_ref[rows,:]=dq.astype(bf16)
        sv=sv+jnp.sum(dv,axis=0,keepdims=True)
        dk_ref[srow,:]=dk.astype(bf16); dv_ref[srow,:]=dv.astype(bf16)
    dimg_ref[0,:,:,IP:]=jnp.zeros((2,IP,IL-IP),f32)
    dvec_ref[0:1,:]=sq; dvec_ref[1:2,:]=sv

def attb(q,k,v,da,p,ni):
    R=ni*IP; S=jax.ShapeDtypeStruct
    col=pl.BlockSpec((R,128),lambda i:(0,i))
    return pl.pallas_call(functools.partial(attb_kernel,ni),grid=(6,),
        in_specs=[col]*4+[pl.BlockSpec((1,ni//2,2,2,2,IP,IL),lambda p:(p,0,0,0,0,0,0))],
        out_shape=[S((R,D),bf16)]*3+[S((6,2,IP,IL),f32),S((8,D),f32)],
        out_specs=[col]*3+[pl.BlockSpec((1,2,IP,IL),lambda i:(i,0,0,0)),pl.BlockSpec((8,128),lambda i:(0,i))],
        compiler_params=pltpu.CompilerParams(vmem_limit_bytes=56<<20),name="attb",
    )(q,k,v,da,p)

def qkvb_kernel(ni,x_ref,dres_ref,dq_ref,dk_ref,dv_ref,wq_ref,vec_ref,dimg_ref,idx_ref,
                dtok_ref,dw_ref,dvec_ref,dtab_ref,a1T,act1,acc):
    for i in range(ni):
        rows=pl.ds(i*IP,IP)
        n,r=ln_parts(x_ref[rows,:].astype(f32))
        act1[rows,:]=(n*vec_ref[0:1,:]+vec_ref[1:2,:]).astype(bf16)
    a1T[...]=act1[...].T
    for j,r_ in enumerate((dq_ref,dk_ref,dv_ref)):
        dw_ref[:,pl.ds(j*D,D)]=mm(a1T[...],r_[...]).astype(bf16)
    sg=jnp.zeros((1,D),f32); sb=jnp.zeros((1,D),f32)
    for i in range(ni):
        rows=pl.ds(i*IP,IP)
        e=mmt(dq_ref[rows,:],wq_ref[:,0:D])+mmt(dk_ref[rows,:],wq_ref[:,D:2*D])+mmt(dv_ref[rows,:],wq_ref[:,2*D:])
        n,r=ln_parts(x_ref[rows,:].astype(f32))
        dn=e*vec_ref[0:1,:]
        dx=dres_ref[rows,:]+r*(dn-jnp.mean(dn,axis=-1,keepdims=True)-n*jnp.mean(dn*n,axis=-1,keepdims=True))
        dtok_ref[rows,:]=dx.astype(bf16)
        sg=sg+jnp.sum(e*n,axis=0,keepdims=True); sb=sb+jnp.sum(e,axis=0,keepdims=True)
    dvec_ref[0:1,:]=sg; dvec_ref[1:2,:]=sb
    acc[...]=jnp.zeros_like(acc)
    sub8=lax.broadcasted_iota(jnp.int32,(8,IL),0)
    sub128=lax.broadcasted_iota(jnp.int32,(128,IL),0)
    def body(j,_):
        ix=idx_ref[pl.ds(j,1),:]
        lo=jnp.bitwise_and(ix,127); hi=jnp.right_shift(ix,7)
        oh=jnp.where(sub128==lo,1.0,0.0).astype(bf16)
        hm=sub8==hi
        As=[]
        for h in range(HEADS):
            d=dimg_ref[h//2,h%2,pl.ds(j,1),:]
            As.append(jnp.where(hm,jnp.broadcast_to(d,(8,IL)),0.0))
        A=jnp.concatenate(As,axis=0)
        Ah=A.astype(bf16); Al=(A-Ah.astype(f32)).astype(bf16)
        acc[...]+=mmt(Ah,oh)+mmt(Al,oh)
        return 0
    lax.fori_loop(0,PATCH,body,0)
    dtab_ref[...]=acc[...]

def qkvb(x,dres,dq,dk,dv,wq,vec,dimg,idx,ni):
    R=ni*IP; S=jax.ShapeDtypeStruct
    return pl.pallas_call(functools.partial(qkvb_kernel,ni),
        in_specs=[vm()]*9,
        out_shape=[S((R,D),bf16),S((D,3*D),bf16),S((8,D),f32),S((96,128),f32)],
        out_specs=[vm()]*4,
        scratch_shapes=[pltpu.VMEM((D,R),bf16),pltpu.VMEM((R,D),bf16),pltpu.VMEM((96,128),f32)],
        compiler_params=pltpu.CompilerParams(vmem_limit_bytes=56<<20),name="qkvb",
    )(x,dres,dq,dk,dv,wq,vec,dimg,idx)


MESH = pl.DeviceIdType.MESH
NZ, NY, NX, NC = 4, 2, 2, 2
PR, UW = 24, 768
DMA = pltpu.SemaphoreType.DMA


def place():
    gx, gy = lax.axis_index("gx"), lax.axis_index("gy")
    return gx // NY, lax.rem(gx, NY), gy // NC, lax.rem(gy, NC)


def at_place(z, y, x, c):
    return (z * NY + y, x * NC + c)


def greet():
    z, y, x, c = place()
    peers = [at_place(lax.rem(z + k, NZ), y, x, c) for k in (1, 2, 3)]
    peers += [at_place(z, y, 1 - x, c), at_place(z, 1 - y, x, c), at_place(z, y, x, 1 - c)]
    barrier = pltpu.get_barrier_semaphore()
    for t in peers:
        pl.semaphore_signal(barrier, inc=1, device_id=t, device_id_type=MESH)
    pl.semaphore_wait(barrier, len(peers))


def remote(src, dst, send, recv, to):
    return pltpu.make_async_remote_copy(src_ref=src, dst_ref=dst, send_sem=send, recv_sem=recv, device_id=to, device_id_type=MESH)


class Gather:
    def __init__(self, units, local, z_s, z_r, p_s, p_r, d_s, d_r, c_s, c_r):
        self.u = units
        self.sems = (local, z_s, z_r, p_s, p_r, d_s, d_r, c_s, c_r)
        self.pos = place()
        self.one = [None] * len(units)
        self.two = [None] * len(units)
        self.three = [None] * len(units)
        self.sib = [[] for _ in units]

    @staticmethod
    def scratch(n):
        return [DMA((n,)), DMA((n, 3)), DMA((n, 3)), DMA((n, 2)), DMA((n, 2)), DMA((n, 2)), DMA((n, 2)), DMA((n, 4)), DMA((n, 4))]

    def start(self, a):
        z, y, x, c = self.pos
        local, z_s, z_r = self.sems[:3]
        src, view = self.u[a]
        mine = pltpu.make_async_copy(src, view(z, y, x, c), local.at[a])
        mine.start()
        cps = [remote(src, view(z, y, x, c), z_s.at[a, k], z_r.at[a, k], at_place(lax.rem(z + k + 1, NZ), y, x, c)) for k in range(3)]
        for d in cps:
            d.start()
        self.one[a] = [mine] + cps

    def plane(self, a):
        z, y, x, c = self.pos
        p_s, p_r, c_s, c_r = self.sems[3], self.sems[4], self.sems[7], self.sems[8]
        for d in self.one[a]:
            d.wait()
        v = self.u[a][1](slice(None), y, x, c)
        dx = remote(v, v, p_s.at[a, 0], p_r.at[a, 0], at_place(z, y, 1 - x, c))
        dy = remote(v, v, p_s.at[a, 1], p_r.at[a, 1], at_place(z, 1 - y, x, c))
        dc = remote(v, v, c_s.at[a, 0], c_r.at[a, 0], at_place(z, y, x, 1 - c))
        for d in (dx, dy, dc):
            d.start()
        self.two[a] = (dx, dy)
        self.sib[a].append(dc)

    def diagonal(self, a):
        z, y, x, c = self.pos
        d_s, d_r, c_s, c_r = self.sems[5:9]
        for d in self.two[a]:
            d.wait()
        view = self.u[a][1]
        vx, vy = view(slice(0, 2), y, 1 - x, c), view(slice(2, 4), 1 - y, x, c)
        d1 = remote(vx, vx, d_s.at[a, 0], d_r.at[a, 0], at_place(z, 1 - y, x, c))
        d2 = remote(vy, vy, d_s.at[a, 1], d_r.at[a, 1], at_place(z, y, 1 - x, c))
        d1.start()
        d2.start()
        self.three[a] = (d1, d2)
        for k, v in ((1, view(slice(None), y, 1 - x, c)), (2, view(slice(None), 1 - y, x, c))):
            dc = remote(v, v, c_s.at[a, k], c_r.at[a, k], at_place(z, y, x, 1 - c))
            dc.start()
            self.sib[a].append(dc)

    def sibling(self, a):
        z, y, x, c = self.pos
        c_s, c_r = self.sems[7:9]
        for d in self.three[a]:
            d.wait()
        v = self.u[a][1](slice(None), 1 - y, 1 - x, c)
        dc = remote(v, v, c_s.at[a, 3], c_r.at[a, 3], at_place(z, y, x, 1 - c))
        dc.start()
        self.sib[a].append(dc)

    def finish(self, a):
        for d in self.sib[a]:
            d.wait()

    def steps(self):
        n, out, whole = len(self.u), [], {}
        for t in range(n + 3):
            if t < n:
                out.append(functools.partial(self.plane, t))
            if 0 <= t - 1 < n:
                out.append(functools.partial(self.diagonal, t - 1))
            if 0 <= t - 2 < n:
                out.append(functools.partial(self.sibling, t - 2))
            if 0 <= t - 3 < n:
                out.append(functools.partial(self.finish, t - 3))
                whole[t - 3] = len(out)
        return out, whole


class Scatter:
    def __init__(self, units, bufs, sems):
        self.u = units
        self.own, self.rc, self.rx, self.ry, self.r3, self.rz = bufs
        self.sems = sems
        self.pos = place()
        n = len(units)
        self.one, self.two, self.three, self.four = [None] * n, [None] * n, [None] * n, [None] * n

    @staticmethod
    def scratch(n):
        v = lambda *s: pltpu.VMEM((n,) + s + (PR, UW), bf16)
        bufs = [v(NZ, NY, NX), v(NZ, NY, NX), v(2, NY), v(2, NX), v(NZ), v(3)]
        return bufs, [DMA((n,)), DMA((n, 8)), DMA((n, 8))]

    def send(self, a, k, src, dst, to):
        d = remote(src, dst, self.sems[1].at[a, k], self.sems[2].at[a, k], to)
        d.start()
        return d

    def start(self, a):
        z, y, x, c = self.pos
        view = self.u[a][0]
        mine = pltpu.make_async_copy(view(slice(None), slice(None), slice(None), c), self.own.at[a], self.sems[0].at[a])
        mine.start()
        d = self.send(a, 0, view(slice(None), slice(None), slice(None), 1 - c), self.rc.at[a], at_place(z, y, x, 1 - c))
        self.one[a] = (mine, d)

    def plane(self, a):
        z, y, x, c = self.pos
        for d in self.one[a]:
            d.wait()
        own, rc = self.own.at[a], self.rc.at[a]

        @pl.loop(0, NZ)
        def _(i):
            own[i] = (own[i].astype(f32) + rc[i].astype(f32)).astype(bf16)

        self.two[a] = (
            self.send(a, 1, own.at[0:2, :, 1 - x], self.rx.at[a], at_place(z, y, 1 - x, c)),
            self.send(a, 2, own.at[2:4, 1 - y, :], self.ry.at[a], at_place(z, 1 - y, x, c)),
        )

    def diagonal(self, a):
        z, y, x, c = self.pos
        for d in self.two[a]:
            d.wait()
        own, rx, ry = self.own.at[a], self.rx.at[a], self.ry.at[a]
        for i in range(2):
            for j in range(2):
                own[i, j, x] = (own[i, j, x].astype(f32) + rx[i, j].astype(f32)).astype(bf16)
                own[2 + i, y, j] = (own[2 + i, y, j].astype(f32) + ry[i, j].astype(f32)).astype(bf16)
        r3 = self.r3.at[a]
        self.three[a] = (
            self.send(a, 3, own.at[0:2, 1 - y, x], r3.at[0:2], at_place(z, 1 - y, x, c)),
            self.send(a, 4, own.at[2:4, y, 1 - x], r3.at[2:4], at_place(z, y, 1 - x, c)),
        )

    def line(self, a):
        z, y, x, c = self.pos
        for d in self.three[a]:
            d.wait()
        own, r3 = self.own.at[a], self.r3.at[a]
        for i in range(NZ):
            own[i, y, x] = (own[i, y, x].astype(f32) + r3[i].astype(f32)).astype(bf16)
        self.four[a] = []
        for k in range(3):
            to = lax.rem(z + k + 1, NZ)
            self.four[a].append(self.send(a, 5 + k, own.at[to, y, x], self.rz.at[a, k], at_place(to, y, x, c)))

    def finish(self, a):
        z, y, x, c = self.pos
        for d in self.four[a]:
            d.wait()
        own, rz = self.own.at[a], self.rz.at[a]
        total = own[z, y, x].astype(f32)
        for k in range(3):
            total = total + rz[k].astype(f32)
        self.u[a][1][...] = total

    def steps(self, units=None):
        todo = list(range(len(self.u)) if units is None else units)
        out = []
        for t in range(len(todo) + 3):
            for back, f in enumerate((self.plane, self.diagonal, self.line, self.finish)):
                if 0 <= t - back < len(todo):
                    out.append(functools.partial(f, todo[t - back]))
        return out


class Total:
    def __init__(self, ref, bufs, s_s, s_r, base=0):
        self.ref, self.bufs, self.s, self.r, self.base = ref, bufs, s_s, s_r, base
        z, y, x, c = place()
        near = z + 1 - 2 * lax.rem(z, 2)
        self.to = [at_place(z, y, x, 1 - c), at_place(z, y, 1 - x, c), at_place(z, 1 - y, x, c), at_place(near, y, x, c), at_place(lax.rem(z + 2, NZ), y, x, c)]
        self.d = [None] * 5

    @staticmethod
    def scratch(rows):
        return [pltpu.VMEM((5, rows, D), f32), DMA((5,)), DMA((5,))]

    def send(self, k):
        self.d[k] = remote(self.ref, self.bufs.at[k], self.s.at[k], self.r.at[k], self.to[k])
        self.d[k].start()

    def take(self, k):
        self.d[k].wait()
        self.ref[...] = self.ref[...] + self.bufs[k]

    def steps(self):
        out = [functools.partial(self.send, 0)]
        for k in range(5):
            out.append(functools.partial(self.take, k))
            if k < 4:
                out.append(functools.partial(self.send, k + 1))
        return out


def gather_units(shards, gathered):
    units = []

    def cols(src, dst, j):
        sl = pl.ds(j * UW, UW)
        units.append((src.at[:, sl], lambda z, y, x, c: dst.at[z, y, x, c, :, sl]))

    def rows(src, dst, j):
        sl = pl.ds(j * PR, PR)
        units.append((src.at[sl, :], lambda z, y, x, c: dst.at[z, y, x, c, sl, :]))

    (small, wq, wo, w1, w2), (gsmall, gq, go, g1, g2) = shards, gathered
    units.append((small, lambda z, y, x, c: gsmall.at[z, y, x, c]))
    for j in range(3):
        cols(wq, gq, j)
    cols(wo, go, 0)
    for j in range(4):
        rows(w2, g2, j)
    for j in range(4):
        cols(w1, g1, j)
    return units


def gather_kernel(*refs):
    shards, gathered, sems = refs[:5], refs[5:10], refs[10:]
    greet()
    g = Gather(gather_units(shards, gathered), *sems)
    for a in range(len(g.u)):
        g.start(a)
    for f in g.steps()[0]:
        f()


def gather_all(small, wq, wo, w1, w2):
    shape = lambda a: jax.ShapeDtypeStruct((NZ, NY, NX, NC) + a.shape, a.dtype)
    args = (small, wq, wo, w1, w2)
    hbm = pl.BlockSpec(memory_space=pl.ANY)
    return pl.pallas_call(gather_kernel, out_shape=[shape(a) for a in args], in_specs=[hbm] * 5, out_specs=[hbm] * 5,
                          scratch_shapes=Gather.scratch(13),
                          compiler_params=pltpu.CompilerParams(collective_id=0, has_side_effects=True), name="gather")(*args)


def scatter_units(grads, outs):
    units = []

    def cols(src, out, j):
        sl = pl.ds(j * UW, UW)
        units.append((lambda z, y, x, c: src.at[z, y, x, c, :, sl], out.at[:, sl]))

    def rows(src, out, j):
        sl = pl.ds(j * PR, PR)
        units.append((lambda z, y, x, c: src.at[z, y, x, c, sl, :], out.at[sl, :]))

    (dq, do, d1, d2), (oq, oo, o1, o2) = grads, outs
    for j in range(4):
        cols(d1, o1, j)
    for j in range(4):
        rows(d2, o2, j)
    cols(do, oo, 0)
    for j in range(3):
        cols(dq, oq, j)
    return units


def scatter_kernel(*refs):
    grads, small = refs[:4], refs[4]
    outs, small_out = refs[5:9], refs[9]
    bufs, sems, tot = refs[10:16], refs[16:19], refs[19:22]
    small_out[...] = small[...]
    greet()
    s = Scatter(scatter_units(grads, outs), bufs, sems)
    for a in range(len(s.u)):
        s.start(a)
    t = Total(small_out, *tot)
    a_steps, b_steps = s.steps(), t.steps()
    for i, f in enumerate(a_steps):
        f()
        if i % 2 == 1 and i // 2 < len(b_steps):
            b_steps[i // 2]()
    for f in b_steps[len(a_steps) // 2:]:
        f()


def scatter_all(dq, do, d1, d2, small):
    hbm = pl.BlockSpec(memory_space=pl.ANY)
    outs = [jax.ShapeDtypeStruct((a.shape[-2], a.shape[-1]), f32) for a in (dq, do, d1, d2)] + [jax.ShapeDtypeStruct(small.shape, f32)]
    bufs, sems = Scatter.scratch(12)
    return pl.pallas_call(scatter_kernel, out_shape=outs, in_specs=[hbm] * 4 + [vm()], out_specs=[vm()] * 5,
                          scratch_shapes=bufs + sems + Total.scratch(small.shape[0]),
                          compiler_params=pltpu.CompilerParams(collective_id=1, has_side_effects=True, vmem_limit_bytes=56 << 20), name="scatter")(dq, do, d1, d2, small)


AXES = ("gx", "gy")
NVEC = 10
(LN1G, LN1B, QB, VB, OUTB, GAM1, LN2G, LN2B, FC2B, GAM2) = range(NVEC)


def pad_rows(a, ni):
    return jnp.pad(a.reshape(ni, PATCH, D), ((0, 0), (0, IP - PATCH), (0, 0))).reshape(ni * IP, D)


def unpad_rows(a, ni):
    return a.reshape(ni, IP, D)[:, :PATCH].reshape(ni * PATCH, D)


def local(tokens, image_ids, rel_index, rel_table, ln1_gain, ln1_bias, w_qkv, q_bias, v_bias, w_out, out_bias, gamma1,
          ln2_gain, ln2_bias, w_fc1, fc1_bias, w_fc2, fc2_bias, gamma2, out_grad):
    ni = tokens.shape[0] // PATCH
    n_dev = D // ln1_gain.shape[0]
    me = lax.axis_index("gx") * lax.axis_size("gy") + lax.axis_index("gy")
    own = (lax.axis_size("gx"), lax.axis_size("gy"), ln1_gain.shape[0]) == (NZ * NY, NX * NC, PR)
    gather = lambda a: lax.all_gather(a, AXES, axis=0, tiled=True)
    small = jnp.concatenate([ln1_gain, ln1_bias, q_bias, v_bias, out_bias, gamma1, ln2_gain, ln2_bias, fc2_bias, gamma2, fc1_bias])
    if own:
        small = jnp.pad(small.astype(f32).reshape(1, -1), ((0, 7), (0, 384 - small.shape[0])))
        gathered = gather_all(small, w_qkv, w_out, w_fc1, w_fc2)
        small = gathered[0].reshape(n_dev, 8, 384)[:, 0, : (NVEC + fc1_bias.shape[0] // (D // n_dev)) * (D // n_dev)]
        wq, wo, w1, w2 = (a.reshape(n_dev * a.shape[-2], a.shape[-1]) for a in gathered[1:])
    else:
        wq, wo, w1, w2 = gather(w_qkv), gather(w_out), gather(w_fc1), gather(w_fc2)
        small = lax.all_gather(small, AXES, axis=0, tiled=False).reshape(n_dev, -1).astype(f32)
    per = D // n_dev
    vec = jnp.pad(jnp.transpose(small[:, : NVEC * per].reshape(n_dev, NVEC, per), (1, 0, 2)).reshape(NVEC, D), ((0, 16 - NVEC), (0, 0)))
    b1 = small[:, NVEC * per :].reshape(1, -1)

    x = pad_rows(tokens, ni)
    g = pad_rows(out_grad, ni)
    ids = image_ids.reshape(ni, PATCH)[:, 0]
    table_rows = rel_table.shape[0]
    tab = jnp.pad(rel_table.astype(f32).T, ((0, 0), (0, 768 - table_rows))).reshape(6, 2, 6, 128)
    idx = jnp.pad(rel_index.T, ((0, IP - PATCH), (0, IL - PATCH)))

    att, q, k, v, p = front(ids, x, wq, tab, idx, vec, ni)
    out, dres, datt, dw1, dw2, dwo, db1, dvec = mlp(x, att, g, wo, vec, w1, w2, b1, ni)
    dq, dk, dv, dimg, dvec2 = attb(q, k, v, datt, p, ni)
    dtok, dwq, dvec3, dtab = qkvb(x, dres, dq, dk, dv, wq, vec, dimg, idx, ni)

    split = lambda a: a.reshape((NZ, NY, NX, NC, -1, a.shape[-1]))
    scatter = lambda a: lax.psum_scatter(a.astype(f32), AXES, scatter_dimension=0, tiled=True)
    rows = jnp.concatenate([dvec3[0:2], dvec2[0:2], dvec[5:6], dvec[4:5], dvec[2:4], dvec[0:1], dvec[1:2], db1.reshape(-1, D), dtab.reshape(-1, D)])
    if own:
        gq, go, g1, g2, total = scatter_all(split(dwq), split(dwo), split(dw1), split(dw2), jnp.pad(rows, ((0, 32 - rows.shape[0]), (0, 0))))
        total = total[: rows.shape[0]]
    else:
        gq, go, g1, g2 = (scatter(a) for a in (dwq, dwo, dw1, dw2))
        total = lax.psum(rows, AXES)
    sl = [lax.dynamic_slice(total[i], (me * per,), (per,)) for i in range(NVEC)]
    nb = db1.shape[1] // D
    db1_own = lax.dynamic_slice(total[NVEC : NVEC + nb].reshape(-1), (me * per * nb,), (per * nb,))
    table_grad = total[NVEC + nb :].reshape(HEADS, 1024)[:, :table_rows].T
    return (unpad_rows(out, ni), unpad_rows(dtok, ni), table_grad, sl[LN1G], sl[LN1B], gq, sl[QB], sl[VB], go,
            sl[OUTB], sl[GAM1], sl[LN2G], sl[LN2B], g1, db1_own, g2, sl[FC2B], sl[GAM2])


def solution(mesh):
    rows, vecs, none = P(AXES, None), P(AXES), P()
    return jax.shard_map(
        local,
        mesh=mesh,
        in_specs=(rows, vecs, none, none, vecs, vecs, rows, vecs, vecs, rows, vecs, vecs, vecs, vecs, rows, vecs, rows, vecs, vecs, rows),
        out_specs=(rows, rows, none, vecs, vecs, rows, vecs, vecs, rows, vecs, vecs, vecs, vecs, rows, vecs, rows, vecs, vecs),
        check_vma=False,
    )
```

```python
import functools

import jax
import jax.numpy as jnp
from jax import lax
from jax.experimental import pallas as pl
from jax.experimental.pallas import tpu as pltpu
from jax.sharding import PartitionSpec as P

D=768; HEADS=12; HEAD=64; PATCH=197; IP=208; IL=256
f32=jnp.float32; bf16=jnp.bfloat16
NEG=-1e30
def mm(a,b): return jnp.dot(a,b,preferred_element_type=f32)
def mmt(a,b): return lax.dot_general(a,b,(((1,),(1,)),((),())),preferred_element_type=f32)
def vm(): return pl.BlockSpec(memory_space=pltpu.VMEM)

def ln_parts(x):
    c=x-jnp.mean(x,axis=-1,keepdims=True)
    r=lax.rsqrt(jnp.mean(c*c,axis=-1,keepdims=True)+1e-6)
    return c*r,r

def front_kernel(ni, ids_ref, x_ref, wq_ref, tab_ref, idx_ref, vec_ref, att_ref, q_out, k_out, v_out, p_ref, bias_ref):
    pid=pl.program_id(0)
    R=ni*IP
    @pl.when(pid==0)
    def _():
        for i in range(ni):
            rows=pl.ds(i*IP,IP)
            n,_=ln_parts(x_ref[rows,:].astype(f32))
            a=(n*vec_ref[0:1,:]+vec_ref[1:2,:]).astype(bf16)
            for j in range(3):
                sl=pl.ds(j*D,D)
                o=mm(a,wq_ref[:,sl])
                if j==0: q_out[rows,:]=((o+vec_ref[2:3,:])*0.125).astype(bf16)
                if j==1: k_out[rows,:]=o.astype(bf16)
                if j==2: v_out[rows,:]=(o+vec_ref[3:4,:]).astype(bf16)
    rowi=lax.broadcasted_iota(jnp.int32,(IP,128),0)
    for h in range(2):
        for l in range(2):
            idx=idx_ref[:,pl.ds(l*128,128)]
            lo=jnp.bitwise_and(idx,127); hi=jnp.right_shift(idx,7)
            acc=jnp.zeros((IP,128),f32)
            for k in range(6):
                t=jnp.broadcast_to(tab_ref[0,h,k:k+1,:],(IP,128))
                gth=jnp.take_along_axis(t,lo,axis=1,mode="promise_in_bounds")
                acc=jnp.where(hi==k,gth,acc)
            bias_ref[h,:,pl.ds(l*128,128)]=jnp.where(rowi<PATCH,acc,NEG)
    cols=pl.ds(pl.multiple_of(pid*128,128),128)
    lane=lax.broadcasted_iota(jnp.int32,(1,128),1)
    for s in range(ni//2):
        linked=ids_ref[2*s]==ids_ref[2*s+1]
        mx=jnp.where(jnp.logical_and(lax.broadcasted_iota(jnp.int32,(IP,1),0)<PATCH,linked),0.0,NEG)
        kk=k_out[pl.ds(2*s*IP,2*IP),cols]
        vT=v_out[pl.ds(2*s*IP,2*IP),cols].T
        for a in range(2):
            rows=pl.ds((2*s+a)*IP,IP)
            q=q_out[rows,cols]
            ats=[]
            for h in range(2):
                qm=jnp.where((lane<64) if h==0 else (lane>=64),q,jnp.zeros_like(q))
                st=mmt(kk,qm)
                b=bias_ref[h,:,0:IP]
                if a==0: s0=st[:IP]+b; s1=st[IP:]+mx
                else: s0=st[:IP]+mx; s1=st[IP:]+b
                m=jnp.maximum(jnp.max(s0,axis=0,keepdims=True),jnp.max(s1,axis=0,keepdims=True))
                e0=jnp.exp(s0-m); e1=jnp.exp(s1-m)
                inv=1.0/(jnp.sum(e0,axis=0,keepdims=True)+jnp.sum(e1,axis=0,keepdims=True))
                p0=(e0*inv).astype(bf16); p1=(e1*inv).astype(bf16)
                p_ref[0,s,a,h,0,:,0:IP]=p0
                p_ref[0,s,a,h,1,:,0:IP]=p1
                v_h=vT[h*64:(h+1)*64]
                ats.append(mm(v_h[:,:IP],p0)+mm(v_h[:,IP:],p1))
            att_ref[rows,cols]=jnp.concatenate(ats,axis=0).T.astype(bf16)

def front(ids,x,wq,tab,idx,vec,ni):
    R=ni*IP
    full=lambda *s: pl.BlockSpec(s,lambda p:(0,)*len(s))
    return pl.pallas_call(functools.partial(front_kernel,ni),
        grid=(6,),
        out_shape=[jax.ShapeDtypeStruct((R,D),bf16)]*4+[jax.ShapeDtypeStruct((6,ni//2,2,2,2,IP,IL),bf16)],
        in_specs=[pl.BlockSpec(memory_space=pltpu.SMEM),full(R,D),full(D,3*D),pl.BlockSpec((1,2,6,128),lambda p:(p,0,0,0)),full(IP,IL),full(16,D)],
        out_specs=[full(R,D)]*4+[pl.BlockSpec((1,ni//2,2,2,2,IP,IL),lambda p:(p,0,0,0,0,0,0))],
        scratch_shapes=[pltpu.VMEM((2,IP,IL),f32)],
        compiler_params=pltpu.CompilerParams(vmem_limit_bytes=56<<20),name="front",
    )(ids,x,wq,tab,idx,vec)

def gelu_parts(x):
    z=x*0.7071067811865476
    e=lax.erf(z)
    cdf=0.5+0.5*e
    pdf=jnp.exp(-z*z)*0.3989422804014327
    return cdf, x*pdf

FC=256
def mlp_kernel(ni, nf, x_ref, att_ref, g_ref, wo_ref, vec_ref, w1_ref, w2_ref, b1_ref,
               out_ref, dres_ref, datt_ref, dw1_ref, dw2_ref, dwo_ref, db1_ref, dvec_ref,
               res, n2, r2, branch, act2, act2T, dmlp, mlp, dact):
    pid=pl.program_id(0)
    V=lambda k: vec_ref[k:k+1,:]
    @pl.when(pid==0)
    def _():
        sb=jnp.zeros((1,D),f32)
        for i in range(ni):
            rows=pl.ds(i*IP,IP)
            br=mm(att_ref[rows,:],wo_ref[...])+V(OUTB)
            branch[rows,:]=br
            rs=x_ref[rows,:].astype(f32)+V(GAM1)*br
            res[rows,:]=rs
            n,r=ln_parts(rs)
            n2[rows,:]=n
            r2[rows,:]=jnp.broadcast_to(r,(IP,128))
            act2[rows,:]=(n*V(LN2G)+V(LN2B)).astype(bf16)
            dm=V(GAM2)*g_ref[rows,:].astype(f32)
            sb=sb+jnp.sum(dm,axis=0,keepdims=True)
            dmlp[rows,:]=dm.astype(bf16)
        act2T[...]=act2[...].T
        dvec_ref[0:1,:]=sb
        mlp[...]=jnp.zeros_like(mlp)
        dact[...]=jnp.zeros_like(dact)
    w1=w1_ref[...]; w2=w2_ref[...]
    pre=mm(act2[...],w1)+b1_ref[...]
    cdf,xpdf=gelu_parts(pre)
    hid=(pre*cdf).astype(bf16)
    dh=mmt(dmlp[...],w2)
    dp=dh*(cdf+xpdf)
    db1_ref[...]=jnp.sum(dp,axis=0,keepdims=True)
    dpb=dp.astype(bf16)
    mlp[...]+=mm(hid,w2)
    dact[...]+=mmt(dpb,w1)
    dw1_ref[...]=mm(act2T[...],dpb).astype(bf16)
    dw2_ref[...]=mm(hid.T,dmlp[...]).astype(bf16)
    @pl.when(pid==nf-1)
    def _():
        sums=[jnp.zeros((1,D),f32) for _ in range(5)]
        for i in range(ni):
            rows=pl.ds(i*IP,IP)
            g=g_ref[rows,:].astype(f32)
            ml=mlp[rows,:]+V(FC2B)
            out_ref[rows,:]=(res[rows,:]+V(GAM2)*ml).astype(bf16)
            e=dact[rows,:]; n=n2[rows,:]
            dn=e*V(LN2G)
            dr=g+r2[rows,0:1]*(dn-jnp.mean(dn,axis=-1,keepdims=True)-n*jnp.mean(dn*n,axis=-1,keepdims=True))
            dres_ref[rows,:]=dr
            db=V(GAM1)*dr
            for k,t in enumerate((g*ml,e*n,e,dr*branch[rows,:],db)):
                sums[k]=sums[k]+jnp.sum(t,axis=0,keepdims=True)
            dbb=db.astype(bf16)
            dmlp[rows,:]=dbb
            datt_ref[rows,:]=mmt(dbb,wo_ref[...]).astype(bf16)
        for k in range(5): dvec_ref[k+1:k+2,:]=sums[k]
        dwo_ref[...]=mm(att_ref[...].T,dmlp[...]).astype(bf16)

def mlp(x,att,g,wo,vec,w1,w2,b1,ni):
    R=ni*IP; F=w1.shape[1]; nf=F//FC
    full=lambda *s: pl.BlockSpec(s,lambda p:(0,)*len(s),pipeline_mode=pl.Buffered(1))
    S=jax.ShapeDtypeStruct
    return pl.pallas_call(functools.partial(mlp_kernel,ni,nf),grid=(nf,),
        in_specs=[full(R,D)]*3+[full(D,D),full(16,D),pl.BlockSpec((D,FC),lambda p:(0,p)),pl.BlockSpec((FC,D),lambda p:(p,0)),pl.BlockSpec((1,FC),lambda p:(0,p))],
        out_shape=[S((R,D),bf16),S((R,D),f32),S((R,D),bf16),S((D,F),bf16),S((F,D),bf16),S((D,D),bf16),S((1,F),f32),S((8,D),f32)],
        out_specs=[full(R,D)]*3+[pl.BlockSpec((D,FC),lambda p:(0,p)),pl.BlockSpec((FC,D),lambda p:(p,0)),full(D,D),pl.BlockSpec((1,FC),lambda p:(0,p)),full(8,D)],
        scratch_shapes=[pltpu.VMEM((R,D),f32)]*2+[pltpu.VMEM((R,128),f32),pltpu.VMEM((R,D),f32),pltpu.VMEM((R,D),bf16),pltpu.VMEM((D,R),bf16),pltpu.VMEM((R,D),bf16)]+[pltpu.VMEM((R,D),f32)]*2,
        compiler_params=pltpu.CompilerParams(vmem_limit_bytes=60<<20),name="mlp",
    )(x,att,g,wo,vec,w1,w2,b1)

def attb_kernel(ni, q_ref,k_ref,v_ref,da_ref,p_ref, dq_ref,dk_ref,dv_ref,dimg_ref,dvec_ref):
    lane=lax.broadcasted_iota(jnp.int32,(1,128),1)
    sq=jnp.zeros((1,128),f32); sv=jnp.zeros((1,128),f32)
    for s in range(ni//2):
        srow=pl.ds(2*s*IP,2*IP)
        kk=k_ref[srow,:]; vv=v_ref[srow,:]
        kT=kk.T
        dv=jnp.zeros((2*IP,128),f32); dk=jnp.zeros((2*IP,128),f32)
        for a in range(2):
            rows=pl.ds((2*s+a)*IP,IP)
            q=q_ref[rows,:]; da=da_ref[rows,:]
            dqs=[]
            for h in range(2):
                msk=(lane<64) if h==0 else (lane>=64)
                qm=jnp.where(msk,q,jnp.zeros_like(q)); dam=jnp.where(msk,da,jnp.zeros_like(da))
                pb0=p_ref[0,s,a,h,0,:,0:IP]; pb1=p_ref[0,s,a,h,1,:,0:IP]
                dp=mmt(vv,dam)
                t0=pb0.astype(f32)*dp[:IP]; t1=pb1.astype(f32)*dp[IP:]
                dl=jnp.sum(t0,axis=0,keepdims=True)+jnp.sum(t1,axis=0,keepdims=True)
                d0=t0-pb0.astype(f32)*dl; d1=t1-pb1.astype(f32)*dl
                same=d0 if a==0 else d1
                if s==0 and a==0: dimg_ref[0,h,:,0:IP]=same
                else: dimg_ref[0,h,:,0:IP]+=same
                ds=jnp.concatenate([d0.astype(bf16),d1.astype(bf16)],axis=0)
                pb=jnp.concatenate([pb0,pb1],axis=0)
                dv=dv+mm(pb,dam)
                dk=dk+mm(ds,qm)
                dqs.append(mm(kT[h*64:(h+1)*64],ds))
            dq=jnp.concatenate(dqs,axis=0).T*0.125
            sq=sq+jnp.sum(dq,axis=0,keepdims=True)
            dq_ref[rows,:]=dq.astype(bf16)
        sv=sv+jnp.sum(dv,axis=0,keepdims=True)
        dk_ref[srow,:]=dk.astype(bf16); dv_ref[srow,:]=dv.astype(bf16)
    dimg_ref[0,:,:,IP:]=jnp.zeros((2,IP,IL-IP),f32)
    dvec_ref[0:1,:]=sq; dvec_ref[1:2,:]=sv

def attb(q,k,v,da,p,ni):
    R=ni*IP; S=jax.ShapeDtypeStruct
    col=pl.BlockSpec((R,128),lambda i:(0,i))
    return pl.pallas_call(functools.partial(attb_kernel,ni),grid=(6,),
        in_specs=[col]*4+[pl.BlockSpec((1,ni//2,2,2,2,IP,IL),lambda p:(p,0,0,0,0,0,0))],
        out_shape=[S((R,D),bf16)]*3+[S((6,2,IP,IL),f32),S((8,D),f32)],
        out_specs=[col]*3+[pl.BlockSpec((1,2,IP,IL),lambda i:(i,0,0,0)),pl.BlockSpec((8,128),lambda i:(0,i))],
        compiler_params=pltpu.CompilerParams(vmem_limit_bytes=56<<20),name="attb",
    )(q,k,v,da,p)

def qkvb_kernel(ni,x_ref,dres_ref,dq_ref,dk_ref,dv_ref,wq_ref,vec_ref,dimg_ref,idx_ref,
                dtok_ref,dw_ref,dvec_ref,dtab_ref,a1T,act1,acc):
    for i in range(ni):
        rows=pl.ds(i*IP,IP)
        n,r=ln_parts(x_ref[rows,:].astype(f32))
        act1[rows,:]=(n*vec_ref[0:1,:]+vec_ref[1:2,:]).astype(bf16)
    a1T[...]=act1[...].T
    for j,r_ in enumerate((dq_ref,dk_ref,dv_ref)):
        dw_ref[:,pl.ds(j*D,D)]=mm(a1T[...],r_[...]).astype(bf16)
    sg=jnp.zeros((1,D),f32); sb=jnp.zeros((1,D),f32)
    for i in range(ni):
        rows=pl.ds(i*IP,IP)
        e=mmt(dq_ref[rows,:],wq_ref[:,0:D])+mmt(dk_ref[rows,:],wq_ref[:,D:2*D])+mmt(dv_ref[rows,:],wq_ref[:,2*D:])
        n,r=ln_parts(x_ref[rows,:].astype(f32))
        dn=e*vec_ref[0:1,:]
        dx=dres_ref[rows,:]+r*(dn-jnp.mean(dn,axis=-1,keepdims=True)-n*jnp.mean(dn*n,axis=-1,keepdims=True))
        dtok_ref[rows,:]=dx.astype(bf16)
        sg=sg+jnp.sum(e*n,axis=0,keepdims=True); sb=sb+jnp.sum(e,axis=0,keepdims=True)
    dvec_ref[0:1,:]=sg; dvec_ref[1:2,:]=sb
    acc[...]=jnp.zeros_like(acc)
    sub8=lax.broadcasted_iota(jnp.int32,(8,IL),0)
    sub128=lax.broadcasted_iota(jnp.int32,(128,IL),0)
    def body(j,_):
        ix=idx_ref[pl.ds(j,1),:]
        lo=jnp.bitwise_and(ix,127); hi=jnp.right_shift(ix,7)
        oh=jnp.where(sub128==lo,1.0,0.0).astype(bf16)
        hm=sub8==hi
        As=[]
        for h in range(HEADS):
            d=dimg_ref[h//2,h%2,pl.ds(j,1),:]
            As.append(jnp.where(hm,jnp.broadcast_to(d,(8,IL)),0.0))
        A=jnp.concatenate(As,axis=0)
        Ah=A.astype(bf16); Al=(A-Ah.astype(f32)).astype(bf16)
        acc[...]+=mmt(Ah,oh)+mmt(Al,oh)
        return 0
    lax.fori_loop(0,PATCH,body,0)
    dtab_ref[...]=acc[...]

def qkvb(x,dres,dq,dk,dv,wq,vec,dimg,idx,ni):
    R=ni*IP; S=jax.ShapeDtypeStruct
    return pl.pallas_call(functools.partial(qkvb_kernel,ni),
        in_specs=[vm()]*9,
        out_shape=[S((R,D),bf16),S((D,3*D),bf16),S((8,D),f32),S((96,128),f32)],
        out_specs=[vm()]*4,
        scratch_shapes=[pltpu.VMEM((D,R),bf16),pltpu.VMEM((R,D),bf16),pltpu.VMEM((96,128),f32)],
        compiler_params=pltpu.CompilerParams(vmem_limit_bytes=56<<20),name="qkvb",
    )(x,dres,dq,dk,dv,wq,vec,dimg,idx)


AXES = ("gx", "gy")
NVEC = 10
(LN1G, LN1B, QB, VB, OUTB, GAM1, LN2G, LN2B, FC2B, GAM2) = range(NVEC)

MESH = pl.DeviceIdType.MESH
NZ, NY, NX, NC = 4, 2, 2, 2
PR, UW = 24, 768
DMA = pltpu.SemaphoreType.DMA
ALL = slice(None)


def place():
    gx, gy = lax.axis_index("gx"), lax.axis_index("gy")
    return gx // NY, lax.rem(gx, NY), gy // NC, lax.rem(gy, NC)


def at_place(z, y, x, c):
    return (z * NY + y, x * NC + c)


def neighbours():
    z, y, x, c = place()
    line = [at_place(lax.rem(z + k, NZ), y, x, c) for k in (1, 2, 3)]
    return line, at_place(z, y, 1 - x, c), at_place(z, 1 - y, x, c), at_place(z, y, x, 1 - c)


def greet():
    line, nx, ny, nc = neighbours()
    barrier = pltpu.get_barrier_semaphore()
    for t in line + [nx, ny, nc]:
        pl.semaphore_signal(barrier, inc=1, device_id=t, device_id_type=MESH)
    pl.semaphore_wait(barrier, NZ + 2)


def remote(src, dst, send, recv, to):
    return pltpu.make_async_remote_copy(src_ref=src, dst_ref=dst, send_sem=send, recv_sem=recv, device_id=to, device_id_type=MESH)


class Gather:
    def __init__(self, units, local, z_s, z_r, p_s, p_r, d_s, d_r, c_s, c_r):
        self.u = units
        self.local, self.z_s, self.z_r, self.p_s, self.p_r, self.d_s, self.d_r, self.c_s, self.c_r = local, z_s, z_r, p_s, p_r, d_s, d_r, c_s, c_r
        self.pos = place()
        self.line, self.nx, self.ny, self.nc = neighbours()

    @staticmethod
    def scratch(n):
        return [DMA((n,)), DMA((n, 3)), DMA((n, 3)), DMA((n, 2)), DMA((n, 2)), DMA((n, 2)), DMA((n, 2)), DMA((n, 4)), DMA((n, 4))]

    def first(self, a):
        z, y, x, c = self.pos
        src, view, plane = self.u[a]
        to = view(z if plane is None else plane, y, x, c)
        mine = pltpu.make_async_copy(src, to, self.local.at[a])
        return [mine] + [remote(src, to, self.z_s.at[a, k], self.z_r.at[a, k if plane is None else 0], self.line[k]) for k in range(3)]

    def start(self, a):
        plane = self.u[a][2]
        if plane is None:
            for d in self.first(a):
                d.start()
        else:
            @pl.when(self.pos[0] == plane)
            def _():
                for d in self.first(a):
                    d.start()

    def arrive(self, a):
        plane = self.u[a][2]
        if plane is None:
            for d in self.first(a):
                d.wait()
        else:
            @pl.when(self.pos[0] == plane)
            def _():
                mine, *sent = self.first(a)
                mine.wait()
                for d in sent:
                    d.wait_send()

            @pl.when(self.pos[0] != plane)
            def _():
                z, y, x, c = self.pos
                src, view, plane = self.u[a]
                remote(src, view(plane, y, x, c), self.z_s.at[a, 0], self.z_r.at[a, 0], self.line[0]).wait_recv()

    def to_plane(self, a):
        z, y, x, c = self.pos
        _, view, plane = self.u[a]
        v = view(ALL if plane is None else plane, y, x, c)
        return (remote(v, v, self.p_s.at[a, 0], self.p_r.at[a, 0], self.nx), remote(v, v, self.p_s.at[a, 1], self.p_r.at[a, 1], self.ny))

    def to_diagonal(self, a):
        z, y, x, c = self.pos
        _, view, plane = self.u[a]
        if plane is None:
            vx, vy = view(slice(0, 2), y, 1 - x, c), view(slice(2, 4), 1 - y, x, c)
        else:
            vx, vy = view(plane, y, 1 - x, c), view(plane, 1 - y, x, c)
            half = vx.shape[0] // 2
            vx, vy = vx.at[pl.ds(0, half)], vy.at[pl.ds(half, half)]
        return (remote(vx, vx, self.d_s.at[a, 0], self.d_r.at[a, 0], self.ny), remote(vy, vy, self.d_s.at[a, 1], self.d_r.at[a, 1], self.nx))

    def to_sibling(self, a, k):
        z, y, x, c = self.pos
        _, view, plane = self.u[a]
        v = view(ALL if plane is None else plane, (y, y, 1 - y, 1 - y)[k], (x, 1 - x, x, 1 - x)[k], c)
        return remote(v, v, self.c_s.at[a, k], self.c_r.at[a, k], self.nc)

    def plane(self, a):
        self.arrive(a)
        for d in self.to_plane(a):
            d.start()
        self.to_sibling(a, 0).start()

    def diagonal(self, a):
        for d in self.to_plane(a):
            d.wait()
        for d in self.to_diagonal(a):
            d.start()
        self.to_sibling(a, 1).start()
        self.to_sibling(a, 2).start()

    def sibling(self, a):
        for d in self.to_diagonal(a):
            d.wait()
        self.to_sibling(a, 3).start()

    def finish(self, a):
        for k in range(4):
            self.to_sibling(a, k).wait()

    def groups(self):
        n = len(self.u)
        return [[functools.partial(f, t - back) for back, f in enumerate((self.plane, self.diagonal, self.sibling, self.finish)) if 0 <= t - back < n]
                for t in range(n + 3)]


class Scatter:
    def __init__(self, units, bufs, sems):
        self.u = units
        self.own, self.rc, self.rx, self.ry, self.r3, self.rz = bufs
        self.sems = sems
        self.pos = place()
        self.line, self.nx, self.ny, self.nc = neighbours()
        self.line_z = [lax.rem(self.pos[0] + k, NZ) for k in (1, 2, 3)]

    @staticmethod
    def scratch(n):
        v = lambda *s: pltpu.VMEM((n,) + s + (PR, UW), bf16)
        return [v(NZ, NY, NX), v(NZ, NY, NX), v(2, NY), v(2, NX), v(NZ), v(3)], [DMA((n,)), DMA((n, 8)), DMA((n, 8))]

    def copy(self, a, k, src, dst, to):
        return remote(src, dst, self.sems[1].at[a, k], self.sems[2].at[a, k], to)

    def one(self, a):
        c = self.pos[3]
        view = self.u[a][0]
        mine = pltpu.make_async_copy(view(ALL, ALL, ALL, c), self.own.at[a], self.sems[0].at[a])
        return mine, self.copy(a, 0, view(ALL, ALL, ALL, 1 - c), self.rc.at[a], self.nc)

    def two(self, a):
        z, y, x, c = self.pos
        own = self.own.at[a]
        return (self.copy(a, 1, own.at[0:2, :, 1 - x], self.rx.at[a], self.nx), self.copy(a, 2, own.at[2:4, 1 - y, :], self.ry.at[a], self.ny))

    def three(self, a):
        z, y, x, c = self.pos
        own, r3 = self.own.at[a], self.r3.at[a]
        return (self.copy(a, 3, own.at[0:2, 1 - y, x], r3.at[0:2], self.ny), self.copy(a, 4, own.at[2:4, y, 1 - x], r3.at[2:4], self.nx))

    def four(self, a):
        z, y, x, c = self.pos
        own = self.own.at[a]
        return [self.copy(a, 5 + k, own.at[self.line_z[k], y, x], self.rz.at[a, k], self.line[k]) for k in range(3)]

    def start(self, a):
        for d in self.one(a):
            d.start()

    def plane(self, a):
        for d in self.one(a):
            d.wait()
        own, rc = self.own.at[a], self.rc.at[a]

        @pl.loop(0, NZ)
        def _(i):
            own[i] = (own[i].astype(f32) + rc[i].astype(f32)).astype(bf16)
        for d in self.two(a):
            d.start()

    def diagonal(self, a):
        z, y, x, c = self.pos
        for d in self.two(a):
            d.wait()
        own, rx, ry = self.own.at[a], self.rx.at[a], self.ry.at[a]
        for i in range(2):
            for j in range(2):
                own[i, j, x] = (own[i, j, x].astype(f32) + rx[i, j].astype(f32)).astype(bf16)
                own[2 + i, y, j] = (own[2 + i, y, j].astype(f32) + ry[i, j].astype(f32)).astype(bf16)
        for d in self.three(a):
            d.start()

    def along(self, a):
        z, y, x, c = self.pos
        for d in self.three(a):
            d.wait()
        own, r3 = self.own.at[a], self.r3.at[a]
        for i in range(NZ):
            own[i, y, x] = (own[i, y, x].astype(f32) + r3[i].astype(f32)).astype(bf16)
        for d in self.four(a):
            d.start()

    def finish(self, a):
        z, y, x, c = self.pos
        for d in self.four(a):
            d.wait()
        own, rz = self.own.at[a], self.rz.at[a]
        total = own[z, y, x].astype(f32)
        for k in range(3):
            total = total + rz[k].astype(f32)
        self.u[a][1][...] = total

    def groups(self):
        n = len(self.u)
        return [[functools.partial(f, t - back) for back, f in enumerate((self.plane, self.diagonal, self.along, self.finish)) if 0 <= t - back < n]
                for t in range(n + 3)]


class Total:
    def __init__(self, ref, bufs, s_s, s_r):
        self.ref, self.bufs, self.s, self.r = ref, bufs, s_s, s_r
        z, y, x, c = place()
        near = z + 1 - 2 * lax.rem(z, 2)
        self.to = [at_place(z, y, x, 1 - c), at_place(z, y, 1 - x, c), at_place(z, 1 - y, x, c), at_place(near, y, x, c), at_place(lax.rem(z + 2, NZ), y, x, c)]

    @staticmethod
    def scratch(rows):
        return [pltpu.VMEM((5, rows, D), f32), DMA((5,)), DMA((5,))]

    def copy(self, k):
        return remote(self.ref, self.bufs.at[k], self.s.at[k], self.r.at[k], self.to[k])

    def start(self):
        self.copy(0).start()

    def step(self, k):
        self.copy(k).wait()
        self.ref[...] = self.ref[...] + self.bufs[k]
        if k < 4:
            self.copy(k + 1).start()


def columns(src, j):
    return src.at[:, pl.ds(j * UW, UW)]


def gather_units(shards, gathered):
    (small, wq, wo, w1, w2), (gsmall, gq, go, g1, g2) = shards, gathered
    cols = lambda src, dst, j: (columns(src, j), lambda z, y, x, c: dst.at[z, y, x, c, :, pl.ds(j * UW, UW)], None)
    units = [(small, lambda z, y, x, c: gsmall.at[z, y, x, c], None)]
    units += [cols(wq, gq, j) for j in range(3)] + [cols(wo, go, 0)]
    for j in range(NZ):
        units += [(w2, lambda z, y, x, c: g2.at[z, y, x, c], j), cols(w1, g1, j)]
    return units


def scatter_units(grads, outs):
    (dq, do, d1, d2), (oq, oo, o1, o2) = grads, outs
    cols = lambda src, out, j: (lambda z, y, x, c: src.at[z, y, x, c, :, pl.ds(j * UW, UW)], columns(out, j))
    rows = lambda src, out, j: (lambda z, y, x, c: src.at[z, y, x, c, pl.ds(j * PR, PR), :], out.at[pl.ds(j * PR, PR), :])
    return [cols(d1, o1, j) for j in range(4)] + [rows(d2, o2, j) for j in range(4)] + [cols(do, oo, 0)] + [cols(dq, oq, j) for j in range(3)]


A_PAIR_PLAN = [(1, 7), (3, 8), (5, 9)]
A_MID_PLAN = [10]
A_CHUNK_PLAN = [(0, 11), (1, 12), (2, 13), (4, 14), (6, 15)]


def spread(base, k, part, per):
    rows = lax.broadcasted_iota(jnp.int32, (part.shape[0], D), 0)
    lanes = lax.broadcasted_iota(jnp.int32, (part.shape[0], D), 1)
    full = mm(part, jnp.where(base == k, 1.0, 0.0).astype(bf16))
    return lambda first: jnp.sum(jnp.where(rows == first + lanes // per, full, 0.0), axis=0, keepdims=True)


def forward_pair(ni, p, ids_ref, vec, tab, idxT, q_s, k_s, v_s, att_s, bias_s, put):
    rowi = lax.broadcasted_iota(jnp.int32, (IP, 128), 0)
    for h in range(2):
        for l in range(2):
            idx = idxT[:, pl.ds(l * 128, 128)]
            lo, hi = jnp.bitwise_and(idx, 127), jnp.right_shift(idx, 7)
            acc = jnp.zeros((IP, 128), f32)
            for k in range(6):
                t = jnp.broadcast_to(tab[2 * p + h, k:k + 1, :], (IP, 128))
                acc = jnp.where(hi == k, jnp.take_along_axis(t, lo, axis=1, mode="promise_in_bounds"), acc)
            bias_s[h, :, pl.ds(l * 128, 128)] = jnp.where(rowi < PATCH, acc, NEG)
    cols = pl.ds(pl.multiple_of(p * 128, 128), 128)
    lane = lax.broadcasted_iota(jnp.int32, (1, 128), 1)
    for s in range(ni // 2):
        linked = ids_ref[2 * s * PATCH] == ids_ref[(2 * s + 1) * PATCH]
        mx = jnp.where(jnp.logical_and(lax.broadcasted_iota(jnp.int32, (IP, 1), 0) < PATCH, linked), 0.0, NEG)
        kk = k_s[pl.ds(2 * s * IP, 2 * IP), cols]
        vT = v_s[pl.ds(2 * s * IP, 2 * IP), cols].T
        for a in range(2):
            rows = pl.ds((2 * s + a) * IP, IP)
            q = q_s[rows, cols]
            ats = []
            for h in range(2):
                qm = jnp.where((lane < 64) if h == 0 else (lane >= 64), q, jnp.zeros_like(q))
                st = mmt(kk, qm)
                b = bias_s[h, :, 0:IP]
                s0, s1 = (st[:IP] + b, st[IP:] + mx) if a == 0 else (st[:IP] + mx, st[IP:] + b)
                m = jnp.maximum(jnp.max(s0, axis=0, keepdims=True), jnp.max(s1, axis=0, keepdims=True))
                e0, e1 = jnp.exp(s0 - m), jnp.exp(s1 - m)
                inv = 1.0 / (jnp.sum(e0, axis=0, keepdims=True) + jnp.sum(e1, axis=0, keepdims=True))
                p0, p1 = (e0 * inv).astype(bf16), (e1 * inv).astype(bf16)
                put(s, a, h, 0, p0)
                put(s, a, h, 1, p1)
                v_h = vT[h * 64:(h + 1) * 64]
                ats.append(mm(v_h[:, :IP], p0) + mm(v_h[:, IP:], p1))
            att_s[rows, cols] = jnp.concatenate(ats, axis=0).T.astype(bf16)


def at_step(i, plan):
    for when, steps in plan.items():
        @pl.when(i == when)
        def _(steps=steps):
            for f in steps:
                f()


def fused_a_kernel(ni, nf, ids_ref, tok_ref, g_ref, tab_ref, idx_ref, small_ref, wq_ref, wo_ref, w1_ref, w2_ref,
                   out_ref, x_out, q_s, k_s, v_s, dres_ref, datt_ref, idx_out, dvec_ref, db1_ref, dwo_ref, vec,
                   wq_out, p_out, dw1_out, dw2_out,
                   gs, gq, go, g1, g2, tab, square, bias_s, att_s, gp, act, actT, dmlp, res, n2, branch, mlp, r2,
                   p_st, w1_st, w2_st, b1, p_sem, w_sem, q_sem, *sems):
    R = ni * IP
    dact = dres_ref
    greet()
    ga = Gather(gather_units((small_ref, wq_ref, wo_ref, w1_ref, w2_ref), (gs, gq, go, g1, g2)), *sems)
    for a in range(len(ga.u)):
        ga.start(a)
    groups = ga.groups()
    def padded(src, dst):
        res[pl.ds(0, ni * PATCH), :] = src[...].astype(f32)
        for i in range(ni):
            dst[pl.ds(i * IP, PATCH), :] = res[pl.ds(i * PATCH, PATCH), :].astype(bf16)
            dst[pl.ds(i * IP + PATCH, IP - PATCH), :] = jnp.zeros((IP - PATCH, D), bf16)
    padded(tok_ref, x_out)
    padded(g_ref, gp)
    square[...] = jnp.zeros_like(square)
    square[0:tab_ref.shape[0], 0:HEADS] = tab_ref[...].astype(f32)
    turned = square[:, 0:128].T
    for h in range(HEADS):
        for k in range(6):
            tab[h, k:k + 1, :] = turned[h:h + 1, k * 128:(k + 1) * 128]
    square[0:PATCH, 0:PATCH] = idx_ref[...].astype(f32)
    idx_out[...] = square[0:IL, 0:IL].T[0:IP].astype(jnp.int32)
    for i in range(ni):
        rows = pl.ds(i * IP, IP)
        n2[rows, :], _ = ln_parts(x_out[rows, :].astype(f32))
    for t in range(4):
        for f in groups[t]:
            f()
    n_small = NZ * NY * NX * NC
    flat = gs.reshape(n_small * 8, 384)
    part = jnp.concatenate([flat[8 * d:8 * d + 1, :] for d in range(n_small)], axis=0).astype(bf16)
    per = D // n_small
    base = lax.broadcasted_iota(jnp.int32, (384, D), 0) - lax.rem(lax.broadcasted_iota(jnp.int32, (384, D), 1), per)
    for k in range(NVEC):
        vec[k:k + 1, :] = spread(base, k * per, part, per)(0)
    V = lambda k: vec[k:k + 1, :]
    for i in range(ni):
        rows = pl.ds(i * IP, IP)
        act[rows, :] = (n2[rows, :] * V(LN1G) + V(LN1B)).astype(bf16)
    for j, dst in enumerate((q_s, k_s, v_s)):
        for f in groups[4 + j]:
            f()
        w = gq[:, :, :, :, :, j * D:(j + 1) * D].reshape(D, D)
        for i in range(ni):
            rows = pl.ds(i * IP, IP)
            o = mm(act[rows, :], w)
            if j == 0:
                o = (o + V(QB)) * HEAD ** -0.5
            if j == 2:
                o = o + V(VB)
            dst[rows, :] = o.astype(bf16)
    keep = pltpu.make_async_copy(gq, wq_out, q_sem)
    keep.start()
    fper = small_ref.shape[1]
    base1 = lax.broadcasted_iota(jnp.int32, (384, D), 0) - lax.rem(lax.broadcasted_iota(jnp.int32, (384, D), 1), 4 * per)
    sp = spread(base1, NVEC * per, part, 4 * per)
    for j in range(nf * FC // D):
        line = sp(j * (D // (4 * per)))
        for i in range(D // FC):
            b1[j * (D // FC) + i, 0:1, :] = line[:, i * FC:(i + 1) * FC]

    def pair(p, carry):
        slot = lax.rem(p, 2)
        st = p_st.at[slot]
        cp = pltpu.make_async_copy(st, p_out.at[p], p_sem.at[slot])

        @pl.when(p >= 2)
        def _():
            pltpu.make_async_copy(st, p_out.at[p], p_sem.at[slot]).wait()

        def put(s, a, h, b, v):
            st[s, a, h, b, :, 0:IP] = v
        forward_pair(ni, p, ids_ref, vec, tab, idx_out, q_s, k_s, v_s, att_s, bias_s, put)
        cp.start()
        at_step(p, {i: groups[t] for i, t in A_PAIR_PLAN})
        return carry
    lax.fori_loop(0, HEADS // 2, pair, 0)
    for t in A_MID_PLAN:
        for f in groups[t]:
            f()

    sb = jnp.zeros((1, D), f32)
    wo = go[...].reshape(D, D)
    for i in range(ni):
        rows = pl.ds(i * IP, IP)
        br = mm(att_s[rows, :], wo) + V(OUTB)
        branch[rows, :] = br
        rs = x_out[rows, :].astype(f32) + V(GAM1) * br
        res[rows, :] = rs
        n, r = ln_parts(rs)
        n2[rows, :] = n
        r2[rows, :] = jnp.broadcast_to(r, (IP, 128))
        act[rows, :] = (n * V(LN2G) + V(LN2B)).astype(bf16)
        dm = V(GAM2) * gp[rows, :].astype(f32)
        sb = sb + jnp.sum(dm, axis=0, keepdims=True)
        dmlp[rows, :] = dm.astype(bf16)
    actT[...] = act[...].T
    dvec_ref[0:1, :] = sb
    mlp[...] = jnp.zeros_like(mlp)
    dact[...] = jnp.zeros_like(dact)
    g2v = g2.reshape(nf * FC, D)

    def chunk(c, carry):
        slot = lax.rem(c, 2)
        at = pl.multiple_of(c * FC, FC)
        at_step(c, {i: groups[t] for i, t in A_CHUNK_PLAN})
        w1, w2 = g1[:, :, :, :, :, pl.ds(at, FC)].reshape(D, FC), g2v[pl.ds(at, FC), :]
        cp1 = pltpu.make_async_copy(w1_st.at[slot], dw1_out.at[:, pl.ds(at, FC)], w_sem.at[0, slot])
        cp2 = pltpu.make_async_copy(w2_st.at[slot], dw2_out.at[pl.ds(at, FC), :], w_sem.at[1, slot])
        pre = mm(act[...], w1) + b1[c, 0:1, :]
        cdf, xpdf = gelu_parts(pre)
        hid = (pre * cdf).astype(bf16)
        dp = mmt(dmlp[...], w2) * (cdf + xpdf)
        db1_ref[c, 0:1, :] = jnp.sum(dp, axis=0, keepdims=True)
        dpb = dp.astype(bf16)
        mlp[...] += mm(hid, w2)
        dact[...] += mmt(dpb, w1)

        @pl.when(c >= 2)
        def _():
            pltpu.make_async_copy(w1_st.at[slot], dw1_out.at[:, pl.ds(at, FC)], w_sem.at[0, slot]).wait()
            pltpu.make_async_copy(w2_st.at[slot], dw2_out.at[pl.ds(at, FC), :], w_sem.at[1, slot]).wait()
        w1_st[slot] = mm(actT[...], dpb).astype(bf16)
        w2_st[slot] = mm(hid.T, dmlp[...]).astype(bf16)
        cp1.start()
        cp2.start()
        return carry
    lax.fori_loop(0, nf, chunk, 0)

    wo = go[...].reshape(D, D)
    sums = [jnp.zeros((1, D), f32) for _ in range(5)]
    for i in range(ni):
        rows = pl.ds(i * IP, IP)
        g = gp[rows, :].astype(f32)
        ml = mlp[rows, :] + V(FC2B)
        mlp[pl.ds(i * PATCH, PATCH), :] = (res[rows, :] + V(GAM2) * ml)[:PATCH]
        e, n = dact[rows, :], n2[rows, :]
        dn = e * V(LN2G)
        dr = g + r2[rows, 0:1] * (dn - jnp.mean(dn, axis=-1, keepdims=True) - n * jnp.mean(dn * n, axis=-1, keepdims=True))
        dres_ref[rows, :] = dr
        db = V(GAM1) * dr
        for k, t in enumerate((g * ml, e * n, e, dr * branch[rows, :], db)):
            sums[k] = sums[k] + jnp.sum(t, axis=0, keepdims=True)
        dbb = db.astype(bf16)
        dmlp[rows, :] = dbb
        datt_ref[rows, :] = mmt(dbb, wo).astype(bf16)
    for k in range(5):
        dvec_ref[k + 1:k + 2, :] = sums[k]
    out_ref[...] = mlp[pl.ds(0, ni * PATCH), :].astype(bf16)
    dwo_ref[...] = mm(att_s[...].T, dmlp[...]).astype(bf16)
    keep.wait()
    for slot in range(2):
        pltpu.make_async_copy(p_st.at[slot], p_out.at[0], p_sem.at[slot]).wait()
        pltpu.make_async_copy(w1_st.at[slot], dw1_out.at[:, pl.ds(0, FC)], w_sem.at[0, slot]).wait()
        pltpu.make_async_copy(w2_st.at[slot], dw2_out.at[pl.ds(0, FC), :], w_sem.at[1, slot]).wait()


def fused_a(ids, tok, g, tab, idx, small, wq, wo, w1, w2, ni):
    R, F, S = ni * IP, w1.shape[1], jax.ShapeDtypeStruct
    v, hbm = vm(), pl.BlockSpec(memory_space=pl.ANY)
    six = lambda a: pltpu.VMEM((NZ, NY, NX, NC) + a.shape, a.dtype)
    row = lambda t: pltpu.VMEM((R, D), t)
    nu = 13
    return pl.pallas_call(
        functools.partial(fused_a_kernel, ni, F // FC),
        in_specs=[pl.BlockSpec(memory_space=pltpu.SMEM), v, v, v, v, hbm, hbm, hbm, hbm, hbm],
        out_shape=[S((ni * PATCH, D), bf16)] + [S((R, D), bf16)] * 4 + [S((R, D), f32), S((R, D), bf16), S((IP, IL), jnp.int32), S((8, D), f32), S((F // FC, 8, FC), f32),
                   S((D, D), bf16), S((16, D), f32), S((NZ, NY, NX, NC) + wq.shape, bf16), S((6, ni // 2, 2, 2, 2, IP, IL), bf16), S((D, F), bf16), S((F, D), bf16)],
        out_specs=[v] * 12 + [hbm] * 4,
        scratch_shapes=[six(a) for a in (small, wq, wo, w1, w2)] + [pltpu.VMEM((HEADS, 8, 128), f32), pltpu.VMEM((D, IL), f32), pltpu.VMEM((2, IP, IL), f32), row(bf16), row(bf16),
                        row(bf16), pltpu.VMEM((D, R), bf16), row(bf16)] + [row(f32)] * 4 + [pltpu.VMEM((R, 128), f32), pltpu.VMEM((2, ni // 2, 2, 2, 2, IP, IL), bf16),
                        pltpu.VMEM((2, D, FC), bf16), pltpu.VMEM((2, FC, D), bf16), pltpu.VMEM((F // FC, 8, FC), f32), DMA((2,)), DMA((2, 2)), DMA] + Gather.scratch(nu),
        compiler_params=pltpu.CompilerParams(collective_id=2, has_side_effects=True, vmem_limit_bytes=62 << 20), name="forward_and_mlp",
    )(ids, tok, g, tab, idx, small, wq, wo, w1, w2)


def backward_pair(ni, p, kT_of, q_ref, k_ref, v_ref, da_ref, probs, dqkv, dimg, dvec):
    lane = lax.broadcasted_iota(jnp.int32, (1, 128), 1)
    cols = pl.ds(pl.multiple_of(p * 128, 128), 128)
    sq, sv = jnp.zeros((1, 128), f32), jnp.zeros((1, 128), f32)
    for s in range(ni // 2):
        srow = pl.ds(2 * s * IP, 2 * IP)
        kk, vv = k_ref[srow, cols], v_ref[srow, cols]
        kT = kk.T
        dv, dk = jnp.zeros((2 * IP, 128), f32), jnp.zeros((2 * IP, 128), f32)
        for a in range(2):
            rows = pl.ds((2 * s + a) * IP, IP)
            q, da = q_ref[rows, cols], da_ref[rows, cols]
            dqs = []
            for h in range(2):
                msk = (lane < 64) if h == 0 else (lane >= 64)
                qm, dam = jnp.where(msk, q, jnp.zeros_like(q)), jnp.where(msk, da, jnp.zeros_like(da))
                pb0, pb1 = probs(s, a, h, 0), probs(s, a, h, 1)
                dp = mmt(vv, dam)
                t0, t1 = pb0.astype(f32) * dp[:IP], pb1.astype(f32) * dp[IP:]
                dl = jnp.sum(t0, axis=0, keepdims=True) + jnp.sum(t1, axis=0, keepdims=True)
                d0, d1 = t0 - pb0.astype(f32) * dl, t1 - pb1.astype(f32) * dl
                same = d0 if a == 0 else d1
                if s == 0 and a == 0:
                    dimg[2 * p + h, :, 0:IP] = same
                else:
                    dimg[2 * p + h, :, 0:IP] += same
                ds = jnp.concatenate([d0.astype(bf16), d1.astype(bf16)], axis=0)
                dv = dv + mm(jnp.concatenate([pb0, pb1], axis=0), dam)
                dk = dk + mm(ds, qm)
                dqs.append(mm(kT[h * 64:(h + 1) * 64], ds))
            dq = jnp.concatenate(dqs, axis=0).T * HEAD ** -0.5
            sq = sq + jnp.sum(dq, axis=0, keepdims=True)
            dqkv[0][rows, cols] = dq.astype(bf16)
        sv = sv + jnp.sum(dv, axis=0, keepdims=True)
        dqkv[1][srow, cols] = dk.astype(bf16)
        dqkv[2][srow, cols] = dv.astype(bf16)
    dvec[QB:QB + 1, cols] = sq
    dvec[VB:VB + 1, cols] = sv


def table_step(t, dimg, idx_ref, acc):
    sub8 = lax.broadcasted_iota(jnp.int32, (8, IL), 0)
    sub128 = lax.broadcasted_iota(jnp.int32, (128, IL), 0)
    at = pl.multiple_of(t * 8, 8)
    ix = idx_ref[pl.ds(at, 8), :]
    lo, hi = jnp.bitwise_and(ix, 127), jnp.right_shift(ix, 7)
    ds = [dimg[h, pl.ds(at, 8), :] for h in range(HEADS)]
    left, right = [], []
    for j in range(8):
        right.append(jnp.where(sub128 == lo[j:j + 1], 1.0, 0.0).astype(bf16))
        hm = sub8 == hi[j:j + 1]
        left.append(jnp.concatenate([jnp.where(hm, jnp.broadcast_to(d[j:j + 1], (8, IL)), 0.0) for d in ds], axis=0))
    left = jnp.concatenate(left, axis=1)
    high = left.astype(bf16)
    low = (left - high.astype(f32)).astype(bf16)
    acc[...] += mmt(jnp.concatenate([high, low], axis=0), jnp.concatenate(right, axis=1))


def fused_b_kernel(ni, table_rows, dvec_a, db1, x_ref, dres, q_ref, k_ref, v_ref, da_ref, vec, idx_ref, wq_hbm, p_hbm, d1_hbm, d2_hbm, do_hbm,
                   dtok_ref, table_ref, own_vec, own_b1, oq, oo, o1, o2,
                   wq, dq, dk, dv, dimg, act, actT, dwq, acc, square, tot_a, tot_b, p_st, p_sem, w_sem, *rest):
    bufs, sems, ta, tb = rest[:6], rest[6:9], rest[9:12], rest[12:15]
    greet()
    sc = Scatter(scatter_units((dwq, do_hbm, d1_hbm, d2_hbm), (oq, oo, o1, o2)), bufs, sems)
    for a in range(9):
        sc.start(a)
    groups = sc.groups()
    load = pltpu.make_async_copy(wq_hbm, wq, w_sem)
    load.start()
    fetch = lambda p: pltpu.make_async_copy(p_hbm.at[p], p_st.at[lax.rem(p, 2)], p_sem.at[lax.rem(p, 2)])
    fetch(0).start()
    tot_a[...] = jnp.zeros_like(tot_a)
    tot_b[...] = jnp.zeros_like(tot_b)
    for k, r in ((FC2B, 0), (GAM2, 1), (LN2G, 2), (LN2B, 3), (GAM1, 4), (OUTB, 5)):
        tot_a[k:k + 1, :] = dvec_a[r:r + 1, :]
    nb = o1.shape[1] // D
    for j in range(nb):
        for i in range(D // FC):
            tot_a[NVEC + j:NVEC + j + 1, i * FC:(i + 1) * FC] = db1[j * (D // FC) + i, 0:1, :]
    dimg[...] = jnp.zeros_like(dimg)

    def pair(p, carry):
        fetch(p).wait()

        @pl.when(p + 1 < HEADS // 2)
        def _():
            fetch(p + 1).start()
        st = p_st.at[lax.rem(p, 2)]
        at_step(p, {i: groups[t] for i, t in B_PAIR_PLAN})
        backward_pair(ni, p, None, q_ref, k_ref, v_ref, da_ref, lambda s, a, h, b: st[s, a, h, b, :, 0:IP], (dq, dk, dv), dimg, tot_a)
        return carry
    lax.fori_loop(0, HEADS // 2, pair, 0)

    def run(t):
        for f in groups[t]:
            f()
    V = lambda k: vec[k:k + 1, :]
    for i in range(ni):
        rows = pl.ds(i * IP, IP)
        n, _ = ln_parts(x_ref[rows, :].astype(f32))
        act[rows, :] = (n * V(LN1G) + V(LN1B)).astype(bf16)
    actT[...] = act[...].T
    run(6)
    for j, d in enumerate((dq, dk, dv)):
        dwq[:, :, :, :, :, j * D:(j + 1) * D] = mm(actT[...], d[...]).astype(bf16).reshape(NZ, NY, NX, NC, PR, D)
        sc.start(9 + j)
        if j < 2:
            run(7 + j)
    acc[...] = jnp.zeros_like(acc)

    def table(t, carry):
        table_step(t, dimg, idx_ref, acc)
        at_step(t, {13: groups[9]})
        return carry
    lax.fori_loop(0, -(-PATCH // 8), table, 0)
    for r in range(96):
        tot_a[14 + r // 6:15 + r // 6, (r % 6) * 128:(r % 6 + 1) * 128] = acc[r:r + 1, :] + acc[96 + r:97 + r, :]
    t_a = Total(tot_a, *ta)
    t_a.start()
    run(10)
    load.wait()
    w = wq
    sg, sb = jnp.zeros((1, D), f32), jnp.zeros((1, D), f32)
    for i in range(ni):
        rows = pl.ds(i * IP, IP)
        e = mmt(dq[rows, :], w[:, 0:D]) + mmt(dk[rows, :], w[:, D:2 * D]) + mmt(dv[rows, :], w[:, 2 * D:3 * D])
        n, r = ln_parts(x_ref[rows, :].astype(f32))
        dn = e * V(LN1G)
        dx = dres[rows, :] + r * (dn - jnp.mean(dn, axis=-1, keepdims=True) - n * jnp.mean(dn * n, axis=-1, keepdims=True))
        dres[pl.ds(i * PATCH, PATCH), :] = dx[:PATCH]
        sg = sg + jnp.sum(e * n, axis=0, keepdims=True)
        sb = sb + jnp.sum(e, axis=0, keepdims=True)
    tot_b[LN1G:LN1G + 1, :] = sg
    tot_b[LN1B:LN1B + 1, :] = sb
    t_b = Total(tot_b, *tb)
    t_b.start()
    dtok_ref[...] = dres[pl.ds(0, ni * PATCH), :].astype(bf16)
    for k in range(4):
        run(11 + k)
        t_a.step(k)
        t_b.step(k)
    t_a.step(4)
    t_b.step(4)
    tot_a[LN1G:LN1B + 1, :] = tot_b[LN1G:LN1B + 1, :]

    z, y, x, c = place()
    me = ((z * NY + y) * NX + x) * NC + c
    per = D // (NZ * NY * NX * NC)
    def pick(rows, first, width):
        one = jnp.where(lax.broadcasted_iota(jnp.int32, (D, 128), 0) == first + lax.broadcasted_iota(jnp.int32, (D, 128), 1), 1.0, 0.0).astype(bf16)
        h = rows.astype(bf16)
        m = (rows - h.astype(f32)).astype(bf16)
        l = (rows - h.astype(f32) - m.astype(f32)).astype(bf16)
        return mm(h, one) + mm(m, one) + mm(l, one)
    own_vec[...] = pick(tot_a[0:16, :], me * per, per)
    wide = nb * per
    slab = me // (D // wide)
    part = pick(tot_a[NVEC:NVEC + 8, :], lax.rem(me, D // wide) * wide, wide)
    rowi = lax.broadcasted_iota(jnp.int32, (8, 128), 0)
    own_b1[...] = jnp.broadcast_to(jnp.sum(jnp.where(rowi == slab, part, 0.0), axis=0, keepdims=True), (8, 128))
    square[...] = jnp.zeros_like(square)
    for r in range(96):
        if r % 8 < 6:
            square[r // 8:r // 8 + 1, (r % 8) * 128:(r % 8 + 1) * 128] = tot_a[14 + r // 6:15 + r // 6, (r % 6) * 128:(r % 6 + 1) * 128]
    table_ref[...] = square[...].T[0:table_rows, 0:HEADS]


B_PAIR_PLAN = [(i, i) for i in range(6)]


def fused_b(dvec_a, db1, x, dres, q, k, v, da, vec, idx, wq6, p, d1, d2, do, table_rows, ni):
    R, S = ni * IP, jax.ShapeDtypeStruct
    vmem, hbm = vm(), pl.BlockSpec(memory_space=pl.ANY)
    split = lambda a: a.reshape((NZ, NY, NX, NC, -1, a.shape[-1]))
    d1, d2, do = split(d1), split(d2), split(do)
    own = lambda a: S(a.shape[-2:], f32)
    bufs, sems = Scatter.scratch(12)
    row = lambda t: pltpu.VMEM((R, D), t)
    return pl.pallas_call(
        functools.partial(fused_b_kernel, ni, table_rows),
        in_specs=[vmem] * 10 + [hbm] * 5,
        out_shape=[S((ni * PATCH, D), bf16), S((table_rows, HEADS), f32), S((16, 128), f32), S((8, 128), f32), own(wq6), own(do), own(d1), own(d2)],
        out_specs=[vmem] * 8,
        scratch_shapes=[pltpu.VMEM((D, 3 * D), bf16)] + [row(bf16)] * 3 + [pltpu.VMEM((HEADS, IP, IL), f32), row(bf16), pltpu.VMEM((D, R), bf16), pltpu.VMEM(wq6.shape, bf16),
                        pltpu.VMEM((192, 128), f32), pltpu.VMEM((128, D), f32), pltpu.VMEM((32, D), f32), pltpu.VMEM((8, D), f32),
                        pltpu.VMEM((2, ni // 2, 2, 2, 2, IP, IL), bf16), DMA((2,)), DMA] + bufs + sems + Total.scratch(32) + Total.scratch(8),
        compiler_params=pltpu.CompilerParams(collective_id=3, has_side_effects=True, vmem_limit_bytes=62 << 20), name="attention_backward",
    )(dvec_a, db1, x, dres, q, k, v, da, vec, idx, wq6.reshape(D, 3 * D), p, d1, d2, do)


def pad_rows(a, ni):
    return jnp.pad(a.reshape(ni, PATCH, D), ((0, 0), (0, IP - PATCH), (0, 0))).reshape(ni * IP, D)


def unpad_rows(a, ni):
    return a.reshape(ni, IP, D)[:, :PATCH].reshape(ni * PATCH, D)


def local(tokens, image_ids, rel_index, rel_table, ln1_gain, ln1_bias, w_qkv, q_bias, v_bias, w_out, out_bias, gamma1,
          ln2_gain, ln2_bias, w_fc1, fc1_bias, w_fc2, fc2_bias, gamma2, out_grad):
    ni = tokens.shape[0] // PATCH
    per = ln1_gain.shape[0]
    n_dev = D // per
    small = jnp.concatenate([ln1_gain, ln1_bias, q_bias, v_bias, out_bias, gamma1, ln2_gain, ln2_bias, fc2_bias, gamma2, fc1_bias])
    me = lax.axis_index("gx") * lax.axis_size("gy") + lax.axis_index("gy")
    if (lax.axis_size("gx"), lax.axis_size("gy"), per) == (NZ * NY, NX * NC, PR):
        width = small.shape[0]
        small = jnp.pad(small.astype(f32).reshape(1, -1), ((0, 7), (0, 384 - width)))
        res = fused_a(image_ids, tokens, out_grad, rel_table, rel_index, small, w_qkv, w_out, w_fc1, w_fc2, ni)
        out, x, q, k, v, dres, datt, idx, dvec, db1, dwo, vec, wq6, p, dw1, dw2 = res
        dtok, table_grad, own_vec, own_b1, gq, go, g1, g2 = fused_b(dvec, db1, x, dres, q, k, v, datt, vec, idx, wq6, p, dw1, dw2, dwo, rel_table.shape[0], ni)
        sl = [own_vec[i, :per] for i in range(NVEC)]
        return (out, dtok, table_grad, sl[LN1G], sl[LN1B], gq, sl[QB], sl[VB], go, sl[OUTB], sl[GAM1], sl[LN2G], sl[LN2B], g1,
                own_b1[0, : fc1_bias.shape[0]], g2, sl[FC2B], sl[GAM2])
    gather = lambda a: lax.all_gather(a, AXES, axis=0, tiled=True)
    wq, wo, w1, w2 = gather(w_qkv), gather(w_out), gather(w_fc1), gather(w_fc2)
    small = lax.all_gather(small, AXES, axis=0, tiled=False).reshape(n_dev, -1).astype(f32)
    vec = jnp.pad(jnp.transpose(small[:, : NVEC * per].reshape(n_dev, NVEC, per), (1, 0, 2)).reshape(NVEC, D), ((0, 16 - NVEC), (0, 0)))
    b1 = small[:, NVEC * per :].reshape(1, -1)

    x = pad_rows(tokens, ni)
    g = pad_rows(out_grad, ni)
    ids = image_ids.reshape(ni, PATCH)[:, 0]
    table_rows = rel_table.shape[0]
    tab = jnp.pad(rel_table.astype(f32).T, ((0, 0), (0, 768 - table_rows))).reshape(6, 2, 6, 128)
    idx = jnp.pad(rel_index.T, ((0, IP - PATCH), (0, IL - PATCH)))

    att, q, k, v, p = front(ids, x, wq, tab, idx, vec, ni)
    out, dres, datt, dw1, dw2, dwo, db1, dvec = mlp(x, att, g, wo, vec, w1, w2, b1, ni)
    dq, dk, dv, dimg, dvec2 = attb(q, k, v, datt, p, ni)
    dtok, dwq, dvec3, dtab = qkvb(x, dres, dq, dk, dv, wq, vec, dimg, idx, ni)

    scatter = lambda a: lax.psum_scatter(a.astype(f32), AXES, scatter_dimension=0, tiled=True)
    rows = jnp.concatenate([dvec3[0:2], dvec2[0:2], dvec[5:6], dvec[4:5], dvec[2:4], dvec[0:1], dvec[1:2], db1.reshape(-1, D), dtab.reshape(-1, D)])
    total = lax.psum(rows, AXES)
    sl = [lax.dynamic_slice(total[i], (me * per,), (per,)) for i in range(NVEC)]
    nb = db1.shape[1] // D
    db1_own = lax.dynamic_slice(total[NVEC : NVEC + nb].reshape(-1), (me * per * nb,), (per * nb,))
    table_grad = total[NVEC + nb :].reshape(HEADS, 1024)[:, :table_rows].T
    return (unpad_rows(out, ni), unpad_rows(dtok, ni), table_grad, sl[LN1G], sl[LN1B], scatter(dwq), sl[QB], sl[VB], scatter(dwo),
            sl[OUTB], sl[GAM1], sl[LN2G], sl[LN2B], scatter(dw1), db1_own, scatter(dw2), sl[FC2B], sl[GAM2])


def solution(mesh):
    rows, vecs, none = P(AXES, None), P(AXES), P()
    return jax.shard_map(
        local,
        mesh=mesh,
        in_specs=(rows, vecs, none, none, vecs, vecs, rows, vecs, vecs, rows, vecs, vecs, vecs, vecs, rows, vecs, rows, vecs, vecs, rows),
        out_specs=(rows, rows, none, vecs, vecs, rows, vecs, vecs, rows, vecs, vecs, vecs, vecs, rows, vecs, rows, vecs, vecs),
        check_vma=False,
    )
```

```python
import functools

import jax
import jax.numpy as jnp
from jax import lax
from jax.experimental import pallas as pl
from jax.experimental.pallas import tpu as pltpu
from jax.sharding import PartitionSpec as P

D=768; HEADS=12; HEAD=64; PATCH=197; IP=208; IL=256
f32=jnp.float32; bf16=jnp.bfloat16
NEG=-1e30
def mm(a,b): return jnp.dot(a,b,preferred_element_type=f32)
def mmt(a,b): return lax.dot_general(a,b,(((1,),(1,)),((),())),preferred_element_type=f32)
def vm(): return pl.BlockSpec(memory_space=pltpu.VMEM)

def ln_parts(x):
    c=x-jnp.mean(x,axis=-1,keepdims=True)
    r=lax.rsqrt(jnp.mean(c*c,axis=-1,keepdims=True)+1e-6)
    return c*r,r

def front_kernel(ni, ids_ref, x_ref, wq_ref, tab_ref, idx_ref, vec_ref, att_ref, q_out, k_out, v_out, p_ref, bias_ref):
    pid=pl.program_id(0)
    R=ni*IP
    @pl.when(pid==0)
    def _():
        for i in range(ni):
            rows=pl.ds(i*IP,IP)
            n,_=ln_parts(x_ref[rows,:].astype(f32))
            a=(n*vec_ref[0:1,:]+vec_ref[1:2,:]).astype(bf16)
            for j in range(3):
                sl=pl.ds(j*D,D)
                o=mm(a,wq_ref[:,sl])
                if j==0: q_out[rows,:]=((o+vec_ref[2:3,:])*0.125).astype(bf16)
                if j==1: k_out[rows,:]=o.astype(bf16)
                if j==2: v_out[rows,:]=(o+vec_ref[3:4,:]).astype(bf16)
    rowi=lax.broadcasted_iota(jnp.int32,(IP,128),0)
    for h in range(2):
        for l in range(2):
            idx=idx_ref[:,pl.ds(l*128,128)]
            lo=jnp.bitwise_and(idx,127); hi=jnp.right_shift(idx,7)
            acc=jnp.zeros((IP,128),f32)
            for k in range(6):
                t=jnp.broadcast_to(tab_ref[0,h,k:k+1,:],(IP,128))
                gth=jnp.take_along_axis(t,lo,axis=1,mode="promise_in_bounds")
                acc=jnp.where(hi==k,gth,acc)
            bias_ref[h,:,pl.ds(l*128,128)]=jnp.where(rowi<PATCH,acc,NEG)
    cols=pl.ds(pl.multiple_of(pid*128,128),128)
    lane=lax.broadcasted_iota(jnp.int32,(1,128),1)
    for s in range(ni//2):
        linked=ids_ref[2*s]==ids_ref[2*s+1]
        mx=jnp.where(jnp.logical_and(lax.broadcasted_iota(jnp.int32,(IP,1),0)<PATCH,linked),0.0,NEG)
        kk=k_out[pl.ds(2*s*IP,2*IP),cols]
        vT=v_out[pl.ds(2*s*IP,2*IP),cols].T
        for a in range(2):
            rows=pl.ds((2*s+a)*IP,IP)
            q=q_out[rows,cols]
            ats=[]
            for h in range(2):
                qm=jnp.where((lane<64) if h==0 else (lane>=64),q,jnp.zeros_like(q))
                st=mmt(kk,qm)
                b=bias_ref[h,:,0:IP]
                if a==0: s0=st[:IP]+b; s1=st[IP:]+mx
                else: s0=st[:IP]+mx; s1=st[IP:]+b
                m=jnp.maximum(jnp.max(s0,axis=0,keepdims=True),jnp.max(s1,axis=0,keepdims=True))
                e0=jnp.exp(s0-m); e1=jnp.exp(s1-m)
                inv=1.0/(jnp.sum(e0,axis=0,keepdims=True)+jnp.sum(e1,axis=0,keepdims=True))
                p0=(e0*inv).astype(bf16); p1=(e1*inv).astype(bf16)
                p_ref[0,s,a,h,0,:,0:IP]=p0
                p_ref[0,s,a,h,1,:,0:IP]=p1
                v_h=vT[h*64:(h+1)*64]
                ats.append(mm(v_h[:,:IP],p0)+mm(v_h[:,IP:],p1))
            att_ref[rows,cols]=jnp.concatenate(ats,axis=0).T.astype(bf16)

def front(ids,x,wq,tab,idx,vec,ni):
    R=ni*IP
    full=lambda *s: pl.BlockSpec(s,lambda p:(0,)*len(s))
    return pl.pallas_call(functools.partial(front_kernel,ni),
        grid=(6,),
        out_shape=[jax.ShapeDtypeStruct((R,D),bf16)]*4+[jax.ShapeDtypeStruct((6,ni//2,2,2,2,IP,IL),bf16)],
        in_specs=[pl.BlockSpec(memory_space=pltpu.SMEM),full(R,D),full(D,3*D),pl.BlockSpec((1,2,6,128),lambda p:(p,0,0,0)),full(IP,IL),full(16,D)],
        out_specs=[full(R,D)]*4+[pl.BlockSpec((1,ni//2,2,2,2,IP,IL),lambda p:(p,0,0,0,0,0,0))],
        scratch_shapes=[pltpu.VMEM((2,IP,IL),f32)],
        compiler_params=pltpu.CompilerParams(vmem_limit_bytes=56<<20),name="front",
    )(ids,x,wq,tab,idx,vec)

def gelu_parts(x):
    z=x*0.7071067811865476
    e=lax.erf(z)
    cdf=0.5+0.5*e
    pdf=jnp.exp(-z*z)*0.3989422804014327
    return cdf, x*pdf

FC=256
def mlp_kernel(ni, nf, x_ref, att_ref, g_ref, wo_ref, vec_ref, w1_ref, w2_ref, b1_ref,
               out_ref, dres_ref, datt_ref, dw1_ref, dw2_ref, dwo_ref, db1_ref, dvec_ref,
               res, n2, r2, branch, act2, act2T, dmlp, mlp, dact):
    pid=pl.program_id(0)
    V=lambda k: vec_ref[k:k+1,:]
    @pl.when(pid==0)
    def _():
        sb=jnp.zeros((1,D),f32)
        for i in range(ni):
            rows=pl.ds(i*IP,IP)
            br=mm(att_ref[rows,:],wo_ref[...])+V(OUTB)
            branch[rows,:]=br
            rs=x_ref[rows,:].astype(f32)+V(GAM1)*br
            res[rows,:]=rs
            n,r=ln_parts(rs)
            n2[rows,:]=n
            r2[rows,:]=jnp.broadcast_to(r,(IP,128))
            act2[rows,:]=(n*V(LN2G)+V(LN2B)).astype(bf16)
            dm=V(GAM2)*g_ref[rows,:].astype(f32)
            sb=sb+jnp.sum(dm,axis=0,keepdims=True)
            dmlp[rows,:]=dm.astype(bf16)
        act2T[...]=act2[...].T
        dvec_ref[0:1,:]=sb
        mlp[...]=jnp.zeros_like(mlp)
        dact[...]=jnp.zeros_like(dact)
    w1=w1_ref[...]; w2=w2_ref[...]
    pre=mm(act2[...],w1)+b1_ref[...]
    cdf,xpdf=gelu_parts(pre)
    hid=(pre*cdf).astype(bf16)
    dh=mmt(dmlp[...],w2)
    dp=dh*(cdf+xpdf)
    db1_ref[...]=jnp.sum(dp,axis=0,keepdims=True)
    dpb=dp.astype(bf16)
    mlp[...]+=mm(hid,w2)
    dact[...]+=mmt(dpb,w1)
    dw1_ref[...]=mm(act2T[...],dpb).astype(bf16)
    dw2_ref[...]=mm(hid.T,dmlp[...]).astype(bf16)
    @pl.when(pid==nf-1)
    def _():
        sums=[jnp.zeros((1,D),f32) for _ in range(5)]
        for i in range(ni):
            rows=pl.ds(i*IP,IP)
            g=g_ref[rows,:].astype(f32)
            ml=mlp[rows,:]+V(FC2B)
            out_ref[rows,:]=(res[rows,:]+V(GAM2)*ml).astype(bf16)
            e=dact[rows,:]; n=n2[rows,:]
            dn=e*V(LN2G)
            dr=g+r2[rows,0:1]*(dn-jnp.mean(dn,axis=-1,keepdims=True)-n*jnp.mean(dn*n,axis=-1,keepdims=True))
            dres_ref[rows,:]=dr
            db=V(GAM1)*dr
            for k,t in enumerate((g*ml,e*n,e,dr*branch[rows,:],db)):
                sums[k]=sums[k]+jnp.sum(t,axis=0,keepdims=True)
            dbb=db.astype(bf16)
            dmlp[rows,:]=dbb
            datt_ref[rows,:]=mmt(dbb,wo_ref[...]).astype(bf16)
        for k in range(5): dvec_ref[k+1:k+2,:]=sums[k]
        dwo_ref[...]=mm(att_ref[...].T,dmlp[...]).astype(bf16)

def mlp(x,att,g,wo,vec,w1,w2,b1,ni):
    R=ni*IP; F=w1.shape[1]; nf=F//FC
    full=lambda *s: pl.BlockSpec(s,lambda p:(0,)*len(s),pipeline_mode=pl.Buffered(1))
    S=jax.ShapeDtypeStruct
    return pl.pallas_call(functools.partial(mlp_kernel,ni,nf),grid=(nf,),
        in_specs=[full(R,D)]*3+[full(D,D),full(16,D),pl.BlockSpec((D,FC),lambda p:(0,p)),pl.BlockSpec((FC,D),lambda p:(p,0)),pl.BlockSpec((1,FC),lambda p:(0,p))],
        out_shape=[S((R,D),bf16),S((R,D),f32),S((R,D),bf16),S((D,F),bf16),S((F,D),bf16),S((D,D),bf16),S((1,F),f32),S((8,D),f32)],
        out_specs=[full(R,D)]*3+[pl.BlockSpec((D,FC),lambda p:(0,p)),pl.BlockSpec((FC,D),lambda p:(p,0)),full(D,D),pl.BlockSpec((1,FC),lambda p:(0,p)),full(8,D)],
        scratch_shapes=[pltpu.VMEM((R,D),f32)]*2+[pltpu.VMEM((R,128),f32),pltpu.VMEM((R,D),f32),pltpu.VMEM((R,D),bf16),pltpu.VMEM((D,R),bf16),pltpu.VMEM((R,D),bf16)]+[pltpu.VMEM((R,D),f32)]*2,
        compiler_params=pltpu.CompilerParams(vmem_limit_bytes=60<<20),name="mlp",
    )(x,att,g,wo,vec,w1,w2,b1)

def attb_kernel(ni, q_ref,k_ref,v_ref,da_ref,p_ref, dq_ref,dk_ref,dv_ref,dimg_ref,dvec_ref):
    lane=lax.broadcasted_iota(jnp.int32,(1,128),1)
    sq=jnp.zeros((1,128),f32); sv=jnp.zeros((1,128),f32)
    for s in range(ni//2):
        srow=pl.ds(2*s*IP,2*IP)
        kk=k_ref[srow,:]; vv=v_ref[srow,:]
        kT=kk.T
        dv=jnp.zeros((2*IP,128),f32); dk=jnp.zeros((2*IP,128),f32)
        for a in range(2):
            rows=pl.ds((2*s+a)*IP,IP)
            q=q_ref[rows,:]; da=da_ref[rows,:]
            dqs=[]
            for h in range(2):
                msk=(lane<64) if h==0 else (lane>=64)
                qm=jnp.where(msk,q,jnp.zeros_like(q)); dam=jnp.where(msk,da,jnp.zeros_like(da))
                pb0=p_ref[0,s,a,h,0,:,0:IP]; pb1=p_ref[0,s,a,h,1,:,0:IP]
                dp=mmt(vv,dam)
                t0=pb0.astype(f32)*dp[:IP]; t1=pb1.astype(f32)*dp[IP:]
                dl=jnp.sum(t0,axis=0,keepdims=True)+jnp.sum(t1,axis=0,keepdims=True)
                d0=t0-pb0.astype(f32)*dl; d1=t1-pb1.astype(f32)*dl
                same=d0 if a==0 else d1
                if s==0 and a==0: dimg_ref[0,h,:,0:IP]=same
                else: dimg_ref[0,h,:,0:IP]+=same
                ds=jnp.concatenate([d0.astype(bf16),d1.astype(bf16)],axis=0)
                pb=jnp.concatenate([pb0,pb1],axis=0)
                dv=dv+mm(pb,dam)
                dk=dk+mm(ds,qm)
                dqs.append(mm(kT[h*64:(h+1)*64],ds))
            dq=jnp.concatenate(dqs,axis=0).T*0.125
            sq=sq+jnp.sum(dq,axis=0,keepdims=True)
            dq_ref[rows,:]=dq.astype(bf16)
        sv=sv+jnp.sum(dv,axis=0,keepdims=True)
        dk_ref[srow,:]=dk.astype(bf16); dv_ref[srow,:]=dv.astype(bf16)
    dimg_ref[0,:,:,IP:]=jnp.zeros((2,IP,IL-IP),f32)
    dvec_ref[0:1,:]=sq; dvec_ref[1:2,:]=sv

def attb(q,k,v,da,p,ni):
    R=ni*IP; S=jax.ShapeDtypeStruct
    col=pl.BlockSpec((R,128),lambda i:(0,i))
    return pl.pallas_call(functools.partial(attb_kernel,ni),grid=(6,),
        in_specs=[col]*4+[pl.BlockSpec((1,ni//2,2,2,2,IP,IL),lambda p:(p,0,0,0,0,0,0))],
        out_shape=[S((R,D),bf16)]*3+[S((6,2,IP,IL),f32),S((8,D),f32)],
        out_specs=[col]*3+[pl.BlockSpec((1,2,IP,IL),lambda i:(i,0,0,0)),pl.BlockSpec((8,128),lambda i:(0,i))],
        compiler_params=pltpu.CompilerParams(vmem_limit_bytes=56<<20),name="attb",
    )(q,k,v,da,p)

def qkvb_kernel(ni,x_ref,dres_ref,dq_ref,dk_ref,dv_ref,wq_ref,vec_ref,dimg_ref,idx_ref,
                dtok_ref,dw_ref,dvec_ref,dtab_ref,a1T,act1,acc):
    for i in range(ni):
        rows=pl.ds(i*IP,IP)
        n,r=ln_parts(x_ref[rows,:].astype(f32))
        act1[rows,:]=(n*vec_ref[0:1,:]+vec_ref[1:2,:]).astype(bf16)
    a1T[...]=act1[...].T
    for j,r_ in enumerate((dq_ref,dk_ref,dv_ref)):
        dw_ref[:,pl.ds(j*D,D)]=mm(a1T[...],r_[...]).astype(bf16)
    sg=jnp.zeros((1,D),f32); sb=jnp.zeros((1,D),f32)
    for i in range(ni):
        rows=pl.ds(i*IP,IP)
        e=mmt(dq_ref[rows,:],wq_ref[:,0:D])+mmt(dk_ref[rows,:],wq_ref[:,D:2*D])+mmt(dv_ref[rows,:],wq_ref[:,2*D:])
        n,r=ln_parts(x_ref[rows,:].astype(f32))
        dn=e*vec_ref[0:1,:]
        dx=dres_ref[rows,:]+r*(dn-jnp.mean(dn,axis=-1,keepdims=True)-n*jnp.mean(dn*n,axis=-1,keepdims=True))
        dtok_ref[rows,:]=dx.astype(bf16)
        sg=sg+jnp.sum(e*n,axis=0,keepdims=True); sb=sb+jnp.sum(e,axis=0,keepdims=True)
    dvec_ref[0:1,:]=sg; dvec_ref[1:2,:]=sb
    acc[...]=jnp.zeros_like(acc)
    sub8=lax.broadcasted_iota(jnp.int32,(8,IL),0)
    sub128=lax.broadcasted_iota(jnp.int32,(128,IL),0)
    def body(j,_):
        ix=idx_ref[pl.ds(j,1),:]
        lo=jnp.bitwise_and(ix,127); hi=jnp.right_shift(ix,7)
        oh=jnp.where(sub128==lo,1.0,0.0).astype(bf16)
        hm=sub8==hi
        As=[]
        for h in range(HEADS):
            d=dimg_ref[h//2,h%2,pl.ds(j,1),:]
            As.append(jnp.where(hm,jnp.broadcast_to(d,(8,IL)),0.0))
        A=jnp.concatenate(As,axis=0)
        Ah=A.astype(bf16); Al=(A-Ah.astype(f32)).astype(bf16)
        acc[...]+=mmt(Ah,oh)+mmt(Al,oh)
        return 0
    lax.fori_loop(0,PATCH,body,0)
    dtab_ref[...]=acc[...]

def qkvb(x,dres,dq,dk,dv,wq,vec,dimg,idx,ni):
    R=ni*IP; S=jax.ShapeDtypeStruct
    return pl.pallas_call(functools.partial(qkvb_kernel,ni),
        in_specs=[vm()]*9,
        out_shape=[S((R,D),bf16),S((D,3*D),bf16),S((8,D),f32),S((96,128),f32)],
        out_specs=[vm()]*4,
        scratch_shapes=[pltpu.VMEM((D,R),bf16),pltpu.VMEM((R,D),bf16),pltpu.VMEM((96,128),f32)],
        compiler_params=pltpu.CompilerParams(vmem_limit_bytes=56<<20),name="qkvb",
    )(x,dres,dq,dk,dv,wq,vec,dimg,idx)


AXES = ("gx", "gy")
NVEC = 10
(LN1G, LN1B, QB, VB, OUTB, GAM1, LN2G, LN2B, FC2B, GAM2) = range(NVEC)

MESH = pl.DeviceIdType.MESH
NZ, NY, NX, NC = 4, 2, 2, 2
PR, UW = 24, 768
DMA = pltpu.SemaphoreType.DMA
ALL = slice(None)


def place():
    gx, gy = lax.axis_index("gx"), lax.axis_index("gy")
    return gx // NY, lax.rem(gx, NY), gy // NC, lax.rem(gy, NC)


def at_place(z, y, x, c):
    return (z * NY + y, x * NC + c)


def neighbours():
    z, y, x, c = place()
    line = [at_place(lax.rem(z + k, NZ), y, x, c) for k in (1, 2, 3)]
    return line, at_place(z, y, 1 - x, c), at_place(z, 1 - y, x, c), at_place(z, y, x, 1 - c)


def greet():
    line, nx, ny, nc = neighbours()
    barrier = pltpu.get_barrier_semaphore()
    for t in line + [nx, ny, nc]:
        pl.semaphore_signal(barrier, inc=1, device_id=t, device_id_type=MESH)
    pl.semaphore_wait(barrier, NZ + 2)


def remote(src, dst, send, recv, to):
    return pltpu.make_async_remote_copy(src_ref=src, dst_ref=dst, send_sem=send, recv_sem=recv, device_id=to, device_id_type=MESH)


class Gather:
    def __init__(self, units, local, z_s, z_r, p_s, p_r, d_s, d_r, c_s, c_r):
        self.u = units
        self.local, self.z_s, self.z_r, self.p_s, self.p_r, self.d_s, self.d_r, self.c_s, self.c_r = local, z_s, z_r, p_s, p_r, d_s, d_r, c_s, c_r
        self.pos = place()
        self.line, self.nx, self.ny, self.nc = neighbours()

    @staticmethod
    def scratch(n):
        return [DMA((n,)), DMA((n, 3)), DMA((n, 3)), DMA((n, 2)), DMA((n, 2)), DMA((n, 2)), DMA((n, 2)), DMA((n, 4)), DMA((n, 4))]

    def first(self, a):
        z, y, x, c = self.pos
        src, view, plane = self.u[a]
        to = view(z if plane is None else plane, y, x, c)
        mine = [] if src is None else [pltpu.make_async_copy(src, to, self.local.at[a])]
        src = to if src is None else src
        return mine + [remote(src, to, self.z_s.at[a, k], self.z_r.at[a, k if plane is None else 0], self.line[k]) for k in range(3)]

    def start(self, a):
        plane = self.u[a][2]
        if plane is None:
            for d in self.first(a):
                d.start()
        else:
            @pl.when(self.pos[0] == plane)
            def _():
                for d in self.first(a):
                    d.start()

    def arrive(self, a):
        plane = self.u[a][2]
        if plane is None:
            for d in self.first(a):
                d.wait()
        else:
            @pl.when(self.pos[0] == plane)
            def _():
                mine, *sent = self.first(a)
                mine.wait()
                for d in sent:
                    d.wait_send()

            @pl.when(self.pos[0] != plane)
            def _():
                z, y, x, c = self.pos
                src, view, plane = self.u[a]
                remote(src, view(plane, y, x, c), self.z_s.at[a, 0], self.z_r.at[a, 0], self.line[0]).wait_recv()

    def to_plane(self, a):
        z, y, x, c = self.pos
        _, view, plane = self.u[a]
        v = view(ALL if plane is None else plane, y, x, c)
        return (remote(v, v, self.p_s.at[a, 0], self.p_r.at[a, 0], self.nx), remote(v, v, self.p_s.at[a, 1], self.p_r.at[a, 1], self.ny))

    def to_diagonal(self, a):
        z, y, x, c = self.pos
        _, view, plane = self.u[a]
        if plane is None:
            vx, vy = view(slice(0, 2), y, 1 - x, c), view(slice(2, 4), 1 - y, x, c)
        else:
            vx, vy = view(plane, y, 1 - x, c), view(plane, 1 - y, x, c)
            half = vx.shape[0] // 2
            vx, vy = vx.at[pl.ds(0, half)], vy.at[pl.ds(half, half)]
        return (remote(vx, vx, self.d_s.at[a, 0], self.d_r.at[a, 0], self.ny), remote(vy, vy, self.d_s.at[a, 1], self.d_r.at[a, 1], self.nx))

    def to_sibling(self, a, k):
        z, y, x, c = self.pos
        _, view, plane = self.u[a]
        v = view(ALL if plane is None else plane, (y, y, 1 - y, 1 - y)[k], (x, 1 - x, x, 1 - x)[k], c)
        return remote(v, v, self.c_s.at[a, k], self.c_r.at[a, k], self.nc)

    def plane(self, a):
        self.arrive(a)
        for d in self.to_plane(a):
            d.start()
        self.to_sibling(a, 0).start()

    def diagonal(self, a):
        for d in self.to_plane(a):
            d.wait()
        for d in self.to_diagonal(a):
            d.start()
        self.to_sibling(a, 1).start()
        self.to_sibling(a, 2).start()

    def sibling(self, a):
        for d in self.to_diagonal(a):
            d.wait()
        self.to_sibling(a, 3).start()

    def finish(self, a):
        for k in range(4):
            self.to_sibling(a, k).wait()

    def run(self, text):
        for word in text.split():
            {"P": self.plane, "D": self.diagonal, "S": self.sibling, "F": self.finish}[word[0]](int(word[1:]))


class Scatter:
    def __init__(self, units, bufs, sems):
        self.u = units
        self.own, self.rc, self.rx, self.ry, self.r3, self.rz = bufs
        self.sems = sems
        self.pos = place()
        self.line, self.nx, self.ny, self.nc = neighbours()
        self.line_z = [lax.rem(self.pos[0] + k, NZ) for k in (1, 2, 3)]

    @staticmethod
    def scratch(n):
        v = lambda *s: pltpu.VMEM((n,) + s + (PR, UW), bf16)
        return [v(NZ, NY, NX), v(NZ, NY, NX), v(2, NY), v(2, NX), v(NZ), v(3)], [DMA((n,)), DMA((n, 8)), DMA((n, 8))]

    def copy(self, a, k, src, dst, to):
        return remote(src, dst, self.sems[1].at[a, k], self.sems[2].at[a, k], to)

    def one(self, a):
        c = self.pos[3]
        view = self.u[a][0]
        mine = pltpu.make_async_copy(view(ALL, ALL, ALL, c), self.own.at[a], self.sems[0].at[a])
        return mine, self.copy(a, 0, view(ALL, ALL, ALL, 1 - c), self.rc.at[a], self.nc)

    def two(self, a):
        z, y, x, c = self.pos
        own = self.own.at[a]
        return (self.copy(a, 1, own.at[0:2, :, 1 - x], self.rx.at[a], self.nx), self.copy(a, 2, own.at[2:4, 1 - y, :], self.ry.at[a], self.ny))

    def three(self, a):
        z, y, x, c = self.pos
        own, r3 = self.own.at[a], self.r3.at[a]
        return (self.copy(a, 3, own.at[0:2, 1 - y, x], r3.at[0:2], self.ny), self.copy(a, 4, own.at[2:4, y, 1 - x], r3.at[2:4], self.nx))

    def four(self, a):
        z, y, x, c = self.pos
        own = self.own.at[a]
        return [self.copy(a, 5 + k, own.at[self.line_z[k], y, x], self.rz.at[a, k], self.line[k]) for k in range(3)]

    def start(self, a):
        for d in self.one(a):
            d.start()

    def plane(self, a):
        for d in self.one(a):
            d.wait()
        own, rc = self.own.at[a], self.rc.at[a]

        @pl.loop(0, NZ)
        def _(i):
            own[i] = own[i] + rc[i]
        for d in self.two(a):
            d.start()

    def diagonal(self, a):
        z, y, x, c = self.pos
        for d in self.two(a):
            d.wait()
        own, rx, ry = self.own.at[a], self.rx.at[a], self.ry.at[a]
        for i in range(2):
            for j in range(2):
                own[i, j, x] = own[i, j, x] + rx[i, j]
                own[2 + i, y, j] = own[2 + i, y, j] + ry[i, j]
        for d in self.three(a):
            d.start()

    def along(self, a):
        z, y, x, c = self.pos
        for d in self.three(a):
            d.wait()
        own, r3 = self.own.at[a], self.r3.at[a]
        for i in range(NZ):
            own[i, y, x] = own[i, y, x] + r3[i]
        for d in self.four(a):
            d.start()

    def finish(self, a):
        z, y, x, c = self.pos
        for d in self.four(a):
            d.wait()
        own, rz = self.own.at[a], self.rz.at[a]
        total = own[z, y, x].astype(f32)
        for k in range(3):
            total = total + rz[k].astype(f32)
        self.u[a][1](total)

    def run(self, text):
        for word in text.split():
            {"B": self.start, "P": self.plane, "D": self.diagonal, "L": self.along, "F": self.finish}[word[0]](int(word[1:]))


class Total:
    def __init__(self, ref, bufs, s_s, s_r):
        self.ref, self.bufs, self.s, self.r = ref, bufs, s_s, s_r
        z, y, x, c = place()
        near = z + 1 - 2 * lax.rem(z, 2)
        self.to = [at_place(z, y, x, 1 - c), at_place(z, y, 1 - x, c), at_place(z, 1 - y, x, c), at_place(near, y, x, c), at_place(lax.rem(z + 2, NZ), y, x, c)]

    @staticmethod
    def scratch(rows):
        return [pltpu.VMEM((5, rows, D), f32), DMA((5,)), DMA((5,))]

    def copy(self, k):
        return remote(self.ref, self.bufs.at[k], self.s.at[k], self.r.at[k], self.to[k])

    def start(self):
        self.copy(0).start()

    def step(self, k):
        self.copy(k).wait()
        self.ref[...] = self.ref[...] + self.bufs[k]
        if k < 4:
            self.copy(k + 1).start()


def columns(src, j):
    return src.at[:, pl.ds(j * UW, UW)]


def gather_units(shards, gathered):
    (small, wq, wo, w1, w2), (gsmall, gq, go, g1, g2) = shards, gathered
    cols = lambda src, dst, j: (columns(src, j), lambda z, y, x, c: dst.at[z, y, x, c, :, pl.ds(j * UW, UW)], None)
    units = [(small, lambda z, y, x, c: gsmall.at[z, y, x, c], None)]
    units += [(None, lambda z, y, x, c, j=j: gq.at[z, y, x, c, :, pl.ds(j * UW, UW)], None) for j in range(3)] + [cols(wo, go, 0)]
    for j in range(NZ):
        units += [(w2, lambda z, y, x, c: g2.at[z, y, x, c], j), cols(w1, g1, j)]
    return units


def owned(out, rows, cols):
    def store(total):
        out[rows, cols] = total
    return store


def scatter_units(grads, outs):
    (dq, do, d1, d2), (oq, oo, o1, o2) = grads, outs

    def keep_heads(j):
        def store(total):
            for t in range(3):
                oq[:, t * D + j * HG:t * D + (j + 1) * HG] = total[:, t * HG:(t + 1) * HG]
        return store
    part = lambda src, j: lambda z, y, x, c: src.at[z, y, x, c, :, pl.ds(j * UW, UW)]
    two = [(lambda z, y, x, c, j=j: d2.at[z, y, x, c, pl.ds(j * PR, PR), :], owned(o2, slice(j * PR, (j + 1) * PR), ALL)) for j in range(4)]
    heads = [(part(dq, j), keep_heads(j)) for j in range(3)]
    return [(part(d1, 0), owned(o1, ALL, ALL)), two[0], two[1], heads[0], two[2], two[3], heads[1], (part(do, 0), owned(oo, ALL, ALL)), heads[2]]


HEAD_UNITS = (3, 6, 8)
HG = 256
NB = 9
NA = 3

A_HEAD = ("P0", "P1 D0", "P2 S0 D1", "P3 F0", "S1 D2", "P4 F1", "")
A_HALF = {0: "D3 S2", 1: "P5", 2: "F2 D4", 3: "P6 S3", 4: "F3", 5: "D5 P7 S4", 6: "F4 D6", 7: "P8 S5", 8: "F5 D7", 9: "P9 S6", 10: "F6 D8", 11: "P10 S7"}
A_MID = "F7 D9"
A_CHUNK = {0: "P11 S8", 1: "F8 D10", 2: "P12 S9", 3: "F9 D11", 4: "S10", 5: "F10 D12", 6: "S11", 7: "F11", 8: "S12", 9: "F12"}
A_SCATTER = {3: "B0", 4: "P0", 6: "D0 B1", 7: "P1", 8: "L0", 9: "D1 B2", 10: "P2 F0", 11: "L1"}
A_TAIL = ("D2", "F1", "", "L2", "F2")
B_HALF = {0: "P0", 1: "P1", 3: "D0 P2", 4: "D1", 5: "P3", 6: "D2 L0", 7: "P4 L1", 8: "D3", 9: "P5 L2 F0", 10: "D4 F1", 11: "P6 L3 F2"}
B_TABLE = {0: "P7 D5", 6: "L4 F3", 8: "D6", 12: "P8", 16: "L5 F4 D7", 20: "L6"}
B_NORM = ("F5 D8", "L7 F6", "", "L8")
T_NORM = ((), (0,), (), (1,))
B_TAIL = "F7 F8"


def spread(base, k, part, per):
    rows = lax.broadcasted_iota(jnp.int32, (part.shape[0], D), 0)
    lanes = lax.broadcasted_iota(jnp.int32, (part.shape[0], D), 1)
    full = mm(part, jnp.where(base == k, 1.0, 0.0).astype(bf16))
    return lambda first: jnp.sum(jnp.where(rows == first + lanes // per, full, 0.0), axis=0, keepdims=True)


def bias_at(h):
    return pl.ds(pl.multiple_of(h // 3 * IP, 8), IP), pl.multiple_of(lax.rem(h, 3) * IL, IL)


def head_bias(h, tab, idxT, bias_s):
    rowi = lax.broadcasted_iota(jnp.int32, (IP, 128), 0)
    rows, first = bias_at(h)
    for l in range(2):
        idx = idxT[:, pl.ds(l * 128, 128)]
        lo, hi = jnp.bitwise_and(idx, 127), jnp.right_shift(idx, 7)
        acc = jnp.zeros((IP, 128), f32)
        for k in range(6):
            t = jnp.broadcast_to(tab[h, k:k + 1, :], (IP, 128))
            acc = jnp.where(hi == k, jnp.take_along_axis(t, lo, axis=1, mode="promise_in_bounds"), acc)
        bias_s[rows, pl.ds(first + l * 128, 128)] = jnp.where(rowi < PATCH, acc, NEG)


def forward_half(p, s, ids_ref, q_s, k_s, v_s, att_s, bias_s, put):
    cols = pl.ds(pl.multiple_of(p * 128, 128), 128)
    lane = lax.broadcasted_iota(jnp.int32, (1, 128), 1)
    at = lambda image, n: pl.ds(pl.multiple_of(image * IP, IP), n * IP)
    linked = ids_ref[2 * s * PATCH] == ids_ref[(2 * s + 1) * PATCH]
    mx = jnp.where(jnp.logical_and(lax.broadcasted_iota(jnp.int32, (IP, 1), 0) < PATCH, linked), 0.0, NEG)
    kk = k_s[at(2 * s, 2), cols]
    vT = v_s[at(2 * s, 2), cols].T
    for a in range(2):
        q = q_s[at(2 * s + a, 1), cols]
        ats = []
        for h in range(2):
            qm = jnp.where((lane < 64) if h == 0 else (lane >= 64), q, jnp.zeros_like(q))
            st = mmt(kk, qm)
            rows_b, first = bias_at(2 * p + h)
            b = bias_s[rows_b, pl.ds(first, IL)][:, 0:IP]
            s0, s1 = (st[:IP] + b, st[IP:] + mx) if a == 0 else (st[:IP] + mx, st[IP:] + b)
            m = jnp.maximum(jnp.max(s0, axis=0, keepdims=True), jnp.max(s1, axis=0, keepdims=True))
            e0, e1 = jnp.exp(s0 - m), jnp.exp(s1 - m)
            inv = 1.0 / (jnp.sum(e0, axis=0, keepdims=True) + jnp.sum(e1, axis=0, keepdims=True))
            p0, p1 = (e0 * inv).astype(bf16), (e1 * inv).astype(bf16)
            put(a, h, 0, p0)
            put(a, h, 1, p1)
            v_h = vT[h * 64:(h + 1) * 64]
            ats.append(mm(v_h[:, :IP], p0) + mm(v_h[:, IP:], p1))
        att_s[at(2 * s + a, 1), cols] = jnp.concatenate(ats, axis=0).T.astype(bf16)


def at_step(i, run, plan):
    for when, text in plan.items():
        @pl.when(i == when)
        def _(text=text):
            run(text)


def fused_a_kernel(ni, nf, ids_ref, tok_ref, g_ref, tab_ref, idx_ref, small_ref, wq_ref, wo_ref, w1_ref, w2_ref,
                   out_ref, x_out, q_s, k_s, v_s, dres_ref, datt_ref, idx_out, dvec_ref, db1_ref, dwo_ref, vec, o1_ref,
                   wq_out, p_out, dw1_out, dw2_out,
                   gs, gq, go, g1, g2, tab, square, att_s, act, actT, dmlp, res, n2, branch, mlp, r2,
                   p_st, w2_st, b1, g_b, p_sem, w_sem, q_sem, h_sem, *rest):
    R = ni * IP
    dact, gp = dres_ref, datt_ref
    z, y, x, c = place()
    blocks = [pltpu.make_async_copy(wq_ref.at[:, pl.ds(t * D + j * HG, HG)], gq.at[z, y, x, c, :, pl.ds(j * UW + t * HG, HG)], h_sem.at[j, t])
              for j in range(3) for t in range(3)]
    for d in blocks:
        d.start()
    greet()
    for d in blocks:
        d.wait()
    ga = Gather(gather_units((small_ref, wq_ref, wo_ref, w1_ref, w2_ref), (gs, gq, go, g1, g2)), *rest[:9])
    part_of = lambda j: lambda z, y, x, c: g_b.at[j, z, y, x, c]
    sc = Scatter([(part_of(j), owned(o1_ref, ALL, slice(j * UW, (j + 1) * UW))) for j in range(NA)], rest[9:15], rest[15:18])
    for a in range(len(ga.u)):
        ga.start(a)
    def padded(src, dst):
        res[pl.ds(0, ni * PATCH), :] = src[...].astype(f32)
        for i in range(ni):
            dst[pl.ds(i * IP, PATCH), :] = res[pl.ds(i * PATCH, PATCH), :].astype(bf16)
            dst[pl.ds(i * IP + PATCH, IP - PATCH), :] = jnp.zeros((IP - PATCH, D), bf16)
    def biases(first, last):
        def one(h, carry):
            head_bias(h, tab, idx_out, branch)
            return carry
        lax.fori_loop(first, last, one, 0)
    square[...] = jnp.zeros_like(square)
    square[0:tab_ref.shape[0], 0:HEADS] = tab_ref[...].astype(f32)
    turned = square[:, 0:128].T
    for h in range(HEADS):
        for k in range(6):
            tab[h, k:k + 1, :] = turned[h:h + 1, k * 128:(k + 1) * 128]
    square[0:PATCH, 0:PATCH] = idx_ref[...].astype(f32)
    idx_out[...] = square[0:IL, 0:IL].T[0:IP].astype(jnp.int32)
    ga.run(A_HEAD[0])
    padded(tok_ref, x_out)
    ga.run(A_HEAD[1])
    for i in range(ni):
        rows = pl.ds(i * IP, IP)
        n2[rows, :], _ = ln_parts(x_out[rows, :].astype(f32))
    biases(0, 3)
    ga.run(A_HEAD[2])
    biases(3, 6)
    ga.run(A_HEAD[3])
    n_small = NZ * NY * NX * NC
    flat = gs.reshape(n_small * 8, 384)
    part = jnp.concatenate([flat[8 * d:8 * d + 1, :] for d in range(n_small)], axis=0).astype(bf16)
    per = D // n_small
    base = lax.broadcasted_iota(jnp.int32, (384, D), 0) - lax.rem(lax.broadcasted_iota(jnp.int32, (384, D), 1), per)
    for k in range(NVEC):
        vec[k:k + 1, :] = spread(base, k * per, part, per)(0)
    V = lambda k: vec[k:k + 1, :]
    for i in range(ni):
        rows = pl.ds(i * IP, IP)
        act[rows, :] = (n2[rows, :] * V(LN1G) + V(LN1B)).astype(bf16)
    ga.run(A_HEAD[4])
    biases(6, 9)
    padded(g_ref, gp)
    base1 = lax.broadcasted_iota(jnp.int32, (384, D), 0) - lax.rem(lax.broadcasted_iota(jnp.int32, (384, D), 1), 4 * per)
    sp = spread(base1, NVEC * per, part, 4 * per)
    for j in range(nf * FC // D):
        line = sp(j * (D // (4 * per)))
        for i in range(D // FC):
            b1[j * (D // FC) + i, 0:1, :] = line[:, i * FC:(i + 1) * FC]

    ga.run(A_HEAD[5])
    biases(9, 12)
    ga.run(A_HEAD[6])

    ns = ni // 2

    def half(t, carry):
        p, sq = t // ns, lax.rem(t, ns)
        at_step(t, ga.run, A_HALF)

        @pl.when(lax.rem(t, 2 * ns) == 0)
        def _():
            j = p // 2
            w = gq[:, :, :, :, :, pl.ds(pl.multiple_of(j * UW, UW), UW)].reshape(D, UW)
            cols = pl.ds(pl.multiple_of(j * HG, HG), HG)
            qb, vb = vec[QB:QB + 1, cols], vec[VB:VB + 1, cols]
            for i in range(ni):
                rows = pl.ds(i * IP, IP)
                o = mm(act[rows, :], w)
                q_s[rows, cols] = ((o[:, :HG] + qb) * HEAD ** -0.5).astype(bf16)
                k_s[rows, cols] = o[:, HG:2 * HG].astype(bf16)
                v_s[rows, cols] = (o[:, 2 * HG:] + vb).astype(bf16)

        slot = lax.rem(t, 2)
        st = p_st.at[slot]
        cp = pltpu.make_async_copy(st, p_out.at[p, sq], p_sem.at[slot])

        @pl.when(t >= 2)
        def _():
            pltpu.make_async_copy(st, p_out.at[p, sq], p_sem.at[slot]).wait()

        def put(a, h, b, v):
            st[a, h, b, :, 0:IP] = v
        forward_half(p, sq, ids_ref, q_s, k_s, v_s, att_s, branch, put)
        cp.start()
        return carry
    lax.fori_loop(0, HEADS // 2 * ns, half, 0)
    keep = pltpu.make_async_copy(gq, wq_out, q_sem.at[0])
    keep.start()
    ga.run(A_MID)

    sb = jnp.zeros((1, D), f32)
    wo = go[...].reshape(D, D)
    for i in range(ni):
        rows = pl.ds(i * IP, IP)
        br = mm(att_s[rows, :], wo) + V(OUTB)
        branch[rows, :] = br
        rs = x_out[rows, :].astype(f32) + V(GAM1) * br
        res[rows, :] = rs
        n, r = ln_parts(rs)
        n2[rows, :] = n
        r2[rows, :] = jnp.broadcast_to(r, (IP, 128))
        act[rows, :] = (n * V(LN2G) + V(LN2B)).astype(bf16)
        dm = V(GAM2) * gp[rows, :].astype(f32)
        sb = sb + jnp.sum(dm, axis=0, keepdims=True)
        dmlp[rows, :] = dm.astype(bf16)
    actT[...] = act[...].T
    dvec_ref[0:1, :] = sb
    mlp[...] = jnp.zeros_like(mlp)
    dact[...] = jnp.zeros_like(dact)
    g2v = g2.reshape(nf * FC, D)

    def chunk(c, carry):
        slot = lax.rem(c, 2)
        at = pl.multiple_of(c * FC, FC)
        at_step(c, ga.run, A_CHUNK)
        at_step(c, sc.run, A_SCATTER)
        w1, w2 = g1[:, :, :, :, :, pl.ds(at, FC)].reshape(D, FC), g2v[pl.ds(at, FC), :]
        cp = pltpu.make_async_copy(w2_st.at[slot], dw2_out.at[pl.ds(at, FC), :], w_sem.at[slot])
        pre = mm(act[...], w1) + b1[c, 0:1, :]
        cdf, xpdf = gelu_parts(pre)
        hid = (pre * cdf).astype(bf16)
        dp = mmt(dmlp[...], w2) * (cdf + xpdf)
        db1_ref[c, 0:1, :] = jnp.sum(dp, axis=0, keepdims=True)
        dpb = dp.astype(bf16)
        mlp[...] += mm(hid, w2)
        dact[...] += mmt(dpb, w1)

        @pl.when(c >= 2)
        def _():
            pltpu.make_async_copy(w2_st.at[slot], dw2_out.at[pl.ds(at, FC), :], w_sem.at[slot]).wait()
        g_b[c // (D // FC), :, :, :, :, :, pl.ds(pl.multiple_of(lax.rem(c, D // FC) * FC, FC), FC)] = mm(actT[...], dpb).astype(bf16).reshape(NZ, NY, NX, NC, PR, FC)
        w2_st[slot] = mm(hid.T, dmlp[...]).astype(bf16)
        cp.start()
        return carry
    lax.fori_loop(0, nf, chunk, 0)
    last = pltpu.make_async_copy(g_b.at[NA], dw1_out, q_sem.at[1])
    last.start()

    wo = go[...].reshape(D, D)
    sums = [jnp.zeros((1, D), f32) for _ in range(5)]
    for i in range(ni):
        rows = pl.ds(i * IP, IP)
        g = gp[rows, :].astype(f32)
        ml = mlp[rows, :] + V(FC2B)
        mlp[pl.ds(i * PATCH, PATCH), :] = (res[rows, :] + V(GAM2) * ml)[:PATCH]
        e, n = dact[rows, :], n2[rows, :]
        dn = e * V(LN2G)
        dr = g + r2[rows, 0:1] * (dn - jnp.mean(dn, axis=-1, keepdims=True) - n * jnp.mean(dn * n, axis=-1, keepdims=True))
        dres_ref[rows, :] = dr
        db = V(GAM1) * dr
        for k, t in enumerate((g * ml, e * n, e, dr * branch[rows, :], db)):
            sums[k] = sums[k] + jnp.sum(t, axis=0, keepdims=True)
        dbb = db.astype(bf16)
        dmlp[rows, :] = dbb
        datt_ref[rows, :] = mmt(dbb, wo).astype(bf16)
        sc.run(A_TAIL[i % 4])
    for k in range(5):
        dvec_ref[k + 1:k + 2, :] = sums[k]
    out_ref[...] = mlp[pl.ds(0, ni * PATCH), :].astype(bf16)
    dwo_ref[...] = mm(att_s[...].T, dmlp[...]).astype(bf16)
    keep.wait()
    last.wait()
    sc.run(A_TAIL[4])
    for slot in range(2):
        pltpu.make_async_copy(p_st.at[slot], p_out.at[0, 0], p_sem.at[slot]).wait()
        pltpu.make_async_copy(w2_st.at[slot], dw2_out.at[pl.ds(0, FC), :], w_sem.at[slot]).wait()


def fused_a(ids, tok, g, tab, idx, small, wq, wo, w1, w2, ni):
    R, F, S = ni * IP, w1.shape[1], jax.ShapeDtypeStruct
    v, hbm = vm(), pl.BlockSpec(memory_space=pl.ANY)
    six = lambda a: pltpu.VMEM((NZ, NY, NX, NC) + a.shape, a.dtype)
    row = lambda t: pltpu.VMEM((R, D), t)
    nu = 13
    bufs, s_sems = Scatter.scratch(NA)
    return pl.pallas_call(
        functools.partial(fused_a_kernel, ni, F // FC),
        in_specs=[pl.BlockSpec(memory_space=pltpu.SMEM), v, v, v, v, hbm, hbm, hbm, hbm, hbm],
        out_shape=[S((ni * PATCH, D), bf16)] + [S((R, D), bf16)] * 4 + [S((R, D), f32), S((R, D), bf16), S((IP, IL), jnp.int32), S((8, D), f32), S((F // FC, 8, FC), f32),
                   S((D, D), bf16), S((16, D), f32), S((PR, NA * UW), f32), S((NZ, NY, NX, NC) + wq.shape, bf16), S((6, ni // 2, 2, 2, 2, IP, IL), bf16), S((NZ, NY, NX, NC, PR, UW), bf16), S((F, D), bf16)],
        out_specs=[v] * 13 + [hbm] * 4,
        scratch_shapes=[six(a) for a in (small, wq, wo, w1, w2)] + [pltpu.VMEM((HEADS, 8, 128), f32), pltpu.VMEM((D, IL), f32), row(bf16), row(bf16),
                        pltpu.VMEM((D, R), bf16), row(bf16)] + [row(f32)] * 4 + [pltpu.VMEM((R, 128), f32), pltpu.VMEM((2, 2, 2, 2, IP, IL), bf16),
                        pltpu.VMEM((2, FC, D), bf16), pltpu.VMEM((F // FC, 8, FC), f32), pltpu.VMEM((NA + 1, NZ, NY, NX, NC, PR, UW), bf16), DMA((2,)), DMA((2,)), DMA((2,)), DMA((3, 3))] + Gather.scratch(nu) + bufs + s_sems,
        compiler_params=pltpu.CompilerParams(collective_id=2, has_side_effects=True, vmem_limit_bytes=62 << 20), name="forward_and_mlp",
    )(ids, tok, g, tab, idx, small, wq, wo, w1, w2)


def backward_half(p, s, q_ref, k_ref, v_ref, da_ref, probs, dqkv, dimg, dvec):
    lane = lax.broadcasted_iota(jnp.int32, (1, 128), 1)
    cols = pl.ds(pl.multiple_of(p * 128, 128), 128)
    at = lambda image, n: pl.ds(pl.multiple_of(image * IP, IP), n * IP)
    srow = at(2 * s, 2)
    kk, vv = k_ref[srow, cols], v_ref[srow, cols]
    kT = kk.T
    sq = jnp.zeros((1, 128), f32)
    dv, dk = jnp.zeros((2 * IP, 128), f32), jnp.zeros((2 * IP, 128), f32)
    for a in range(2):
        rows = at(2 * s + a, 1)
        q, da = q_ref[rows, cols], da_ref[rows, cols]
        dqs = []
        for h in range(2):
            msk = (lane < 64) if h == 0 else (lane >= 64)
            qm, dam = jnp.where(msk, q, jnp.zeros_like(q)), jnp.where(msk, da, jnp.zeros_like(da))
            pb0, pb1 = probs(a, h, 0), probs(a, h, 1)
            dp = mmt(vv, dam)
            t0, t1 = pb0.astype(f32) * dp[:IP], pb1.astype(f32) * dp[IP:]
            dl = jnp.sum(t0, axis=0, keepdims=True) + jnp.sum(t1, axis=0, keepdims=True)
            d0, d1 = t0 - pb0.astype(f32) * dl, t1 - pb1.astype(f32) * dl
            dimg[2 * p + h, :, 0:IP] += d0 if a == 0 else d1
            ds = jnp.concatenate([d0.astype(bf16), d1.astype(bf16)], axis=0)
            dv = dv + mm(jnp.concatenate([pb0, pb1], axis=0), dam)
            dk = dk + mm(ds, qm)
            dqs.append(mm(kT[h * 64:(h + 1) * 64], ds))
        dq = jnp.concatenate(dqs, axis=0).T * HEAD ** -0.5
        sq = sq + jnp.sum(dq, axis=0, keepdims=True)
        dqkv[0][rows, cols] = dq.astype(bf16)
    dqkv[1][srow, cols] = dk.astype(bf16)
    dqkv[2][srow, cols] = dv.astype(bf16)
    dvec[QB:QB + 1, cols] += sq
    dvec[VB:VB + 1, cols] += jnp.sum(dv, axis=0, keepdims=True)


def table_step(t, dimg, idx_ref, acc):
    sub8 = lax.broadcasted_iota(jnp.int32, (8, IL), 0)
    sub128 = lax.broadcasted_iota(jnp.int32, (128, IL), 0)
    at = pl.multiple_of(t * 8, 8)
    ix = idx_ref[pl.ds(at, 8), :]
    lo, hi = jnp.bitwise_and(ix, 127), jnp.right_shift(ix, 7)
    ds = [dimg[h, pl.ds(at, 8), :] for h in range(HEADS)]
    left, right = [], []
    for j in range(8):
        right.append(jnp.where(sub128 == lo[j:j + 1], 1.0, 0.0).astype(bf16))
        hm = sub8 == hi[j:j + 1]
        left.append(jnp.concatenate([jnp.where(hm, jnp.broadcast_to(d[j:j + 1], (8, IL)), 0.0) for d in ds], axis=0))
    left = jnp.concatenate(left, axis=1)
    high = left.astype(bf16)
    low = (left - high.astype(f32)).astype(bf16)
    acc[...] += mmt(jnp.concatenate([high, low], axis=0), jnp.concatenate(right, axis=1))


def fused_b_kernel(ni, table_rows, dvec_a, db1, x_ref, dres, q_ref, k_ref, v_ref, da_ref, vec, idx_ref, wq_hbm, p_hbm, d1_hbm, d2_hbm, do_hbm,
                   dtok_ref, table_ref, own_vec, own_b1, oq, oo, o1, o2,
                   wq, dq, dk, dv, dimg, act, actT, dwq, acc, square, tot_a, tot_b, p_st, p_sem, w_sem, *rest):
    bufs, sems, ta, tb = rest[:6], rest[6:9], rest[9:12], rest[12:15]
    greet()
    sc = Scatter(scatter_units((dwq, do_hbm, d1_hbm, d2_hbm), (oq, oo, o1, o2)), bufs, sems)
    for a in range(NB):
        if a not in HEAD_UNITS:
            sc.start(a)
    load = pltpu.make_async_copy(wq_hbm, wq, w_sem)
    load.start()
    ns = ni // 2
    fetch = lambda t: pltpu.make_async_copy(p_hbm.at[t // ns, lax.rem(t, ns)], p_st.at[lax.rem(t, 2)], p_sem.at[lax.rem(t, 2)])
    fetch(0).start()
    tot_a[...] = jnp.zeros_like(tot_a)
    tot_b[...] = jnp.zeros_like(tot_b)
    for k, r in ((FC2B, 0), (GAM2, 1), (LN2G, 2), (LN2B, 3), (GAM1, 4), (OUTB, 5)):
        tot_a[k:k + 1, :] = dvec_a[r:r + 1, :]
    nb = NA + 1
    for j in range(nb):
        for i in range(D // FC):
            tot_a[NVEC + j:NVEC + j + 1, i * FC:(i + 1) * FC] = db1[j * (D // FC) + i, 0:1, :]
    dimg[...] = jnp.zeros_like(dimg)

    def half(t, carry):
        p, sq = t // ns, lax.rem(t, ns)
        fetch(t).wait()

        @pl.when(t + 1 < HEADS // 2 * ns)
        def _():
            fetch(t + 1).start()
        st = p_st.at[lax.rem(t, 2)]
        at_step(t, sc.run, B_HALF)
        backward_half(p, sq, q_ref, k_ref, v_ref, da_ref, lambda a, h, b: st[a, h, b, :, 0:IP], (dq, dk, dv), dimg, tot_a)

        @pl.when(lax.rem(t, 2 * ns) == 2 * ns - 1)
        def _():
            j = p // 2
            for n, d in enumerate((dq, dk, dv)):
                part = mm(actT[...], d[:, pl.ds(pl.multiple_of(j * HG, HG), HG)]).astype(bf16)
                dwq[:, :, :, :, :, pl.ds(pl.multiple_of(j * UW + n * HG, HG), HG)] = part.reshape(NZ, NY, NX, NC, PR, HG)
        at_step(t, sc.run, {(j + 1) * 2 * ns - 1: "B%d" % a for j, a in enumerate(HEAD_UNITS)})
        return carry
    V = lambda k: vec[k:k + 1, :]
    for i in range(ni):
        rows = pl.ds(i * IP, IP)
        n, _ = ln_parts(x_ref[rows, :].astype(f32))
        act[rows, :] = (n * V(LN1G) + V(LN1B)).astype(bf16)
    actT[...] = act[...].T
    lax.fori_loop(0, HEADS // 2 * ns, half, 0)
    acc[...] = jnp.zeros_like(acc)

    def table(t, carry):
        table_step(t, dimg, idx_ref, acc)
        at_step(t, sc.run, B_TABLE)
        return carry
    lax.fori_loop(0, -(-PATCH // 8), table, 0)
    for r in range(96):
        tot_a[14 + r // 6:15 + r // 6, (r % 6) * 128:(r % 6 + 1) * 128] = acc[r:r + 1, :] + acc[96 + r:97 + r, :]
    t_a = Total(tot_a, *ta)
    t_a.start()
    load.wait()
    w = wq
    sg, sb = jnp.zeros((1, D), f32), jnp.zeros((1, D), f32)
    for i in range(ni):
        rows = pl.ds(i * IP, IP)
        e = jnp.zeros((IP, D), f32)
        for j in range(3):
            left = jnp.concatenate([d[rows, j * HG:(j + 1) * HG] for d in (dq, dk, dv)], axis=1)
            e = e + mmt(left, w[:, j * UW:(j + 1) * UW])
        n, r = ln_parts(x_ref[rows, :].astype(f32))
        dn = e * V(LN1G)
        dx = dres[rows, :] + r * (dn - jnp.mean(dn, axis=-1, keepdims=True) - n * jnp.mean(dn * n, axis=-1, keepdims=True))
        dres[pl.ds(i * PATCH, PATCH), :] = dx[:PATCH]
        sg = sg + jnp.sum(e * n, axis=0, keepdims=True)
        sb = sb + jnp.sum(e, axis=0, keepdims=True)
        sc.run(B_NORM[i % 4])
        for k in T_NORM[i % 4]:
            t_a.step(k)
    tot_b[LN1G:LN1G + 1, :] = sg
    tot_b[LN1B:LN1B + 1, :] = sb
    t_b = Total(tot_b, *tb)
    t_b.start()
    dtok_ref[...] = dres[pl.ds(0, ni * PATCH), :].astype(bf16)
    t_a.step(2)
    t_b.step(0)
    sc.run(B_TAIL)
    t_a.step(3)
    t_b.step(1)
    t_a.step(4)
    for k in range(2, 5):
        t_b.step(k)
    tot_a[LN1G:LN1B + 1, :] = tot_b[LN1G:LN1B + 1, :]

    z, y, x, c = place()
    me = ((z * NY + y) * NX + x) * NC + c
    per = D // (NZ * NY * NX * NC)
    def pick(rows, first, width):
        one = jnp.where(lax.broadcasted_iota(jnp.int32, (D, 128), 0) == first + lax.broadcasted_iota(jnp.int32, (D, 128), 1), 1.0, 0.0).astype(bf16)
        h = rows.astype(bf16)
        m = (rows - h.astype(f32)).astype(bf16)
        l = (rows - h.astype(f32) - m.astype(f32)).astype(bf16)
        return mm(h, one) + mm(m, one) + mm(l, one)
    own_vec[...] = pick(tot_a[0:16, :], me * per, per)
    wide = nb * per
    slab = me // (D // wide)
    part = pick(tot_a[NVEC:NVEC + 8, :], lax.rem(me, D // wide) * wide, wide)
    rowi = lax.broadcasted_iota(jnp.int32, (8, 128), 0)
    own_b1[...] = jnp.broadcast_to(jnp.sum(jnp.where(rowi == slab, part, 0.0), axis=0, keepdims=True), (8, 128))
    square[...] = jnp.zeros_like(square)
    for r in range(96):
        if r % 8 < 6:
            square[r // 8:r // 8 + 1, (r % 8) * 128:(r % 8 + 1) * 128] = tot_a[14 + r // 6:15 + r // 6, (r % 6) * 128:(r % 6 + 1) * 128]
    table_ref[...] = square[...].T[0:table_rows, 0:HEADS]


def fused_b(dvec_a, db1, x, dres, q, k, v, da, vec, idx, wq6, p, d1, d2, do, table_rows, ni):
    R, S = ni * IP, jax.ShapeDtypeStruct
    vmem, hbm = vm(), pl.BlockSpec(memory_space=pl.ANY)
    split = lambda a: a.reshape((NZ, NY, NX, NC, -1, a.shape[-1]))
    d2, do = split(d2), split(do)
    own = lambda a: S(a.shape[-2:], f32)
    bufs, sems = Scatter.scratch(NB)
    row = lambda t: pltpu.VMEM((R, D), t)
    return pl.pallas_call(
        functools.partial(fused_b_kernel, ni, table_rows),
        in_specs=[vmem] * 10 + [hbm] * 5,
        out_shape=[S((ni * PATCH, D), bf16), S((table_rows, HEADS), f32), S((16, 128), f32), S((8, 128), f32), own(wq6), own(do), own(d1), own(d2)],
        out_specs=[vmem] * 8,
        scratch_shapes=[pltpu.VMEM((D, 3 * D), bf16)] + [row(bf16)] * 3 + [pltpu.VMEM((HEADS, IP, IL), f32), row(bf16), pltpu.VMEM((D, R), bf16), pltpu.VMEM(wq6.shape, bf16),
                        pltpu.VMEM((192, 128), f32), pltpu.VMEM((128, D), f32), pltpu.VMEM((32, D), f32), pltpu.VMEM((2, D), f32),
                        pltpu.VMEM((2, 2, 2, 2, IP, IL), bf16), DMA((2,)), DMA] + bufs + sems + Total.scratch(32) + Total.scratch(2),
        compiler_params=pltpu.CompilerParams(collective_id=3, has_side_effects=True, vmem_limit_bytes=62 << 20), name="attention_backward",
    )(dvec_a, db1, x, dres, q, k, v, da, vec, idx, wq6.reshape(D, 3 * D), p, d1, d2, do)


def pad_rows(a, ni):
    return jnp.pad(a.reshape(ni, PATCH, D), ((0, 0), (0, IP - PATCH), (0, 0))).reshape(ni * IP, D)


def unpad_rows(a, ni):
    return a.reshape(ni, IP, D)[:, :PATCH].reshape(ni * PATCH, D)


def local(tokens, image_ids, rel_index, rel_table, ln1_gain, ln1_bias, w_qkv, q_bias, v_bias, w_out, out_bias, gamma1,
          ln2_gain, ln2_bias, w_fc1, fc1_bias, w_fc2, fc2_bias, gamma2, out_grad):
    ni = tokens.shape[0] // PATCH
    per = ln1_gain.shape[0]
    n_dev = D // per
    small = jnp.concatenate([ln1_gain, ln1_bias, q_bias, v_bias, out_bias, gamma1, ln2_gain, ln2_bias, fc2_bias, gamma2, fc1_bias])
    me = lax.axis_index("gx") * lax.axis_size("gy") + lax.axis_index("gy")
    if (lax.axis_size("gx"), lax.axis_size("gy"), per) == (NZ * NY, NX * NC, PR):
        width = small.shape[0]
        small = jnp.pad(small.astype(f32).reshape(1, -1), ((0, 7), (0, 384 - width)))
        res = fused_a(image_ids, tokens, out_grad, rel_table, rel_index, small, w_qkv, w_out, w_fc1, w_fc2, ni)
        out, x, q, k, v, dres, datt, idx, dvec, db1, dwo, vec, g1, wq6, p, dw1, dw2 = res
        dtok, table_grad, own_vec, own_b1, gq, go, g1b, g2 = fused_b(dvec, db1, x, dres, q, k, v, datt, vec, idx, wq6, p, dw1, dw2, dwo, rel_table.shape[0], ni)
        sl = [own_vec[i, :per] for i in range(NVEC)]
        return (out, dtok, table_grad, sl[LN1G], sl[LN1B], gq, sl[QB], sl[VB], go, sl[OUTB], sl[GAM1], sl[LN2G], sl[LN2B], jnp.concatenate([g1, g1b], axis=1),
                own_b1[0, : fc1_bias.shape[0]], g2, sl[FC2B], sl[GAM2])
    gather = lambda a: lax.all_gather(a, AXES, axis=0, tiled=True)
    wq, wo, w1, w2 = gather(w_qkv), gather(w_out), gather(w_fc1), gather(w_fc2)
    small = lax.all_gather(small, AXES, axis=0, tiled=False).reshape(n_dev, -1).astype(f32)
    vec = jnp.pad(jnp.transpose(small[:, : NVEC * per].reshape(n_dev, NVEC, per), (1, 0, 2)).reshape(NVEC, D), ((0, 16 - NVEC), (0, 0)))
    b1 = small[:, NVEC * per :].reshape(1, -1)

    x = pad_rows(tokens, ni)
    g = pad_rows(out_grad, ni)
    ids = image_ids.reshape(ni, PATCH)[:, 0]
    table_rows = rel_table.shape[0]
    tab = jnp.pad(rel_table.astype(f32).T, ((0, 0), (0, 768 - table_rows))).reshape(6, 2, 6, 128)
    idx = jnp.pad(rel_index.T, ((0, IP - PATCH), (0, IL - PATCH)))

    att, q, k, v, p = front(ids, x, wq, tab, idx, vec, ni)
    out, dres, datt, dw1, dw2, dwo, db1, dvec = mlp(x, att, g, wo, vec, w1, w2, b1, ni)
    dq, dk, dv, dimg, dvec2 = attb(q, k, v, datt, p, ni)
    dtok, dwq, dvec3, dtab = qkvb(x, dres, dq, dk, dv, wq, vec, dimg, idx, ni)

    scatter = lambda a: lax.psum_scatter(a.astype(f32), AXES, scatter_dimension=0, tiled=True)
    rows = jnp.concatenate([dvec3[0:2], dvec2[0:2], dvec[5:6], dvec[4:5], dvec[2:4], dvec[0:1], dvec[1:2], db1.reshape(-1, D), dtab.reshape(-1, D)])
    total = lax.psum(rows, AXES)
    sl = [lax.dynamic_slice(total[i], (me * per,), (per,)) for i in range(NVEC)]
    nb = db1.shape[1] // D
    db1_own = lax.dynamic_slice(total[NVEC : NVEC + nb].reshape(-1), (me * per * nb,), (per * nb,))
    table_grad = total[NVEC + nb :].reshape(HEADS, 1024)[:, :table_rows].T
    return (unpad_rows(out, ni), unpad_rows(dtok, ni), table_grad, sl[LN1G], sl[LN1B], scatter(dwq), sl[QB], sl[VB], scatter(dwo),
            sl[OUTB], sl[GAM1], sl[LN2G], sl[LN2B], scatter(dw1), db1_own, scatter(dw2), sl[FC2B], sl[GAM2])


def solution(mesh):
    rows, vecs, none = P(AXES, None), P(AXES), P()
    return jax.shard_map(
        local,
        mesh=mesh,
        in_specs=(rows, vecs, none, none, vecs, vecs, rows, vecs, vecs, rows, vecs, vecs, vecs, vecs, rows, vecs, rows, vecs, vecs, rows),
        out_specs=(rows, rows, none, vecs, vecs, rows, vecs, vecs, rows, vecs, vecs, vecs, vecs, rows, vecs, rows, vecs, vecs),
        check_vma=False,
    )
```

```python
import functools

import jax
import jax.numpy as jnp
from jax import lax
from jax.experimental import pallas as pl
from jax.experimental.pallas import tpu as pltpu
from jax.sharding import PartitionSpec as P

D=768; HEADS=12; HEAD=64; PATCH=197; IP=208; IL=256
f32=jnp.float32; bf16=jnp.bfloat16
NEG=-1e30
def mm(a,b): return jnp.dot(a,b,preferred_element_type=f32)
def mmt(a,b): return lax.dot_general(a,b,(((1,),(1,)),((),())),preferred_element_type=f32)
def vm(): return pl.BlockSpec(memory_space=pltpu.VMEM)

def ln_parts(x):
    c=x-jnp.mean(x,axis=-1,keepdims=True)
    r=lax.rsqrt(jnp.mean(c*c,axis=-1,keepdims=True)+1e-6)
    return c*r,r

def front_kernel(ni, ids_ref, x_ref, wq_ref, tab_ref, idx_ref, vec_ref, att_ref, q_out, k_out, v_out, p_ref, bias_ref):
    pid=pl.program_id(0)
    R=ni*IP
    @pl.when(pid==0)
    def _():
        for i in range(ni):
            rows=pl.ds(i*IP,IP)
            n,_=ln_parts(x_ref[rows,:].astype(f32))
            a=(n*vec_ref[0:1,:]+vec_ref[1:2,:]).astype(bf16)
            for j in range(3):
                sl=pl.ds(j*D,D)
                o=mm(a,wq_ref[:,sl])
                if j==0: q_out[rows,:]=((o+vec_ref[2:3,:])*0.125).astype(bf16)
                if j==1: k_out[rows,:]=o.astype(bf16)
                if j==2: v_out[rows,:]=(o+vec_ref[3:4,:]).astype(bf16)
    rowi=lax.broadcasted_iota(jnp.int32,(IP,128),0)
    for h in range(2):
        for l in range(2):
            idx=idx_ref[:,pl.ds(l*128,128)]
            lo=jnp.bitwise_and(idx,127); hi=jnp.right_shift(idx,7)
            acc=jnp.zeros((IP,128),f32)
            for k in range(6):
                t=jnp.broadcast_to(tab_ref[0,h,k:k+1,:],(IP,128))
                gth=jnp.take_along_axis(t,lo,axis=1,mode="promise_in_bounds")
                acc=jnp.where(hi==k,gth,acc)
            bias_ref[h,:,pl.ds(l*128,128)]=jnp.where(rowi<PATCH,acc,NEG)
    cols=pl.ds(pl.multiple_of(pid*128,128),128)
    lane=lax.broadcasted_iota(jnp.int32,(1,128),1)
    for s in range(ni//2):
        linked=ids_ref[2*s]==ids_ref[2*s+1]
        mx=jnp.where(jnp.logical_and(lax.broadcasted_iota(jnp.int32,(IP,1),0)<PATCH,linked),0.0,NEG)
        kk=k_out[pl.ds(2*s*IP,2*IP),cols]
        vT=v_out[pl.ds(2*s*IP,2*IP),cols].T
        for a in range(2):
            rows=pl.ds((2*s+a)*IP,IP)
            q=q_out[rows,cols]
            ats=[]
            for h in range(2):
                qm=jnp.where((lane<64) if h==0 else (lane>=64),q,jnp.zeros_like(q))
                st=mmt(kk,qm)
                b=bias_ref[h,:,0:IP]
                if a==0: s0=st[:IP]+b; s1=st[IP:]+mx
                else: s0=st[:IP]+mx; s1=st[IP:]+b
                m=jnp.maximum(jnp.max(s0,axis=0,keepdims=True),jnp.max(s1,axis=0,keepdims=True))
                e0=jnp.exp(s0-m); e1=jnp.exp(s1-m)
                inv=1.0/(jnp.sum(e0,axis=0,keepdims=True)+jnp.sum(e1,axis=0,keepdims=True))
                p0=(e0*inv).astype(bf16); p1=(e1*inv).astype(bf16)
                p_ref[0,s,a,h,0,:,0:IP]=p0
                p_ref[0,s,a,h,1,:,0:IP]=p1
                v_h=vT[h*64:(h+1)*64]
                ats.append(mm(v_h[:,:IP],p0)+mm(v_h[:,IP:],p1))
            att_ref[rows,cols]=jnp.concatenate(ats,axis=0).T.astype(bf16)

def front(ids,x,wq,tab,idx,vec,ni):
    R=ni*IP
    full=lambda *s: pl.BlockSpec(s,lambda p:(0,)*len(s))
    return pl.pallas_call(functools.partial(front_kernel,ni),
        grid=(6,),
        out_shape=[jax.ShapeDtypeStruct((R,D),bf16)]*4+[jax.ShapeDtypeStruct((6,ni//2,2,2,2,IP,IL),bf16)],
        in_specs=[pl.BlockSpec(memory_space=pltpu.SMEM),full(R,D),full(D,3*D),pl.BlockSpec((1,2,6,128),lambda p:(p,0,0,0)),full(IP,IL),full(16,D)],
        out_specs=[full(R,D)]*4+[pl.BlockSpec((1,ni//2,2,2,2,IP,IL),lambda p:(p,0,0,0,0,0,0))],
        scratch_shapes=[pltpu.VMEM((2,IP,IL),f32)],
        compiler_params=pltpu.CompilerParams(vmem_limit_bytes=56<<20),name="front",
    )(ids,x,wq,tab,idx,vec)

def gelu_parts(x):
    z=x*0.7071067811865476
    e=lax.erf(z)
    cdf=0.5+0.5*e
    pdf=jnp.exp(-z*z)*0.3989422804014327
    return cdf, x*pdf

FC=256
def mlp_kernel(ni, nf, x_ref, att_ref, g_ref, wo_ref, vec_ref, w1_ref, w2_ref, b1_ref,
               out_ref, dres_ref, datt_ref, dw1_ref, dw2_ref, dwo_ref, db1_ref, dvec_ref,
               res, n2, r2, branch, act2, act2T, dmlp, mlp, dact):
    pid=pl.program_id(0)
    V=lambda k: vec_ref[k:k+1,:]
    @pl.when(pid==0)
    def _():
        sb=jnp.zeros((1,D),f32)
        for i in range(ni):
            rows=pl.ds(i*IP,IP)
            br=mm(att_ref[rows,:],wo_ref[...])+V(OUTB)
            branch[rows,:]=br
            rs=x_ref[rows,:].astype(f32)+V(GAM1)*br
            res[rows,:]=rs
            n,r=ln_parts(rs)
            n2[rows,:]=n
            r2[rows,:]=jnp.broadcast_to(r,(IP,128))
            act2[rows,:]=(n*V(LN2G)+V(LN2B)).astype(bf16)
            dm=V(GAM2)*g_ref[rows,:].astype(f32)
            sb=sb+jnp.sum(dm,axis=0,keepdims=True)
            dmlp[rows,:]=dm.astype(bf16)
        act2T[...]=act2[...].T
        dvec_ref[0:1,:]=sb
        mlp[...]=jnp.zeros_like(mlp)
        dact[...]=jnp.zeros_like(dact)
    w1=w1_ref[...]; w2=w2_ref[...]
    pre=mm(act2[...],w1)+b1_ref[...]
    cdf,xpdf=gelu_parts(pre)
    hid=(pre*cdf).astype(bf16)
    dh=mmt(dmlp[...],w2)
    dp=dh*(cdf+xpdf)
    db1_ref[...]=jnp.sum(dp,axis=0,keepdims=True)
    dpb=dp.astype(bf16)
    mlp[...]+=mm(hid,w2)
    dact[...]+=mmt(dpb,w1)
    dw1_ref[...]=mm(act2T[...],dpb).astype(bf16)
    dw2_ref[...]=mm(hid.T,dmlp[...]).astype(bf16)
    @pl.when(pid==nf-1)
    def _():
        sums=[jnp.zeros((1,D),f32) for _ in range(5)]
        for i in range(ni):
            rows=pl.ds(i*IP,IP)
            g=g_ref[rows,:].astype(f32)
            ml=mlp[rows,:]+V(FC2B)
            out_ref[rows,:]=(res[rows,:]+V(GAM2)*ml).astype(bf16)
            e=dact[rows,:]; n=n2[rows,:]
            dn=e*V(LN2G)
            dr=g+r2[rows,0:1]*(dn-jnp.mean(dn,axis=-1,keepdims=True)-n*jnp.mean(dn*n,axis=-1,keepdims=True))
            dres_ref[rows,:]=dr
            db=V(GAM1)*dr
            for k,t in enumerate((g*ml,e*n,e,dr*branch[rows,:],db)):
                sums[k]=sums[k]+jnp.sum(t,axis=0,keepdims=True)
            dbb=db.astype(bf16)
            dmlp[rows,:]=dbb
            datt_ref[rows,:]=mmt(dbb,wo_ref[...]).astype(bf16)
        for k in range(5): dvec_ref[k+1:k+2,:]=sums[k]
        dwo_ref[...]=mm(att_ref[...].T,dmlp[...]).astype(bf16)

def mlp(x,att,g,wo,vec,w1,w2,b1,ni):
    R=ni*IP; F=w1.shape[1]; nf=F//FC
    full=lambda *s: pl.BlockSpec(s,lambda p:(0,)*len(s),pipeline_mode=pl.Buffered(1))
    S=jax.ShapeDtypeStruct
    return pl.pallas_call(functools.partial(mlp_kernel,ni,nf),grid=(nf,),
        in_specs=[full(R,D)]*3+[full(D,D),full(16,D),pl.BlockSpec((D,FC),lambda p:(0,p)),pl.BlockSpec((FC,D),lambda p:(p,0)),pl.BlockSpec((1,FC),lambda p:(0,p))],
        out_shape=[S((R,D),bf16),S((R,D),f32),S((R,D),bf16),S((D,F),bf16),S((F,D),bf16),S((D,D),bf16),S((1,F),f32),S((8,D),f32)],
        out_specs=[full(R,D)]*3+[pl.BlockSpec((D,FC),lambda p:(0,p)),pl.BlockSpec((FC,D),lambda p:(p,0)),full(D,D),pl.BlockSpec((1,FC),lambda p:(0,p)),full(8,D)],
        scratch_shapes=[pltpu.VMEM((R,D),f32)]*2+[pltpu.VMEM((R,128),f32),pltpu.VMEM((R,D),f32),pltpu.VMEM((R,D),bf16),pltpu.VMEM((D,R),bf16),pltpu.VMEM((R,D),bf16)]+[pltpu.VMEM((R,D),f32)]*2,
        compiler_params=pltpu.CompilerParams(vmem_limit_bytes=60<<20),name="mlp",
    )(x,att,g,wo,vec,w1,w2,b1)

def attb_kernel(ni, q_ref,k_ref,v_ref,da_ref,p_ref, dq_ref,dk_ref,dv_ref,dimg_ref,dvec_ref):
    lane=lax.broadcasted_iota(jnp.int32,(1,128),1)
    sq=jnp.zeros((1,128),f32); sv=jnp.zeros((1,128),f32)
    for s in range(ni//2):
        srow=pl.ds(2*s*IP,2*IP)
        kk=k_ref[srow,:]; vv=v_ref[srow,:]
        kT=kk.T
        dv=jnp.zeros((2*IP,128),f32); dk=jnp.zeros((2*IP,128),f32)
        for a in range(2):
            rows=pl.ds((2*s+a)*IP,IP)
            q=q_ref[rows,:]; da=da_ref[rows,:]
            dqs=[]
            for h in range(2):
                msk=(lane<64) if h==0 else (lane>=64)
                qm=jnp.where(msk,q,jnp.zeros_like(q)); dam=jnp.where(msk,da,jnp.zeros_like(da))
                pb0=p_ref[0,s,a,h,0,:,0:IP]; pb1=p_ref[0,s,a,h,1,:,0:IP]
                dp=mmt(vv,dam)
                t0=pb0.astype(f32)*dp[:IP]; t1=pb1.astype(f32)*dp[IP:]
                dl=jnp.sum(t0,axis=0,keepdims=True)+jnp.sum(t1,axis=0,keepdims=True)
                d0=t0-pb0.astype(f32)*dl; d1=t1-pb1.astype(f32)*dl
                same=d0 if a==0 else d1
                if s==0 and a==0: dimg_ref[0,h,:,0:IP]=same
                else: dimg_ref[0,h,:,0:IP]+=same
                ds=jnp.concatenate([d0.astype(bf16),d1.astype(bf16)],axis=0)
                pb=jnp.concatenate([pb0,pb1],axis=0)
                dv=dv+mm(pb,dam)
                dk=dk+mm(ds,qm)
                dqs.append(mm(kT[h*64:(h+1)*64],ds))
            dq=jnp.concatenate(dqs,axis=0).T*0.125
            sq=sq+jnp.sum(dq,axis=0,keepdims=True)
            dq_ref[rows,:]=dq.astype(bf16)
        sv=sv+jnp.sum(dv,axis=0,keepdims=True)
        dk_ref[srow,:]=dk.astype(bf16); dv_ref[srow,:]=dv.astype(bf16)
    dimg_ref[0,:,:,IP:]=jnp.zeros((2,IP,IL-IP),f32)
    dvec_ref[0:1,:]=sq; dvec_ref[1:2,:]=sv

def attb(q,k,v,da,p,ni):
    R=ni*IP; S=jax.ShapeDtypeStruct
    col=pl.BlockSpec((R,128),lambda i:(0,i))
    return pl.pallas_call(functools.partial(attb_kernel,ni),grid=(6,),
        in_specs=[col]*4+[pl.BlockSpec((1,ni//2,2,2,2,IP,IL),lambda p:(p,0,0,0,0,0,0))],
        out_shape=[S((R,D),bf16)]*3+[S((6,2,IP,IL),f32),S((8,D),f32)],
        out_specs=[col]*3+[pl.BlockSpec((1,2,IP,IL),lambda i:(i,0,0,0)),pl.BlockSpec((8,128),lambda i:(0,i))],
        compiler_params=pltpu.CompilerParams(vmem_limit_bytes=56<<20),name="attb",
    )(q,k,v,da,p)

def qkvb_kernel(ni,x_ref,dres_ref,dq_ref,dk_ref,dv_ref,wq_ref,vec_ref,dimg_ref,idx_ref,
                dtok_ref,dw_ref,dvec_ref,dtab_ref,a1T,act1,acc):
    for i in range(ni):
        rows=pl.ds(i*IP,IP)
        n,r=ln_parts(x_ref[rows,:].astype(f32))
        act1[rows,:]=(n*vec_ref[0:1,:]+vec_ref[1:2,:]).astype(bf16)
    a1T[...]=act1[...].T
    for j,r_ in enumerate((dq_ref,dk_ref,dv_ref)):
        dw_ref[:,pl.ds(j*D,D)]=mm(a1T[...],r_[...]).astype(bf16)
    sg=jnp.zeros((1,D),f32); sb=jnp.zeros((1,D),f32)
    for i in range(ni):
        rows=pl.ds(i*IP,IP)
        e=mmt(dq_ref[rows,:],wq_ref[:,0:D])+mmt(dk_ref[rows,:],wq_ref[:,D:2*D])+mmt(dv_ref[rows,:],wq_ref[:,2*D:])
        n,r=ln_parts(x_ref[rows,:].astype(f32))
        dn=e*vec_ref[0:1,:]
        dx=dres_ref[rows,:]+r*(dn-jnp.mean(dn,axis=-1,keepdims=True)-n*jnp.mean(dn*n,axis=-1,keepdims=True))
        dtok_ref[rows,:]=dx.astype(bf16)
        sg=sg+jnp.sum(e*n,axis=0,keepdims=True); sb=sb+jnp.sum(e,axis=0,keepdims=True)
    dvec_ref[0:1,:]=sg; dvec_ref[1:2,:]=sb
    acc[...]=jnp.zeros_like(acc)
    sub8=lax.broadcasted_iota(jnp.int32,(8,IL),0)
    sub128=lax.broadcasted_iota(jnp.int32,(128,IL),0)
    def body(j,_):
        ix=idx_ref[pl.ds(j,1),:]
        lo=jnp.bitwise_and(ix,127); hi=jnp.right_shift(ix,7)
        oh=jnp.where(sub128==lo,1.0,0.0).astype(bf16)
        hm=sub8==hi
        As=[]
        for h in range(HEADS):
            d=dimg_ref[h//2,h%2,pl.ds(j,1),:]
            As.append(jnp.where(hm,jnp.broadcast_to(d,(8,IL)),0.0))
        A=jnp.concatenate(As,axis=0)
        Ah=A.astype(bf16); Al=(A-Ah.astype(f32)).astype(bf16)
        acc[...]+=mmt(Ah,oh)+mmt(Al,oh)
        return 0
    lax.fori_loop(0,PATCH,body,0)
    dtab_ref[...]=acc[...]

def qkvb(x,dres,dq,dk,dv,wq,vec,dimg,idx,ni):
    R=ni*IP; S=jax.ShapeDtypeStruct
    return pl.pallas_call(functools.partial(qkvb_kernel,ni),
        in_specs=[vm()]*9,
        out_shape=[S((R,D),bf16),S((D,3*D),bf16),S((8,D),f32),S((96,128),f32)],
        out_specs=[vm()]*4,
        scratch_shapes=[pltpu.VMEM((D,R),bf16),pltpu.VMEM((R,D),bf16),pltpu.VMEM((96,128),f32)],
        compiler_params=pltpu.CompilerParams(vmem_limit_bytes=56<<20),name="qkvb",
    )(x,dres,dq,dk,dv,wq,vec,dimg,idx)


AXES = ("gx", "gy")
NVEC = 10
(LN1G, LN1B, QB, VB, OUTB, GAM1, LN2G, LN2B, FC2B, GAM2) = range(NVEC)

MESH = pl.DeviceIdType.MESH
NZ, NY, NX, NC = 4, 2, 2, 2
PR, UW = 24, 768
DMA = pltpu.SemaphoreType.DMA
ALL = slice(None)


def place():
    gx, gy = lax.axis_index("gx"), lax.axis_index("gy")
    return gx // NY, lax.rem(gx, NY), gy // NC, lax.rem(gy, NC)


def at_place(z, y, x, c):
    return (z * NY + y, x * NC + c)


def neighbours():
    z, y, x, c = place()
    line = [at_place(lax.rem(z + k, NZ), y, x, c) for k in (1, 2, 3)]
    return line, at_place(z, y, 1 - x, c), at_place(z, 1 - y, x, c), at_place(z, y, x, 1 - c)


def across():
    z, y, x, c = place()
    return at_place(z, y, 1 - x, 1 - c)


def greet(also=()):
    line, nx, ny, nc = neighbours()
    peers = line + [nx, ny, nc] + list(also)
    barrier = pltpu.get_barrier_semaphore()
    for t in peers:
        pl.semaphore_signal(barrier, inc=1, device_id=t, device_id_type=MESH)
    pl.semaphore_wait(barrier, len(peers))


def remote(src, dst, send, recv, to):
    return pltpu.make_async_remote_copy(src_ref=src, dst_ref=dst, send_sem=send, recv_sem=recv, device_id=to, device_id_type=MESH)


class Gather:
    def __init__(self, units, local, z_s, z_r, p_s, p_r, d_s, d_r, c_s, c_r):
        self.u = units
        self.local, self.z_s, self.z_r, self.p_s, self.p_r, self.d_s, self.d_r, self.c_s, self.c_r = local, z_s, z_r, p_s, p_r, d_s, d_r, c_s, c_r
        self.pos = place()
        self.line, self.nx, self.ny, self.nc = neighbours()

    @staticmethod
    def scratch(n):
        return [DMA((n,)), DMA((n, 3)), DMA((n, 3)), DMA((n, 2)), DMA((n, 2)), DMA((n, 2)), DMA((n, 2)), DMA((n, 4)), DMA((n, 4))]

    def first(self, a):
        z, y, x, c = self.pos
        src, view, plane = self.u[a]
        to = view(z if plane is None else plane, y, x, c)
        mine = [] if src is None else [pltpu.make_async_copy(src, to, self.local.at[a])]
        src = to if src is None else src
        return mine + [remote(src, to, self.z_s.at[a, k], self.z_r.at[a, k if plane is None else 0], self.line[k]) for k in range(3)]

    def start(self, a):
        plane = self.u[a][2]
        if plane is None:
            for d in self.first(a):
                d.start()
        else:
            @pl.when(self.pos[0] == plane)
            def _():
                for d in self.first(a):
                    d.start()

    def arrive(self, a):
        plane = self.u[a][2]
        if plane is None:
            for d in self.first(a):
                d.wait()
        else:
            @pl.when(self.pos[0] == plane)
            def _():
                mine, *sent = self.first(a)
                mine.wait()
                for d in sent:
                    d.wait_send()

            @pl.when(self.pos[0] != plane)
            def _():
                z, y, x, c = self.pos
                src, view, plane = self.u[a]
                remote(src, view(plane, y, x, c), self.z_s.at[a, 0], self.z_r.at[a, 0], self.line[0]).wait_recv()

    def to_plane(self, a):
        z, y, x, c = self.pos
        _, view, plane = self.u[a]
        v = view(ALL if plane is None else plane, y, x, c)
        return (remote(v, v, self.p_s.at[a, 0], self.p_r.at[a, 0], self.nx), remote(v, v, self.p_s.at[a, 1], self.p_r.at[a, 1], self.ny))

    def to_diagonal(self, a):
        z, y, x, c = self.pos
        _, view, plane = self.u[a]
        if plane is None:
            vx, vy = view(slice(0, 2), y, 1 - x, c), view(slice(2, 4), 1 - y, x, c)
        else:
            vx, vy = view(plane, y, 1 - x, c), view(plane, 1 - y, x, c)
            half = vx.shape[0] // 2
            vx, vy = vx.at[pl.ds(0, half)], vy.at[pl.ds(half, half)]
        return (remote(vx, vx, self.d_s.at[a, 0], self.d_r.at[a, 0], self.ny), remote(vy, vy, self.d_s.at[a, 1], self.d_r.at[a, 1], self.nx))

    def to_sibling(self, a, k):
        z, y, x, c = self.pos
        _, view, plane = self.u[a]
        v = view(ALL if plane is None else plane, (y, y, 1 - y, 1 - y)[k], (x, 1 - x, x, 1 - x)[k], c)
        return remote(v, v, self.c_s.at[a, k], self.c_r.at[a, k], self.nc)

    def plane(self, a):
        self.arrive(a)
        for d in self.to_plane(a):
            d.start()
        self.to_sibling(a, 0).start()

    def diagonal(self, a):
        for d in self.to_plane(a):
            d.wait()
        for d in self.to_diagonal(a):
            d.start()
        self.to_sibling(a, 1).start()
        self.to_sibling(a, 2).start()

    def sibling(self, a):
        for d in self.to_diagonal(a):
            d.wait()
        self.to_sibling(a, 3).start()

    def finish(self, a):
        for k in range(4):
            self.to_sibling(a, k).wait()

    def run(self, text):
        for word in text.split():
            {"P": self.plane, "D": self.diagonal, "S": self.sibling, "F": self.finish}[word[0]](int(word[1:]))


class Scatter:
    def __init__(self, units, bufs, sems):
        self.u = units
        self.own, self.rc, self.rx, self.ry, self.r3, self.rz = bufs
        self.sems = sems
        self.pos = place()
        self.line, self.nx, self.ny, self.nc = neighbours()
        self.line_z = [lax.rem(self.pos[0] + k, NZ) for k in (1, 2, 3)]

    @staticmethod
    def scratch(n):
        v = lambda *s: pltpu.VMEM((n,) + s + (PR, UW), bf16)
        return [v(NZ, NY, NX), v(NZ, NY, NX), v(2, NY), v(2, NX), v(NZ), v(3)], [DMA((n,)), DMA((n, 8)), DMA((n, 8))]

    def copy(self, a, k, src, dst, to):
        return remote(src, dst, self.sems[1].at[a, k], self.sems[2].at[a, k], to)

    def one(self, a):
        c = self.pos[3]
        view = self.u[a][0]
        mine = pltpu.make_async_copy(view(ALL, ALL, ALL, c), self.own.at[a], self.sems[0].at[a])
        return mine, self.copy(a, 0, view(ALL, ALL, ALL, 1 - c), self.rc.at[a], self.nc)

    def two(self, a):
        z, y, x, c = self.pos
        own = self.own.at[a]
        return (self.copy(a, 1, own.at[0:2, :, 1 - x], self.rx.at[a], self.nx), self.copy(a, 2, own.at[2:4, 1 - y, :], self.ry.at[a], self.ny))

    def three(self, a):
        z, y, x, c = self.pos
        own, r3 = self.own.at[a], self.r3.at[a]
        return (self.copy(a, 3, own.at[0:2, 1 - y, x], r3.at[0:2], self.ny), self.copy(a, 4, own.at[2:4, y, 1 - x], r3.at[2:4], self.nx))

    def four(self, a):
        z, y, x, c = self.pos
        own = self.own.at[a]
        return [self.copy(a, 5 + k, own.at[self.line_z[k], y, x], self.rz.at[a, k], self.line[k]) for k in range(3)]

    def start(self, a):
        for d in self.one(a):
            d.start()

    def plane(self, a):
        for d in self.one(a):
            d.wait()
        own, rc = self.own.at[a], self.rc.at[a]

        @pl.loop(0, NZ)
        def _(i):
            own[i] = own[i] + rc[i]
        for d in self.two(a):
            d.start()

    def diagonal(self, a):
        z, y, x, c = self.pos
        for d in self.two(a):
            d.wait()
        own, rx, ry = self.own.at[a], self.rx.at[a], self.ry.at[a]
        for i in range(2):
            for j in range(2):
                own[i, j, x] = own[i, j, x] + rx[i, j]
                own[2 + i, y, j] = own[2 + i, y, j] + ry[i, j]
        for d in self.three(a):
            d.start()

    def along(self, a):
        z, y, x, c = self.pos
        for d in self.three(a):
            d.wait()
        own, r3 = self.own.at[a], self.r3.at[a]
        for i in range(NZ):
            own[i, y, x] = own[i, y, x] + r3[i]
        for d in self.four(a):
            d.start()

    def finish(self, a):
        z, y, x, c = self.pos
        for d in self.four(a):
            d.wait()
        own, rz = self.own.at[a], self.rz.at[a]
        total = own[z, y, x].astype(f32)
        for k in range(3):
            total = total + rz[k].astype(f32)
        self.u[a][1](total)

    def run(self, text):
        for word in text.split():
            {"B": self.start, "P": self.plane, "D": self.diagonal, "L": self.along, "F": self.finish}[word[0]](int(word[1:]))


class Total:
    def __init__(self, ref, hops, bufs, s_s, s_r):
        self.ref, self.hops, self.bufs, self.s, self.r = ref, hops, bufs, s_s, s_r

    @staticmethod
    def pairs():
        z, y, x, c = place()
        near = z + 1 - 2 * lax.rem(z, 2)
        _, nx, ny, nc = neighbours()
        return [[nc], [nx], [ny], [at_place(near, y, x, c)], [at_place(lax.rem(z + 2, NZ), y, x, c)]]

    @staticmethod
    def groups():
        line, nx, ny, nc = neighbours()
        return [[nc, nx, across()], [ny], line]

    @staticmethod
    def scratch(n, *shape):
        return [pltpu.VMEM((n,) + shape, f32), DMA((n,)), DMA((n,))]

    def copies(self, k):
        first = sum(len(h) for h in self.hops[:k])
        return [remote(self.ref, self.bufs.at[first + i], self.s.at[first + i], self.r.at[first + i], to) for i, to in enumerate(self.hops[k])]

    def start(self):
        for d in self.copies(0):
            d.start()

    def step(self, k):
        for d in self.copies(k):
            d.wait()
        first = sum(len(h) for h in self.hops[:k])
        for i in range(len(self.hops[k])):
            self.ref[...] = self.ref[...] + self.bufs[first + i]
        if k + 1 < len(self.hops):
            for d in self.copies(k + 1):
                d.start()


def columns(src, j):
    return src.at[:, pl.ds(j * UW, UW)]


def gather_units(shards, gathered):
    (small, wq, wo, w1, w2), (gsmall, gq, go, g1, g2) = shards, gathered
    cols = lambda src, dst, j: (columns(src, j), lambda z, y, x, c: dst.at[z, y, x, c, :, pl.ds(j * UW, UW)], None)
    units = [(small, lambda z, y, x, c: gsmall.at[z, y, x, c], None)]
    units += [(None, lambda z, y, x, c, j=j: gq.at[z, y, x, c, :, pl.ds(j * UW, UW)], None) for j in range(3)] + [cols(wo, go, 0)]
    for j in range(NZ):
        units += [(w2, lambda z, y, x, c: g2.at[z, y, x, c], j), cols(w1, g1, j)]
    return units


def owned(out, rows, cols):
    def store(total):
        out[rows, cols] = total
    return store


def scatter_units(grads, outs):
    (dq, do, d1, d2), (oq, oo, o1, o2) = grads, outs

    def keep_heads(j):
        def store(total):
            for t in range(3):
                oq[:, t * D + j * HG:t * D + (j + 1) * HG] = total[:, t * HG:(t + 1) * HG]
        return store
    part = lambda src, j: lambda z, y, x, c: src.at[z, y, x, c, :, pl.ds(j * UW, UW)]
    two = [(lambda z, y, x, c, j=j: d2.at[z, y, x, c, pl.ds(j * PR, PR), :], owned(o2, slice(j * PR, (j + 1) * PR), ALL)) for j in range(4)]
    heads = [(part(dq, j), keep_heads(j)) for j in range(3)]
    return [(part(d1, 0), owned(o1, ALL, ALL)), two[0], two[1], heads[0], two[2], two[3], heads[1], (part(do, 0), owned(oo, ALL, ALL)), heads[2]]


HEAD_UNITS = (3, 6, 8)
HG = 256
NB = 9
NA = 3

A_HEAD = ('P0', 'P1 D0', 'S0 P2', 'D1 F0', 'S1 P3', 'F1 D2 P4')
A_HALF = {0: 'P5 S2', 1: 'D3', 2: 'P6 F2', 3: 'D4', 4: 'P7 S3', 5: 'D5', 6: 'P8 S4 F3', 7: 'D6', 8: 'P9 S5 F4', 9: 'D7', 10: 'P10 S6 F5', 11: 'D8'}
A_MID = 'P11 S7 F6'
A_CHUNK = {0: 'D9 P12', 1: 'S8 F7', 2: 'D10 F8', 3: 'S9 D11', 4: 'F9 S10', 5: 'D12 F10', 6: 'S11', 7: 'F11', 8: 'S12', 9: 'F12'}
A_SCATTER = {3: "B0", 4: "P0", 6: "D0 B1", 7: "P1", 8: "L0", 9: "D1 B2", 10: "P2 F0", 11: "L1"}
A_TAIL = ("D2", "F1", "", "L2", "F2")
B_HALF = {0: "P0", 1: "P1", 3: "D0 P2", 4: "D1", 5: "P3", 6: "D2 L0", 7: "P4 L1", 8: "D3", 9: "P5 L2 F0", 10: "D4 F1", 11: "P6 L3 F2"}
B_TABLE = {0: "P7 D5", 6: "L4 F3", 8: "D6", 12: "P8", 16: "L5 F4 D7", 20: "L6"}
B_NORM = ("F5 D8", "L7 F6", "", "L8")
T_NORM = ((), (0,), (1,), (2,))
B_TAIL = "F7 F8"
V_TABLE = {6: 0, 18: 1}
V_NORM = ((2,), (), (3,), ())


def spread(base, k, part, per):
    rows = lax.broadcasted_iota(jnp.int32, (part.shape[0], D), 0)
    lanes = lax.broadcasted_iota(jnp.int32, (part.shape[0], D), 1)
    full = mm(part, jnp.where(base == k, 1.0, 0.0).astype(bf16))
    return lambda first: jnp.sum(jnp.where(rows == first + lanes // per, full, 0.0), axis=0, keepdims=True)


def bias_at(h):
    return pl.ds(pl.multiple_of(h // 3 * IP, 8), IP), pl.multiple_of(lax.rem(h, 3) * IL, IL)


def head_bias(h, tab, idxT, bias_s):
    rowi = lax.broadcasted_iota(jnp.int32, (IP, 128), 0)
    rows, first = bias_at(h)
    for l in range(2):
        idx = idxT[:, pl.ds(l * 128, 128)]
        lo, hi = jnp.bitwise_and(idx, 127), jnp.right_shift(idx, 7)
        acc = jnp.zeros((IP, 128), f32)
        for k in range(6):
            t = jnp.broadcast_to(tab[h, k:k + 1, :], (IP, 128))
            acc = jnp.where(hi == k, jnp.take_along_axis(t, lo, axis=1, mode="promise_in_bounds"), acc)
        bias_s[rows, pl.ds(first + l * 128, 128)] = jnp.where(rowi < PATCH, acc, NEG)


def forward_half(p, s, ids_ref, q_s, k_s, v_s, att_s, bias_s, put):
    cols = pl.ds(pl.multiple_of(p * 128, 128), 128)
    lane = lax.broadcasted_iota(jnp.int32, (1, 128), 1)
    at = lambda image, n: pl.ds(pl.multiple_of(image * IP, IP), n * IP)
    linked = ids_ref[2 * s * PATCH] == ids_ref[(2 * s + 1) * PATCH]
    mx = jnp.where(jnp.logical_and(lax.broadcasted_iota(jnp.int32, (IP, 1), 0) < PATCH, linked), 0.0, NEG)
    kk = k_s[at(2 * s, 2), cols]
    vT = v_s[at(2 * s, 2), cols].T
    for a in range(2):
        q = q_s[at(2 * s + a, 1), cols]
        ats = []
        for h in range(2):
            qm = jnp.where((lane < 64) if h == 0 else (lane >= 64), q, jnp.zeros_like(q))
            st = mmt(kk, qm)
            rows_b, first = bias_at(2 * p + h)
            b = bias_s[rows_b, pl.ds(first, IL)][:, 0:IP]
            s0, s1 = (st[:IP] + b, st[IP:] + mx) if a == 0 else (st[:IP] + mx, st[IP:] + b)
            m = jnp.maximum(jnp.max(s0, axis=0, keepdims=True), jnp.max(s1, axis=0, keepdims=True))
            e0, e1 = jnp.exp(s0 - m), jnp.exp(s1 - m)
            inv = 1.0 / (jnp.sum(e0, axis=0, keepdims=True) + jnp.sum(e1, axis=0, keepdims=True))
            p0, p1 = (e0 * inv).astype(bf16), (e1 * inv).astype(bf16)
            put(a, h, 0, p0)
            put(a, h, 1, p1)
            v_h = vT[h * 64:(h + 1) * 64]
            ats.append(mm(v_h[:, :IP], p0) + mm(v_h[:, IP:], p1))
        att_s[at(2 * s + a, 1), cols] = jnp.concatenate(ats, axis=0).T.astype(bf16)


def at_step(i, run, plan):
    for when, text in plan.items():
        @pl.when(i == when)
        def _(text=text):
            run(text)


def fused_a_kernel(ni, nf, ids_ref, tok_ref, g_ref, tab_ref, idx_ref, *refs):
    smalls, refs = refs[:NVEC + 1], refs[NVEC + 1:]
    fused_a_body(ni, nf, smalls, ids_ref, tok_ref, g_ref, tab_ref, idx_ref, *refs)


def fused_a_body(ni, nf, smalls, ids_ref, tok_ref, g_ref, tab_ref, idx_ref, wq_ref, wo_ref, w1_ref, w2_ref,
                   out_ref, x_out, q_s, k_s, v_s, dres_ref, datt_ref, idx_out, dvec_ref, db1_ref, dwo_ref, vec, o1_ref,
                   wq_out, p_out, dw1_out, dw2_out,
                   gs, gq, go, g1, g2, tab, square, att_s, act, actT, dmlp, res, n2, branch, mlp, r2,
                   p_st, w2_st, b1, g_b, p_sem, w_sem, q_sem, h_sem, small_ref, *rest):
    R = ni * IP
    dact, gp = dres_ref, datt_ref
    z, y, x, c = place()
    blocks = [pltpu.make_async_copy(wq_ref.at[:, pl.ds(t * D + j * HG, HG)], gq.at[z, y, x, c, :, pl.ds(j * UW + t * HG, HG)], h_sem.at[j, t])
              for j in range(3) for t in range(3)]
    for d in blocks:
        d.start()
    first = 0
    small_ref[...] = jnp.zeros_like(small_ref)
    for r in smalls:
        small_ref[0:1, first:first + r.shape[1]] = r[...].astype(f32)
        first += r.shape[1]
    greet()
    for d in blocks:
        d.wait()
    ga = Gather(gather_units((small_ref, wq_ref, wo_ref, w1_ref, w2_ref), (gs, gq, go, g1, g2)), *rest[:9])
    part_of = lambda j: lambda z, y, x, c: g_b.at[j, z, y, x, c]
    sc = Scatter([(part_of(j), owned(o1_ref, ALL, slice(j * UW, (j + 1) * UW))) for j in range(NA)], rest[9:15], rest[15:18])
    for a in range(len(ga.u)):
        ga.start(a)
    def padded(src, dst):
        res[pl.ds(0, ni * PATCH), :] = src[...].astype(f32)
        for i in range(ni):
            dst[pl.ds(i * IP, PATCH), :] = res[pl.ds(i * PATCH, PATCH), :].astype(bf16)
            dst[pl.ds(i * IP + PATCH, IP - PATCH), :] = jnp.zeros((IP - PATCH, D), bf16)
    def biases(first, last):
        def one(h, carry):
            head_bias(h, tab, idx_out, branch)
            return carry
        lax.fori_loop(first, last, one, 0)
    tab[...] = jnp.zeros_like(tab)
    for k in range(6):
        n = min(128, tab_ref.shape[1] - k * 128)
        piece = tab_ref[:, k * 128:k * 128 + n].astype(f32)
        for h in range(HEADS):
            tab[h, k:k + 1, 0:n] = piece[h:h + 1]
    square[...] = jnp.zeros_like(square)
    square[0:PATCH, 0:PATCH] = idx_ref[...].astype(f32)
    idx_out[...] = square[...].T[0:IP].astype(jnp.int32)
    padded(tok_ref, x_out)
    ga.run(A_HEAD[0])
    for i in range(ni):
        rows = pl.ds(i * IP, IP)
        n2[rows, :], _ = ln_parts(x_out[rows, :].astype(f32))
    biases(0, 2)
    ga.run(A_HEAD[1])
    biases(2, 4)
    ga.run(A_HEAD[2])
    biases(4, 6)
    ga.run(A_HEAD[3])
    n_small = NZ * NY * NX * NC
    flat = gs.reshape(n_small * 8, 384)
    part = jnp.concatenate([flat[8 * d:8 * d + 1, :] for d in range(n_small)], axis=0).astype(bf16)
    per = D // n_small
    base = lax.broadcasted_iota(jnp.int32, (384, D), 0) - lax.rem(lax.broadcasted_iota(jnp.int32, (384, D), 1), per)
    for k in range(NVEC):
        vec[k:k + 1, :] = spread(base, k * per, part, per)(0)
    V = lambda k: vec[k:k + 1, :]
    for i in range(ni):
        rows = pl.ds(i * IP, IP)
        act[rows, :] = (n2[rows, :] * V(LN1G) + V(LN1B)).astype(bf16)
    ga.run(A_HEAD[4])
    biases(6, 9)
    ga.run(A_HEAD[5])
    padded(g_ref, gp)
    base1 = lax.broadcasted_iota(jnp.int32, (384, D), 0) - lax.rem(lax.broadcasted_iota(jnp.int32, (384, D), 1), 4 * per)
    sp = spread(base1, NVEC * per, part, 4 * per)
    for j in range(nf * FC // D):
        line = sp(j * (D // (4 * per)))
        for i in range(D // FC):
            b1[j * (D // FC) + i, 0:1, :] = line[:, i * FC:(i + 1) * FC]

    biases(9, 12)

    ns = ni // 2

    def half(t, carry):
        p, sq = t // ns, lax.rem(t, ns)
        at_step(t, ga.run, A_HALF)

        @pl.when(lax.rem(t, 2 * ns) == 0)
        def _():
            j = p // 2
            w = gq[:, :, :, :, :, pl.ds(pl.multiple_of(j * UW, UW), UW)].reshape(D, UW)
            cols = pl.ds(pl.multiple_of(j * HG, HG), HG)
            qb, vb = vec[QB:QB + 1, cols], vec[VB:VB + 1, cols]
            for i in range(ni):
                rows = pl.ds(i * IP, IP)
                o = mm(act[rows, :], w)
                q_s[rows, cols] = ((o[:, :HG] + qb) * HEAD ** -0.5).astype(bf16)
                k_s[rows, cols] = o[:, HG:2 * HG].astype(bf16)
                v_s[rows, cols] = (o[:, 2 * HG:] + vb).astype(bf16)

        slot = lax.rem(t, 2)
        st = p_st.at[slot]
        cp = pltpu.make_async_copy(st, p_out.at[p, sq], p_sem.at[slot])

        @pl.when(t >= 2)
        def _():
            pltpu.make_async_copy(st, p_out.at[p, sq], p_sem.at[slot]).wait()

        def put(a, h, b, v):
            st[a, h, b, :, 0:IP] = v
        forward_half(p, sq, ids_ref, q_s, k_s, v_s, att_s, branch, put)
        cp.start()
        return carry
    lax.fori_loop(0, HEADS // 2 * ns, half, 0)
    keep = pltpu.make_async_copy(gq, wq_out, q_sem.at[0])
    keep.start()
    ga.run(A_MID)

    sb = jnp.zeros((1, D), f32)
    wo = go[...].reshape(D, D)
    for i in range(ni):
        rows = pl.ds(i * IP, IP)
        br = mm(att_s[rows, :], wo) + V(OUTB)
        branch[rows, :] = br
        rs = x_out[rows, :].astype(f32) + V(GAM1) * br
        res[rows, :] = rs
        n, r = ln_parts(rs)
        n2[rows, :] = n
        r2[rows, :] = jnp.broadcast_to(r, (IP, 128))
        act[rows, :] = (n * V(LN2G) + V(LN2B)).astype(bf16)
        dm = V(GAM2) * gp[rows, :].astype(f32)
        sb = sb + jnp.sum(dm, axis=0, keepdims=True)
        dmlp[rows, :] = dm.astype(bf16)
    actT[...] = act[...].T
    dvec_ref[0:1, :] = sb
    mlp[...] = jnp.zeros_like(mlp)
    dact[...] = jnp.zeros_like(dact)
    g2v = g2.reshape(nf * FC, D)

    def chunk(c, carry):
        slot = lax.rem(c, 2)
        at = pl.multiple_of(c * FC, FC)
        at_step(c, ga.run, A_CHUNK)
        at_step(c, sc.run, A_SCATTER)
        w1, w2 = g1[:, :, :, :, :, pl.ds(at, FC)].reshape(D, FC), g2v[pl.ds(at, FC), :]
        cp = pltpu.make_async_copy(w2_st.at[slot], dw2_out.at[pl.ds(at, FC), :], w_sem.at[slot])
        pre = mm(act[...], w1) + b1[c, 0:1, :]
        cdf, xpdf = gelu_parts(pre)
        hid = (pre * cdf).astype(bf16)
        dp = mmt(dmlp[...], w2) * (cdf + xpdf)
        db1_ref[c, 0:1, :] = jnp.sum(dp, axis=0, keepdims=True)
        dpb = dp.astype(bf16)
        mlp[...] += mm(hid, w2)
        dact[...] += mmt(dpb, w1)

        @pl.when(c >= 2)
        def _():
            pltpu.make_async_copy(w2_st.at[slot], dw2_out.at[pl.ds(at, FC), :], w_sem.at[slot]).wait()
        g_b[c // (D // FC), :, :, :, :, :, pl.ds(pl.multiple_of(lax.rem(c, D // FC) * FC, FC), FC)] = mm(actT[...], dpb).astype(bf16).reshape(NZ, NY, NX, NC, PR, FC)
        w2_st[slot] = mm(hid.T, dmlp[...]).astype(bf16)
        cp.start()
        return carry
    lax.fori_loop(0, nf, chunk, 0)
    last = pltpu.make_async_copy(g_b.at[NA], dw1_out, q_sem.at[1])
    last.start()

    wo = go[...].reshape(D, D)
    sums = [jnp.zeros((1, D), f32) for _ in range(5)]
    for i in range(ni):
        rows = pl.ds(i * IP, IP)
        g = gp[rows, :].astype(f32)
        ml = mlp[rows, :] + V(FC2B)
        mlp[pl.ds(i * PATCH, PATCH), :] = (res[rows, :] + V(GAM2) * ml)[:PATCH]
        e, n = dact[rows, :], n2[rows, :]
        dn = e * V(LN2G)
        dr = g + r2[rows, 0:1] * (dn - jnp.mean(dn, axis=-1, keepdims=True) - n * jnp.mean(dn * n, axis=-1, keepdims=True))
        dres_ref[rows, :] = dr
        db = V(GAM1) * dr
        for k, t in enumerate((g * ml, e * n, e, dr * branch[rows, :], db)):
            sums[k] = sums[k] + jnp.sum(t, axis=0, keepdims=True)
        dbb = db.astype(bf16)
        dmlp[rows, :] = dbb
        datt_ref[rows, :] = mmt(dbb, wo).astype(bf16)
        sc.run(A_TAIL[i % 4])
    for k in range(5):
        dvec_ref[k + 1:k + 2, :] = sums[k]
    out_ref[...] = mlp[pl.ds(0, ni * PATCH), :].astype(bf16)
    dwo_ref[...] = mm(att_s[...].T, dmlp[...]).astype(bf16)
    keep.wait()
    last.wait()
    sc.run(A_TAIL[4])
    for slot in range(2):
        pltpu.make_async_copy(p_st.at[slot], p_out.at[0, 0], p_sem.at[slot]).wait()
        pltpu.make_async_copy(w2_st.at[slot], dw2_out.at[pl.ds(0, FC), :], w_sem.at[slot]).wait()


def fused_a(ids, tok, g, tab, idx, smalls, wq, wo, w1, w2, ni):
    R, F, S = ni * IP, w1.shape[1], jax.ShapeDtypeStruct
    v, hbm = vm(), pl.BlockSpec(memory_space=pl.ANY)
    small = S((8, 384), f32)
    six = lambda a: pltpu.VMEM((NZ, NY, NX, NC) + a.shape, a.dtype)
    row = lambda t: pltpu.VMEM((R, D), t)
    nu = 13
    bufs, s_sems = Scatter.scratch(NA)
    return pl.pallas_call(
        functools.partial(fused_a_kernel, ni, F // FC),
        in_specs=[pl.BlockSpec(memory_space=pltpu.SMEM)] + [v] * (5 + NVEC) + [hbm] * 4,
        out_shape=[S((ni * PATCH, D), bf16)] + [S((R, D), bf16)] * 4 + [S((R, D), f32), S((R, D), bf16), S((IP, IL), jnp.int32), S((8, D), f32), S((F // FC, 8, FC), f32),
                   S((D, D), bf16), S((16, D), f32), S((PR, NA * UW), f32), S((NZ, NY, NX, NC) + wq.shape, bf16), S((6, ni // 2, 2, 2, 2, IP, IL), bf16), S((NZ, NY, NX, NC, PR, UW), bf16), S((F, D), bf16)],
        out_specs=[v] * 13 + [hbm] * 4,
        scratch_shapes=[six(a) for a in (small, wq, wo, w1, w2)] + [pltpu.VMEM((HEADS, 8, 128), f32), pltpu.VMEM((IL, IL), f32), row(bf16), row(bf16),
                        pltpu.VMEM((D, R), bf16), row(bf16)] + [row(f32)] * 4 + [pltpu.VMEM((R, 128), f32), pltpu.VMEM((2, 2, 2, 2, IP, IL), bf16),
                        pltpu.VMEM((2, FC, D), bf16), pltpu.VMEM((F // FC, 8, FC), f32), pltpu.VMEM((NA + 1, NZ, NY, NX, NC, PR, UW), bf16), DMA((2,)), DMA((2,)), DMA((2,)), DMA((3, 3)), pltpu.VMEM((8, 384), f32)] + Gather.scratch(nu) + bufs + s_sems,
        compiler_params=pltpu.CompilerParams(collective_id=2, has_side_effects=True, vmem_limit_bytes=62 << 20), name="forward_and_mlp",
    )(ids, tok, g, tab, idx, *smalls, wq, wo, w1, w2)


def backward_half(p, s, q_ref, k_ref, v_ref, da_ref, probs, dqkv, dimg, dvec):
    lane = lax.broadcasted_iota(jnp.int32, (1, 128), 1)
    cols = pl.ds(pl.multiple_of(p * 128, 128), 128)
    at = lambda image, n: pl.ds(pl.multiple_of(image * IP, IP), n * IP)
    srow = at(2 * s, 2)
    kk, vv = k_ref[srow, cols], v_ref[srow, cols]
    kT = kk.T
    sq = jnp.zeros((1, 128), f32)
    dv, dk = jnp.zeros((2 * IP, 128), f32), jnp.zeros((2 * IP, 128), f32)
    for a in range(2):
        rows = at(2 * s + a, 1)
        q, da = q_ref[rows, cols], da_ref[rows, cols]
        dqs = []
        for h in range(2):
            msk = (lane < 64) if h == 0 else (lane >= 64)
            qm, dam = jnp.where(msk, q, jnp.zeros_like(q)), jnp.where(msk, da, jnp.zeros_like(da))
            pb0, pb1 = probs(a, h, 0), probs(a, h, 1)
            dp = mmt(vv, dam)
            t0, t1 = pb0.astype(f32) * dp[:IP], pb1.astype(f32) * dp[IP:]
            dl = jnp.sum(t0, axis=0, keepdims=True) + jnp.sum(t1, axis=0, keepdims=True)
            d0, d1 = t0 - pb0.astype(f32) * dl, t1 - pb1.astype(f32) * dl
            dimg[2 * p + h, :, 0:IP] += d0 if a == 0 else d1
            ds = jnp.concatenate([d0.astype(bf16), d1.astype(bf16)], axis=0)
            dv = dv + mm(jnp.concatenate([pb0, pb1], axis=0), dam)
            dk = dk + mm(ds, qm)
            dqs.append(mm(kT[h * 64:(h + 1) * 64], ds))
        dq = jnp.concatenate(dqs, axis=0).T * HEAD ** -0.5
        sq = sq + jnp.sum(dq, axis=0, keepdims=True)
        dqkv[0][rows, cols] = dq.astype(bf16)
    dqkv[1][srow, cols] = dk.astype(bf16)
    dqkv[2][srow, cols] = dv.astype(bf16)
    dvec[QB:QB + 1, cols] += sq
    dvec[VB:VB + 1, cols] += jnp.sum(dv, axis=0, keepdims=True)


def table_step(t, dimg, idx_ref, acc):
    sub8 = lax.broadcasted_iota(jnp.int32, (8, IL), 0)
    sub128 = lax.broadcasted_iota(jnp.int32, (128, IL), 0)
    at = pl.multiple_of(t * 8, 8)
    ix = idx_ref[pl.ds(at, 8), :]
    lo, hi = jnp.bitwise_and(ix, 127), jnp.right_shift(ix, 7)
    ds = [dimg[h, pl.ds(at, 8), :] for h in range(HEADS)]
    left, right = [], []
    for j in range(8):
        right.append(jnp.where(sub128 == lo[j:j + 1], 1.0, 0.0).astype(bf16))
        hm = sub8 == hi[j:j + 1]
        left.append(jnp.concatenate([jnp.where(hm, jnp.broadcast_to(d[j:j + 1], (8, IL)), 0.0) for d in ds], axis=0))
    left = jnp.concatenate(left, axis=1)
    high = left.astype(bf16)
    low = (left - high.astype(f32)).astype(bf16)
    acc[...] += mmt(jnp.concatenate([high, low], axis=0), jnp.concatenate(right, axis=1))


def fused_b_kernel(ni, table_rows, dvec_a, db1, x_ref, dres, q_ref, k_ref, v_ref, da_ref, vec, idx_ref, wq_hbm, p_hbm, d1_hbm, d2_hbm, do_hbm,
                   dtok_ref, table_ref, own_vec, own_b1, oq, oo, o1, o2,
                   wq, dq, dk, dv, dimg, act, actT, dwq, acc, tot_t, tot_a, tot_b, p_st, p_sem, w_sem, *rest):
    bufs, sems, ta, tb, tt = rest[:6], rest[6:9], rest[9:12], rest[12:15], rest[15:18]
    greet([across()])
    sc = Scatter(scatter_units((dwq, do_hbm, d1_hbm, d2_hbm), (oq, oo, o1, o2)), bufs, sems)
    for a in range(NB):
        if a not in HEAD_UNITS:
            sc.start(a)
    load = pltpu.make_async_copy(wq_hbm, wq, w_sem)
    load.start()
    ns = ni // 2
    fetch = lambda t: pltpu.make_async_copy(p_hbm.at[t // ns, lax.rem(t, ns)], p_st.at[lax.rem(t, 2)], p_sem.at[lax.rem(t, 2)])
    fetch(0).start()
    tot_a[...] = jnp.zeros_like(tot_a)
    tot_b[...] = jnp.zeros_like(tot_b)
    for k, r in ((FC2B, 0), (GAM2, 1), (LN2G, 2), (LN2B, 3), (GAM1, 4), (OUTB, 5)):
        tot_a[k:k + 1, :] = dvec_a[r:r + 1, :]
    nb = NA + 1
    for j in range(nb):
        for i in range(D // FC):
            tot_a[NVEC + j:NVEC + j + 1, i * FC:(i + 1) * FC] = db1[j * (D // FC) + i, 0:1, :]
    dimg[...] = jnp.zeros_like(dimg)

    def half(t, carry):
        p, sq = t // ns, lax.rem(t, ns)
        fetch(t).wait()

        @pl.when(t + 1 < HEADS // 2 * ns)
        def _():
            fetch(t + 1).start()
        st = p_st.at[lax.rem(t, 2)]
        at_step(t, sc.run, B_HALF)
        backward_half(p, sq, q_ref, k_ref, v_ref, da_ref, lambda a, h, b: st[a, h, b, :, 0:IP], (dq, dk, dv), dimg, tot_a)

        @pl.when(lax.rem(t, 2 * ns) == 2 * ns - 1)
        def _():
            j = p // 2
            for n, d in enumerate((dq, dk, dv)):
                part = mm(actT[...], d[:, pl.ds(pl.multiple_of(j * HG, HG), HG)]).astype(bf16)
                dwq[:, :, :, :, :, pl.ds(pl.multiple_of(j * UW + n * HG, HG), HG)] = part.reshape(NZ, NY, NX, NC, PR, HG)
        at_step(t, sc.run, {(j + 1) * 2 * ns - 1: "B%d" % a for j, a in enumerate(HEAD_UNITS)})
        return carry
    V = lambda k: vec[k:k + 1, :]
    for i in range(ni):
        rows = pl.ds(i * IP, IP)
        n, _ = ln_parts(x_ref[rows, :].astype(f32))
        act[rows, :] = (n * V(LN1G) + V(LN1B)).astype(bf16)
    actT[...] = act[...].T
    lax.fori_loop(0, HEADS // 2 * ns, half, 0)
    t_a = Total(tot_a, Total.pairs(), *ta)
    t_a.start()
    acc[...] = jnp.zeros_like(acc)

    def table(t, carry):
        table_step(t, dimg, idx_ref, acc)
        at_step(t, sc.run, B_TABLE)
        at_step(t, t_a.step, V_TABLE)
        return carry
    lax.fori_loop(0, -(-PATCH // 8), table, 0)
    tot_t[...] = acc[0:96, :] + acc[96:192, :]
    t_t = Total(tot_t, Total.pairs(), *tt)
    t_t.start()
    load.wait()
    w = wq
    sg, sb = jnp.zeros((1, D), f32), jnp.zeros((1, D), f32)
    for i in range(ni):
        rows = pl.ds(i * IP, IP)
        e = jnp.zeros((IP, D), f32)
        for j in range(3):
            left = jnp.concatenate([d[rows, j * HG:(j + 1) * HG] for d in (dq, dk, dv)], axis=1)
            e = e + mmt(left, w[:, j * UW:(j + 1) * UW])
        n, r = ln_parts(x_ref[rows, :].astype(f32))
        dn = e * V(LN1G)
        dx = dres[rows, :] + r * (dn - jnp.mean(dn, axis=-1, keepdims=True) - n * jnp.mean(dn * n, axis=-1, keepdims=True))
        dres[pl.ds(i * PATCH, PATCH), :] = dx[:PATCH]
        sg = sg + jnp.sum(e * n, axis=0, keepdims=True)
        sb = sb + jnp.sum(e, axis=0, keepdims=True)
        sc.run(B_NORM[i % 4])
        for k in T_NORM[i % 4]:
            t_t.step(k)
        for k in V_NORM[i % 4]:
            t_a.step(k)
    tot_b[LN1G:LN1G + 1, :] = sg
    tot_b[LN1B:LN1B + 1, :] = sb
    t_b = Total(tot_b, Total.groups(), *tb)
    t_b.start()
    dtok_ref[...] = dres[pl.ds(0, ni * PATCH), :].astype(bf16)
    t_a.step(4)
    t_b.step(0)
    t_t.step(3)
    t_b.step(1)
    sc.run(B_TAIL)
    t_b.step(2)
    t_t.step(4)
    tot_a[LN1G:LN1B + 1, :] = tot_b[LN1G:LN1B + 1, :]

    z, y, x, c = place()
    me = ((z * NY + y) * NX + x) * NC + c
    per = D // (NZ * NY * NX * NC)
    def pick(rows, first, width):
        one = jnp.where(lax.broadcasted_iota(jnp.int32, (D, 128), 0) == first + lax.broadcasted_iota(jnp.int32, (D, 128), 1), 1.0, 0.0).astype(bf16)
        h = rows.astype(bf16)
        m = (rows - h.astype(f32)).astype(bf16)
        l = (rows - h.astype(f32) - m.astype(f32)).astype(bf16)
        return mm(h, one) + mm(m, one) + mm(l, one)
    own_vec[...] = pick(tot_a[0:16, :], me * per, per)
    wide = nb * per
    slab = me // (D // wide)
    part = pick(tot_a[8:16, :], lax.rem(me, D // wide) * wide, wide)
    rowi = lax.broadcasted_iota(jnp.int32, (8, 128), 0)
    own_b1[...] = jnp.broadcast_to(jnp.sum(jnp.where(rowi == slab + NVEC - 8, part, 0.0), axis=0, keepdims=True), (8, 128))
    for r in range(96):
        if r % 8 < 6:
            n = min(128, table_rows - r % 8 * 128)
            table_ref[r // 8:r // 8 + 1, (r % 8) * 128:(r % 8) * 128 + n] = tot_t[r:r + 1, 0:n]


def fused_b(dvec_a, db1, x, dres, q, k, v, da, vec, idx, wq6, p, d1, d2, do, table_rows, ni):
    R, S = ni * IP, jax.ShapeDtypeStruct
    vmem, hbm = vm(), pl.BlockSpec(memory_space=pl.ANY)
    split = lambda a: a.reshape((NZ, NY, NX, NC, -1, a.shape[-1]))
    d2, do = split(d2), split(do)
    own = lambda a: S(a.shape[-2:], f32)
    bufs, sems = Scatter.scratch(NB)
    row = lambda t: pltpu.VMEM((R, D), t)
    return pl.pallas_call(
        functools.partial(fused_b_kernel, ni, table_rows),
        in_specs=[vmem] * 10 + [hbm] * 5,
        out_shape=[S((ni * PATCH, D), bf16), S((HEADS, table_rows), f32), S((16, 128), f32), S((8, 128), f32), own(wq6), own(do), own(d1), own(d2)],
        out_specs=[vmem] * 8,
        scratch_shapes=[pltpu.VMEM((D, 3 * D), bf16)] + [row(bf16)] * 3 + [pltpu.VMEM((HEADS, IP, IL), f32), row(bf16), pltpu.VMEM((D, R), bf16), pltpu.VMEM(wq6.shape, bf16),
                        pltpu.VMEM((192, 128), f32), pltpu.VMEM((96, 128), f32), pltpu.VMEM((16, D), f32), pltpu.VMEM((2, D), f32),
                        pltpu.VMEM((2, 2, 2, 2, IP, IL), bf16), DMA((2,)), DMA] + bufs + sems + Total.scratch(5, 16, D) + Total.scratch(7, 2, D) + Total.scratch(5, 96, 128),
        compiler_params=pltpu.CompilerParams(collective_id=3, has_side_effects=True, vmem_limit_bytes=62 << 20), name="attention_backward",
    )(dvec_a, db1, x, dres, q, k, v, da, vec, idx, wq6.reshape(D, 3 * D), p, d1, d2, do)


def place_kernel(per, wide, out, dtok, table, vecs, b1, oq, oo, o1a, o1b, o2, *outs):
    for a, b in ((out, outs[0]), (dtok, outs[1]), (table, outs[2]), (oq, outs[3]), (oo, outs[4]), (o2, outs[6])):
        b[...] = a[...]
    outs[5][:, 0:o1a.shape[1]] = o1a[...]
    outs[5][:, o1a.shape[1]:] = o1b[...]
    outs[7][...] = b1[0:1, 0:wide]
    for k in range(NVEC):
        outs[8 + k][...] = vecs[k:k + 1, 0:per]


def place_outputs(out, dtok, table, vecs, b1, oq, oo, o1a, o1b, o2, per, wide):
    S = jax.ShapeDtypeStruct
    like = lambda a: S(a.shape, a.dtype)
    return pl.pallas_call(
        functools.partial(place_kernel, per, wide),
        in_specs=[vm()] * 10,
        out_shape=[like(out), like(dtok), like(table), like(oq), like(oo), S((PR, o1a.shape[1] + o1b.shape[1]), f32), like(o2), S((1, wide), f32)] + [S((1, per), f32)] * NVEC,
        out_specs=[vm()] * (8 + NVEC),
        compiler_params=pltpu.CompilerParams(vmem_limit_bytes=32 << 20), name="place_outputs",
    )(out, dtok, table, vecs, b1, oq, oo, o1a, o1b, o2)


def pad_rows(a, ni):
    return jnp.pad(a.reshape(ni, PATCH, D), ((0, 0), (0, IP - PATCH), (0, 0))).reshape(ni * IP, D)


def unpad_rows(a, ni):
    return a.reshape(ni, IP, D)[:, :PATCH].reshape(ni * PATCH, D)


def local(tokens, image_ids, rel_index, rel_table, ln1_gain, ln1_bias, w_qkv, q_bias, v_bias, w_out, out_bias, gamma1,
          ln2_gain, ln2_bias, w_fc1, fc1_bias, w_fc2, fc2_bias, gamma2, out_grad):
    ni = tokens.shape[0] // PATCH
    per = ln1_gain.shape[0]
    n_dev = D // per
    small = jnp.concatenate([ln1_gain, ln1_bias, q_bias, v_bias, out_bias, gamma1, ln2_gain, ln2_bias, fc2_bias, gamma2, fc1_bias])
    me = lax.axis_index("gx") * lax.axis_size("gy") + lax.axis_index("gy")
    if (lax.axis_size("gx"), lax.axis_size("gy"), per) == (NZ * NY, NX * NC, PR):
        smalls = [a.reshape(1, -1) for a in (ln1_gain, ln1_bias, q_bias, v_bias, out_bias, gamma1, ln2_gain, ln2_bias, fc2_bias, gamma2, fc1_bias)]
        res = fused_a(image_ids, tokens, out_grad, rel_table.T, rel_index, smalls, w_qkv, w_out, w_fc1, w_fc2, ni)
        out, x, q, k, v, dres, datt, idx, dvec, db1, dwo, vec, g1, wq6, p, dw1, dw2 = res
        dtok, table_grad, own_vec, own_b1, gq, go, g1b, g2 = fused_b(dvec, db1, x, dres, q, k, v, datt, vec, idx, wq6, p, dw1, dw2, dwo, rel_table.shape[0], ni)
        res = place_outputs(out, dtok, table_grad, own_vec, own_b1, gq, go, g1, g1b, g2, per, fc1_bias.shape[0])
        out, dtok, table_grad, gq, go, g1, g2, b1 = res[:8]
        sl = [a.reshape(-1) for a in res[8:]]
        return (out, dtok, table_grad.T, sl[LN1G], sl[LN1B], gq, sl[QB], sl[VB], go, sl[OUTB], sl[GAM1], sl[LN2G], sl[LN2B], g1,
                b1.reshape(-1), g2, sl[FC2B], sl[GAM2])
    gather = lambda a: lax.all_gather(a, AXES, axis=0, tiled=True)
    wq, wo, w1, w2 = gather(w_qkv), gather(w_out), gather(w_fc1), gather(w_fc2)
    small = lax.all_gather(small, AXES, axis=0, tiled=False).reshape(n_dev, -1).astype(f32)
    vec = jnp.pad(jnp.transpose(small[:, : NVEC * per].reshape(n_dev, NVEC, per), (1, 0, 2)).reshape(NVEC, D), ((0, 16 - NVEC), (0, 0)))
    b1 = small[:, NVEC * per :].reshape(1, -1)

    x = pad_rows(tokens, ni)
    g = pad_rows(out_grad, ni)
    ids = image_ids.reshape(ni, PATCH)[:, 0]
    table_rows = rel_table.shape[0]
    tab = jnp.pad(rel_table.astype(f32).T, ((0, 0), (0, 768 - table_rows))).reshape(6, 2, 6, 128)
    idx = jnp.pad(rel_index.T, ((0, IP - PATCH), (0, IL - PATCH)))

    att, q, k, v, p = front(ids, x, wq, tab, idx, vec, ni)
    out, dres, datt, dw1, dw2, dwo, db1, dvec = mlp(x, att, g, wo, vec, w1, w2, b1, ni)
    dq, dk, dv, dimg, dvec2 = attb(q, k, v, datt, p, ni)
    dtok, dwq, dvec3, dtab = qkvb(x, dres, dq, dk, dv, wq, vec, dimg, idx, ni)

    scatter = lambda a: lax.psum_scatter(a.astype(f32), AXES, scatter_dimension=0, tiled=True)
    rows = jnp.concatenate([dvec3[0:2], dvec2[0:2], dvec[5:6], dvec[4:5], dvec[2:4], dvec[0:1], dvec[1:2], db1.reshape(-1, D), dtab.reshape(-1, D)])
    total = lax.psum(rows, AXES)
    sl = [lax.dynamic_slice(total[i], (me * per,), (per,)) for i in range(NVEC)]
    nb = db1.shape[1] // D
    db1_own = lax.dynamic_slice(total[NVEC : NVEC + nb].reshape(-1), (me * per * nb,), (per * nb,))
    table_grad = total[NVEC + nb :].reshape(HEADS, 1024)[:, :table_rows].T
    return (unpad_rows(out, ni), unpad_rows(dtok, ni), table_grad, sl[LN1G], sl[LN1B], scatter(dwq), sl[QB], sl[VB], scatter(dwo),
            sl[OUTB], sl[GAM1], sl[LN2G], sl[LN2B], scatter(dw1), db1_own, scatter(dw2), sl[FC2B], sl[GAM2])


def solution(mesh):
    rows, vecs, none = P(AXES, None), P(AXES), P()
    return jax.shard_map(
        local,
        mesh=mesh,
        in_specs=(rows, vecs, none, none, vecs, vecs, rows, vecs, vecs, rows, vecs, vecs, vecs, vecs, rows, vecs, rows, vecs, vecs, rows),
        out_specs=(rows, rows, none, vecs, vecs, rows, vecs, vecs, rows, vecs, vecs, vecs, vecs, rows, vecs, rows, vecs, vecs),
        check_vma=False,
    )
```

```python
import functools

import jax
import jax.numpy as jnp
from jax import lax
from jax.experimental import pallas as pl
from jax.experimental.pallas import tpu as pltpu
from jax.sharding import PartitionSpec as P

D=768; HEADS=12; HEAD=64; PATCH=197; IP=208; IL=256
f32=jnp.float32; bf16=jnp.bfloat16
NEG=-1e30
def mm(a,b): return jnp.dot(a,b,preferred_element_type=f32)
def mmt(a,b): return lax.dot_general(a,b,(((1,),(1,)),((),())),preferred_element_type=f32)
def vm(): return pl.BlockSpec(memory_space=pltpu.VMEM)

def ln_parts(x):
    c=x-jnp.mean(x,axis=-1,keepdims=True)
    r=lax.rsqrt(jnp.mean(c*c,axis=-1,keepdims=True)+1e-6)
    return c*r,r

def front_kernel(ni, ids_ref, x_ref, wq_ref, tab_ref, idx_ref, vec_ref, att_ref, q_out, k_out, v_out, p_ref, bias_ref):
    pid=pl.program_id(0)
    R=ni*IP
    @pl.when(pid==0)
    def _():
        for i in range(ni):
            rows=pl.ds(i*IP,IP)
            n,_=ln_parts(x_ref[rows,:].astype(f32))
            a=(n*vec_ref[0:1,:]+vec_ref[1:2,:]).astype(bf16)
            for j in range(3):
                sl=pl.ds(j*D,D)
                o=mm(a,wq_ref[:,sl])
                if j==0: q_out[rows,:]=((o+vec_ref[2:3,:])*0.125).astype(bf16)
                if j==1: k_out[rows,:]=o.astype(bf16)
                if j==2: v_out[rows,:]=(o+vec_ref[3:4,:]).astype(bf16)
    rowi=lax.broadcasted_iota(jnp.int32,(IP,128),0)
    for h in range(2):
        for l in range(2):
            idx=idx_ref[:,pl.ds(l*128,128)]
            lo=jnp.bitwise_and(idx,127); hi=jnp.right_shift(idx,7)
            acc=jnp.zeros((IP,128),f32)
            for k in range(6):
                t=jnp.broadcast_to(tab_ref[0,h,k:k+1,:],(IP,128))
                gth=jnp.take_along_axis(t,lo,axis=1,mode="promise_in_bounds")
                acc=jnp.where(hi==k,gth,acc)
            bias_ref[h,:,pl.ds(l*128,128)]=jnp.where(rowi<PATCH,acc,NEG)
    cols=pl.ds(pl.multiple_of(pid*128,128),128)
    lane=lax.broadcasted_iota(jnp.int32,(1,128),1)
    for s in range(ni//2):
        linked=ids_ref[2*s]==ids_ref[2*s+1]
        mx=jnp.where(jnp.logical_and(lax.broadcasted_iota(jnp.int32,(IP,1),0)<PATCH,linked),0.0,NEG)
        kk=k_out[pl.ds(2*s*IP,2*IP),cols]
        vT=v_out[pl.ds(2*s*IP,2*IP),cols].T
        for a in range(2):
            rows=pl.ds((2*s+a)*IP,IP)
            q=q_out[rows,cols]
            ats=[]
            for h in range(2):
                qm=jnp.where((lane<64) if h==0 else (lane>=64),q,jnp.zeros_like(q))
                st=mmt(kk,qm)
                b=bias_ref[h,:,0:IP]
                if a==0: s0=st[:IP]+b; s1=st[IP:]+mx
                else: s0=st[:IP]+mx; s1=st[IP:]+b
                m=jnp.maximum(jnp.max(s0,axis=0,keepdims=True),jnp.max(s1,axis=0,keepdims=True))
                e0=jnp.exp(s0-m); e1=jnp.exp(s1-m)
                inv=1.0/(jnp.sum(e0,axis=0,keepdims=True)+jnp.sum(e1,axis=0,keepdims=True))
                p0=(e0*inv).astype(bf16); p1=(e1*inv).astype(bf16)
                p_ref[0,s,a,h,0,:,0:IP]=p0
                p_ref[0,s,a,h,1,:,0:IP]=p1
                v_h=vT[h*64:(h+1)*64]
                ats.append(mm(v_h[:,:IP],p0)+mm(v_h[:,IP:],p1))
            att_ref[rows,cols]=jnp.concatenate(ats,axis=0).T.astype(bf16)

def front(ids,x,wq,tab,idx,vec,ni):
    R=ni*IP
    full=lambda *s: pl.BlockSpec(s,lambda p:(0,)*len(s))
    return pl.pallas_call(functools.partial(front_kernel,ni),
        grid=(6,),
        out_shape=[jax.ShapeDtypeStruct((R,D),bf16)]*4+[jax.ShapeDtypeStruct((6,ni//2,2,2,2,IP,IL),bf16)],
        in_specs=[pl.BlockSpec(memory_space=pltpu.SMEM),full(R,D),full(D,3*D),pl.BlockSpec((1,2,6,128),lambda p:(p,0,0,0)),full(IP,IL),full(16,D)],
        out_specs=[full(R,D)]*4+[pl.BlockSpec((1,ni//2,2,2,2,IP,IL),lambda p:(p,0,0,0,0,0,0))],
        scratch_shapes=[pltpu.VMEM((2,IP,IL),f32)],
        compiler_params=pltpu.CompilerParams(vmem_limit_bytes=56<<20),name="front",
    )(ids,x,wq,tab,idx,vec)

def gelu_parts(x):
    z=x*0.7071067811865476
    e=lax.erf(z)
    cdf=0.5+0.5*e
    pdf=jnp.exp(-z*z)*0.3989422804014327
    return cdf, x*pdf

FC=256
def mlp_kernel(ni, nf, x_ref, att_ref, g_ref, wo_ref, vec_ref, w1_ref, w2_ref, b1_ref,
               out_ref, dres_ref, datt_ref, dw1_ref, dw2_ref, dwo_ref, db1_ref, dvec_ref,
               res, n2, r2, branch, act2, act2T, dmlp, mlp, dact):
    pid=pl.program_id(0)
    V=lambda k: vec_ref[k:k+1,:]
    @pl.when(pid==0)
    def _():
        sb=jnp.zeros((1,D),f32)
        for i in range(ni):
            rows=pl.ds(i*IP,IP)
            br=mm(att_ref[rows,:],wo_ref[...])+V(OUTB)
            branch[rows,:]=br
            rs=x_ref[rows,:].astype(f32)+V(GAM1)*br
            res[rows,:]=rs
            n,r=ln_parts(rs)
            n2[rows,:]=n
            r2[rows,:]=jnp.broadcast_to(r,(IP,128))
            act2[rows,:]=(n*V(LN2G)+V(LN2B)).astype(bf16)
            dm=V(GAM2)*g_ref[rows,:].astype(f32)
            sb=sb+jnp.sum(dm,axis=0,keepdims=True)
            dmlp[rows,:]=dm.astype(bf16)
        act2T[...]=act2[...].T
        dvec_ref[0:1,:]=sb
        mlp[...]=jnp.zeros_like(mlp)
        dact[...]=jnp.zeros_like(dact)
    w1=w1_ref[...]; w2=w2_ref[...]
    pre=mm(act2[...],w1)+b1_ref[...]
    cdf,xpdf=gelu_parts(pre)
    hid=(pre*cdf).astype(bf16)
    dh=mmt(dmlp[...],w2)
    dp=dh*(cdf+xpdf)
    db1_ref[...]=jnp.sum(dp,axis=0,keepdims=True)
    dpb=dp.astype(bf16)
    mlp[...]+=mm(hid,w2)
    dact[...]+=mmt(dpb,w1)
    dw1_ref[...]=mm(act2T[...],dpb).astype(bf16)
    dw2_ref[...]=mm(hid.T,dmlp[...]).astype(bf16)
    @pl.when(pid==nf-1)
    def _():
        sums=[jnp.zeros((1,D),f32) for _ in range(5)]
        for i in range(ni):
            rows=pl.ds(i*IP,IP)
            g=g_ref[rows,:].astype(f32)
            ml=mlp[rows,:]+V(FC2B)
            out_ref[rows,:]=(res[rows,:]+V(GAM2)*ml).astype(bf16)
            e=dact[rows,:]; n=n2[rows,:]
            dn=e*V(LN2G)
            dr=g+r2[rows,0:1]*(dn-jnp.mean(dn,axis=-1,keepdims=True)-n*jnp.mean(dn*n,axis=-1,keepdims=True))
            dres_ref[rows,:]=dr
            db=V(GAM1)*dr
            for k,t in enumerate((g*ml,e*n,e,dr*branch[rows,:],db)):
                sums[k]=sums[k]+jnp.sum(t,axis=0,keepdims=True)
            dbb=db.astype(bf16)
            dmlp[rows,:]=dbb
            datt_ref[rows,:]=mmt(dbb,wo_ref[...]).astype(bf16)
        for k in range(5): dvec_ref[k+1:k+2,:]=sums[k]
        dwo_ref[...]=mm(att_ref[...].T,dmlp[...]).astype(bf16)

def mlp(x,att,g,wo,vec,w1,w2,b1,ni):
    R=ni*IP; F=w1.shape[1]; nf=F//FC
    full=lambda *s: pl.BlockSpec(s,lambda p:(0,)*len(s),pipeline_mode=pl.Buffered(1))
    S=jax.ShapeDtypeStruct
    return pl.pallas_call(functools.partial(mlp_kernel,ni,nf),grid=(nf,),
        in_specs=[full(R,D)]*3+[full(D,D),full(16,D),pl.BlockSpec((D,FC),lambda p:(0,p)),pl.BlockSpec((FC,D),lambda p:(p,0)),pl.BlockSpec((1,FC),lambda p:(0,p))],
        out_shape=[S((R,D),bf16),S((R,D),f32),S((R,D),bf16),S((D,F),bf16),S((F,D),bf16),S((D,D),bf16),S((1,F),f32),S((8,D),f32)],
        out_specs=[full(R,D)]*3+[pl.BlockSpec((D,FC),lambda p:(0,p)),pl.BlockSpec((FC,D),lambda p:(p,0)),full(D,D),pl.BlockSpec((1,FC),lambda p:(0,p)),full(8,D)],
        scratch_shapes=[pltpu.VMEM((R,D),f32)]*2+[pltpu.VMEM((R,128),f32),pltpu.VMEM((R,D),f32),pltpu.VMEM((R,D),bf16),pltpu.VMEM((D,R),bf16),pltpu.VMEM((R,D),bf16)]+[pltpu.VMEM((R,D),f32)]*2,
        compiler_params=pltpu.CompilerParams(vmem_limit_bytes=60<<20),name="mlp",
    )(x,att,g,wo,vec,w1,w2,b1)

def attb_kernel(ni, q_ref,k_ref,v_ref,da_ref,p_ref, dq_ref,dk_ref,dv_ref,dimg_ref,dvec_ref):
    lane=lax.broadcasted_iota(jnp.int32,(1,128),1)
    sq=jnp.zeros((1,128),f32); sv=jnp.zeros((1,128),f32)
    for s in range(ni//2):
        srow=pl.ds(2*s*IP,2*IP)
        kk=k_ref[srow,:]; vv=v_ref[srow,:]
        kT=kk.T
        dv=jnp.zeros((2*IP,128),f32); dk=jnp.zeros((2*IP,128),f32)
        for a in range(2):
            rows=pl.ds((2*s+a)*IP,IP)
            q=q_ref[rows,:]; da=da_ref[rows,:]
            dqs=[]
            for h in range(2):
                msk=(lane<64) if h==0 else (lane>=64)
                qm=jnp.where(msk,q,jnp.zeros_like(q)); dam=jnp.where(msk,da,jnp.zeros_like(da))
                pb0=p_ref[0,s,a,h,0,:,0:IP]; pb1=p_ref[0,s,a,h,1,:,0:IP]
                dp=mmt(vv,dam)
                t0=pb0.astype(f32)*dp[:IP]; t1=pb1.astype(f32)*dp[IP:]
                dl=jnp.sum(t0,axis=0,keepdims=True)+jnp.sum(t1,axis=0,keepdims=True)
                d0=t0-pb0.astype(f32)*dl; d1=t1-pb1.astype(f32)*dl
                same=d0 if a==0 else d1
                if s==0 and a==0: dimg_ref[0,h,:,0:IP]=same
                else: dimg_ref[0,h,:,0:IP]+=same
                ds=jnp.concatenate([d0.astype(bf16),d1.astype(bf16)],axis=0)
                pb=jnp.concatenate([pb0,pb1],axis=0)
                dv=dv+mm(pb,dam)
                dk=dk+mm(ds,qm)
                dqs.append(mm(kT[h*64:(h+1)*64],ds))
            dq=jnp.concatenate(dqs,axis=0).T*0.125
            sq=sq+jnp.sum(dq,axis=0,keepdims=True)
            dq_ref[rows,:]=dq.astype(bf16)
        sv=sv+jnp.sum(dv,axis=0,keepdims=True)
        dk_ref[srow,:]=dk.astype(bf16); dv_ref[srow,:]=dv.astype(bf16)
    dimg_ref[0,:,:,IP:]=jnp.zeros((2,IP,IL-IP),f32)
    dvec_ref[0:1,:]=sq; dvec_ref[1:2,:]=sv

def attb(q,k,v,da,p,ni):
    R=ni*IP; S=jax.ShapeDtypeStruct
    col=pl.BlockSpec((R,128),lambda i:(0,i))
    return pl.pallas_call(functools.partial(attb_kernel,ni),grid=(6,),
        in_specs=[col]*4+[pl.BlockSpec((1,ni//2,2,2,2,IP,IL),lambda p:(p,0,0,0,0,0,0))],
        out_shape=[S((R,D),bf16)]*3+[S((6,2,IP,IL),f32),S((8,D),f32)],
        out_specs=[col]*3+[pl.BlockSpec((1,2,IP,IL),lambda i:(i,0,0,0)),pl.BlockSpec((8,128),lambda i:(0,i))],
        compiler_params=pltpu.CompilerParams(vmem_limit_bytes=56<<20),name="attb",
    )(q,k,v,da,p)

def qkvb_kernel(ni,x_ref,dres_ref,dq_ref,dk_ref,dv_ref,wq_ref,vec_ref,dimg_ref,idx_ref,
                dtok_ref,dw_ref,dvec_ref,dtab_ref,a1T,act1,acc):
    for i in range(ni):
        rows=pl.ds(i*IP,IP)
        n,r=ln_parts(x_ref[rows,:].astype(f32))
        act1[rows,:]=(n*vec_ref[0:1,:]+vec_ref[1:2,:]).astype(bf16)
    a1T[...]=act1[...].T
    for j,r_ in enumerate((dq_ref,dk_ref,dv_ref)):
        dw_ref[:,pl.ds(j*D,D)]=mm(a1T[...],r_[...]).astype(bf16)
    sg=jnp.zeros((1,D),f32); sb=jnp.zeros((1,D),f32)
    for i in range(ni):
        rows=pl.ds(i*IP,IP)
        e=mmt(dq_ref[rows,:],wq_ref[:,0:D])+mmt(dk_ref[rows,:],wq_ref[:,D:2*D])+mmt(dv_ref[rows,:],wq_ref[:,2*D:])
        n,r=ln_parts(x_ref[rows,:].astype(f32))
        dn=e*vec_ref[0:1,:]
        dx=dres_ref[rows,:]+r*(dn-jnp.mean(dn,axis=-1,keepdims=True)-n*jnp.mean(dn*n,axis=-1,keepdims=True))
        dtok_ref[rows,:]=dx.astype(bf16)
        sg=sg+jnp.sum(e*n,axis=0,keepdims=True); sb=sb+jnp.sum(e,axis=0,keepdims=True)
    dvec_ref[0:1,:]=sg; dvec_ref[1:2,:]=sb
    acc[...]=jnp.zeros_like(acc)
    sub8=lax.broadcasted_iota(jnp.int32,(8,IL),0)
    sub128=lax.broadcasted_iota(jnp.int32,(128,IL),0)
    def body(j,_):
        ix=idx_ref[pl.ds(j,1),:]
        lo=jnp.bitwise_and(ix,127); hi=jnp.right_shift(ix,7)
        oh=jnp.where(sub128==lo,1.0,0.0).astype(bf16)
        hm=sub8==hi
        As=[]
        for h in range(HEADS):
            d=dimg_ref[h//2,h%2,pl.ds(j,1),:]
            As.append(jnp.where(hm,jnp.broadcast_to(d,(8,IL)),0.0))
        A=jnp.concatenate(As,axis=0)
        Ah=A.astype(bf16); Al=(A-Ah.astype(f32)).astype(bf16)
        acc[...]+=mmt(Ah,oh)+mmt(Al,oh)
        return 0
    lax.fori_loop(0,PATCH,body,0)
    dtab_ref[...]=acc[...]

def qkvb(x,dres,dq,dk,dv,wq,vec,dimg,idx,ni):
    R=ni*IP; S=jax.ShapeDtypeStruct
    return pl.pallas_call(functools.partial(qkvb_kernel,ni),
        in_specs=[vm()]*9,
        out_shape=[S((R,D),bf16),S((D,3*D),bf16),S((8,D),f32),S((96,128),f32)],
        out_specs=[vm()]*4,
        scratch_shapes=[pltpu.VMEM((D,R),bf16),pltpu.VMEM((R,D),bf16),pltpu.VMEM((96,128),f32)],
        compiler_params=pltpu.CompilerParams(vmem_limit_bytes=56<<20),name="qkvb",
    )(x,dres,dq,dk,dv,wq,vec,dimg,idx)


AXES = ("gx", "gy")
NVEC = 10
(LN1G, LN1B, QB, VB, OUTB, GAM1, LN2G, LN2B, FC2B, GAM2) = range(NVEC)

MESH = pl.DeviceIdType.MESH
NZ, NY, NX, NC = 4, 2, 2, 2
PR, UW = 24, 768
DMA = pltpu.SemaphoreType.DMA
ALL = slice(None)


def place():
    gx, gy = lax.axis_index("gx"), lax.axis_index("gy")
    return gx // NY, lax.rem(gx, NY), gy // NC, lax.rem(gy, NC)


def at_place(z, y, x, c):
    return (z * NY + y, x * NC + c)


def neighbours():
    z, y, x, c = place()
    line = [at_place(lax.rem(z + k, NZ), y, x, c) for k in (1, 2, 3)]
    return line, at_place(z, y, 1 - x, c), at_place(z, 1 - y, x, c), at_place(z, y, x, 1 - c)


def across():
    z, y, x, c = place()
    return at_place(z, y, 1 - x, 1 - c)


def greet(also=()):
    line, nx, ny, nc = neighbours()
    peers = line + [nx, ny, nc] + list(also)
    barrier = pltpu.get_barrier_semaphore()
    for t in peers:
        pl.semaphore_signal(barrier, inc=1, device_id=t, device_id_type=MESH)
    pl.semaphore_wait(barrier, len(peers))


def remote(src, dst, send, recv, to):
    return pltpu.make_async_remote_copy(src_ref=src, dst_ref=dst, send_sem=send, recv_sem=recv, device_id=to, device_id_type=MESH)


class Gather:
    def __init__(self, units, local, z_s, z_r, p_s, p_r, d_s, d_r, c_s, c_r):
        self.u = units
        self.local, self.z_s, self.z_r, self.p_s, self.p_r, self.d_s, self.d_r, self.c_s, self.c_r = local, z_s, z_r, p_s, p_r, d_s, d_r, c_s, c_r
        self.pos = place()
        self.line, self.nx, self.ny, self.nc = neighbours()

    @staticmethod
    def scratch(n):
        return [DMA((n,)), DMA((n, 3)), DMA((n, 3)), DMA((n, 2)), DMA((n, 2)), DMA((n, 2)), DMA((n, 2)), DMA((n, 4)), DMA((n, 4))]

    def first(self, a):
        z, y, x, c = self.pos
        src, view, plane = self.u[a]
        to = view(z if plane is None else plane, y, x, c)
        mine = [] if src is None else [pltpu.make_async_copy(src, to, self.local.at[a])]
        src = to if src is None else src
        return mine + [remote(src, to, self.z_s.at[a, k], self.z_r.at[a, k if plane is None else 0], self.line[k]) for k in range(3)]

    def start(self, a):
        plane = self.u[a][2]
        if plane is None:
            for d in self.first(a):
                d.start()
        else:
            @pl.when(self.pos[0] == plane)
            def _():
                for d in self.first(a):
                    d.start()

    def arrive(self, a):
        plane = self.u[a][2]
        if plane is None:
            for d in self.first(a):
                d.wait()
        else:
            @pl.when(self.pos[0] == plane)
            def _():
                mine, *sent = self.first(a)
                mine.wait()
                for d in sent:
                    d.wait_send()

            @pl.when(self.pos[0] != plane)
            def _():
                z, y, x, c = self.pos
                src, view, plane = self.u[a]
                remote(src, view(plane, y, x, c), self.z_s.at[a, 0], self.z_r.at[a, 0], self.line[0]).wait_recv()

    def to_plane(self, a):
        z, y, x, c = self.pos
        _, view, plane = self.u[a]
        v = view(ALL if plane is None else plane, y, x, c)
        return (remote(v, v, self.p_s.at[a, 0], self.p_r.at[a, 0], self.nx), remote(v, v, self.p_s.at[a, 1], self.p_r.at[a, 1], self.ny))

    def to_diagonal(self, a):
        z, y, x, c = self.pos
        _, view, plane = self.u[a]
        if plane is None:
            vx, vy = view(slice(0, 2), y, 1 - x, c), view(slice(2, 4), 1 - y, x, c)
        else:
            vx, vy = view(plane, y, 1 - x, c), view(plane, 1 - y, x, c)
            half = vx.shape[0] // 2
            vx, vy = vx.at[pl.ds(0, half)], vy.at[pl.ds(half, half)]
        return (remote(vx, vx, self.d_s.at[a, 0], self.d_r.at[a, 0], self.ny), remote(vy, vy, self.d_s.at[a, 1], self.d_r.at[a, 1], self.nx))

    def to_sibling(self, a, k):
        z, y, x, c = self.pos
        _, view, plane = self.u[a]
        v = view(ALL if plane is None else plane, (y, y, 1 - y, 1 - y)[k], (x, 1 - x, x, 1 - x)[k], c)
        return remote(v, v, self.c_s.at[a, k], self.c_r.at[a, k], self.nc)

    def plane(self, a):
        self.arrive(a)
        for d in self.to_plane(a):
            d.start()
        self.to_sibling(a, 0).start()

    def diagonal(self, a):
        for d in self.to_plane(a):
            d.wait()
        for d in self.to_diagonal(a):
            d.start()
        self.to_sibling(a, 1).start()
        self.to_sibling(a, 2).start()

    def sibling(self, a):
        for d in self.to_diagonal(a):
            d.wait()
        self.to_sibling(a, 3).start()

    def finish(self, a):
        for k in range(4):
            self.to_sibling(a, k).wait()

    def run(self, text):
        for word in text.split():
            {"P": self.plane, "D": self.diagonal, "S": self.sibling, "F": self.finish}[word[0]](int(word[1:]))


class Scatter:
    def __init__(self, units, bufs, sems):
        self.u = units
        self.own, self.rc, self.rx, self.ry, self.r3, self.rz = bufs
        self.sems = sems
        self.pos = place()
        self.line, self.nx, self.ny, self.nc = neighbours()
        self.line_z = [lax.rem(self.pos[0] + k, NZ) for k in (1, 2, 3)]

    @staticmethod
    def scratch(n):
        v = lambda *s: pltpu.VMEM((n,) + s + (PR, UW), bf16)
        return [v(NZ, NY, NX), v(NZ, NY, NX), v(2, NY), v(2, NX), v(NZ), v(3)], [DMA((n,)), DMA((n, 8)), DMA((n, 8))]

    def copy(self, a, k, src, dst, to):
        return remote(src, dst, self.sems[1].at[a, k], self.sems[2].at[a, k], to)

    def one(self, a):
        c = self.pos[3]
        view = self.u[a][0]
        mine = pltpu.make_async_copy(view(ALL, ALL, ALL, c), self.own.at[a], self.sems[0].at[a])
        return mine, self.copy(a, 0, view(ALL, ALL, ALL, 1 - c), self.rc.at[a], self.nc)

    def two(self, a):
        z, y, x, c = self.pos
        own = self.own.at[a]
        return (self.copy(a, 1, own.at[0:2, :, 1 - x], self.rx.at[a], self.nx), self.copy(a, 2, own.at[2:4, 1 - y, :], self.ry.at[a], self.ny))

    def three(self, a):
        z, y, x, c = self.pos
        own, r3 = self.own.at[a], self.r3.at[a]
        return (self.copy(a, 3, own.at[0:2, 1 - y, x], r3.at[0:2], self.ny), self.copy(a, 4, own.at[2:4, y, 1 - x], r3.at[2:4], self.nx))

    def four(self, a):
        z, y, x, c = self.pos
        own = self.own.at[a]
        return [self.copy(a, 5 + k, own.at[self.line_z[k], y, x], self.rz.at[a, k], self.line[k]) for k in range(3)]

    def start(self, a):
        for d in self.one(a):
            d.start()

    def plane(self, a):
        for d in self.one(a):
            d.wait()
        own, rc = self.own.at[a], self.rc.at[a]

        @pl.loop(0, NZ)
        def _(i):
            own[i] = own[i] + rc[i]
        for d in self.two(a):
            d.start()

    def diagonal(self, a):
        z, y, x, c = self.pos
        for d in self.two(a):
            d.wait()
        own, rx, ry = self.own.at[a], self.rx.at[a], self.ry.at[a]
        for i in range(2):
            for j in range(2):
                own[i, j, x] = own[i, j, x] + rx[i, j]
                own[2 + i, y, j] = own[2 + i, y, j] + ry[i, j]
        for d in self.three(a):
            d.start()

    def along(self, a):
        z, y, x, c = self.pos
        for d in self.three(a):
            d.wait()
        own, r3 = self.own.at[a], self.r3.at[a]
        for i in range(NZ):
            own[i, y, x] = own[i, y, x] + r3[i]
        for d in self.four(a):
            d.start()

    def finish(self, a):
        z, y, x, c = self.pos
        for d in self.four(a):
            d.wait()
        own, rz = self.own.at[a], self.rz.at[a]
        total = own[z, y, x].astype(f32)
        for k in range(3):
            total = total + rz[k].astype(f32)
        self.u[a][1](total)

    def run(self, text):
        for word in text.split():
            {"B": self.start, "P": self.plane, "D": self.diagonal, "L": self.along, "F": self.finish}[word[0]](int(word[1:]))


class Total:
    def __init__(self, ref, hops, bufs, s_s, s_r):
        self.ref, self.hops, self.bufs, self.s, self.r = ref, hops, bufs, s_s, s_r

    @staticmethod
    def pairs():
        z, y, x, c = place()
        near = z + 1 - 2 * lax.rem(z, 2)
        _, nx, ny, nc = neighbours()
        return [[nc], [nx], [ny], [at_place(near, y, x, c)], [at_place(lax.rem(z + 2, NZ), y, x, c)]]

    @staticmethod
    def groups():
        line, nx, ny, nc = neighbours()
        return [[nc, nx, across()], [ny], line]

    @staticmethod
    def scratch(n, *shape):
        return [pltpu.VMEM((n,) + shape, f32), DMA((n,)), DMA((n,))]

    def copies(self, k):
        first = sum(len(h) for h in self.hops[:k])
        return [remote(self.ref, self.bufs.at[first + i], self.s.at[first + i], self.r.at[first + i], to) for i, to in enumerate(self.hops[k])]

    def start(self):
        for d in self.copies(0):
            d.start()

    def step(self, k):
        for d in self.copies(k):
            d.wait()
        first = sum(len(h) for h in self.hops[:k])
        for i in range(len(self.hops[k])):
            self.ref[...] = self.ref[...] + self.bufs[first + i]
        if k + 1 < len(self.hops):
            for d in self.copies(k + 1):
                d.start()


def columns(src, j):
    return src.at[:, pl.ds(j * UW, UW)]


def gather_units(shards, gathered):
    (small, wq, wo, w1, w2), (gsmall, gq, go, g1, g2) = shards, gathered
    cols = lambda src, dst, j: (columns(src, j), lambda z, y, x, c: dst.at[z, y, x, c, :, pl.ds(j * UW, UW)], None)
    units = [(small, lambda z, y, x, c: gsmall.at[z, y, x, c], None)]
    units += [(None, lambda z, y, x, c, j=j: gq.at[z, y, x, c, :, pl.ds(j * UW, UW)], None) for j in range(3)] + [cols(wo, go, 0)]
    for j in range(NZ):
        units += [(w2, lambda z, y, x, c: g2.at[z, y, x, c], j), cols(w1, g1, j)]
    return units


def owned(out, rows, cols):
    def store(total):
        out[rows, cols] = total
    return store


def scatter_units(grads, outs):
    (dq, do, d1, d2), (oq, oo, o1, o2) = grads, outs

    def keep_heads(j):
        def store(total):
            for t in range(3):
                oq[:, t * D + j * HG:t * D + (j + 1) * HG] = total[:, t * HG:(t + 1) * HG]
        return store
    part = lambda src, j: lambda z, y, x, c: src.at[z, y, x, c, :, pl.ds(j * UW, UW)]
    two = [(lambda z, y, x, c, j=j: d2.at[z, y, x, c, pl.ds(j * PR, PR), :], owned(o2, slice(j * PR, (j + 1) * PR), ALL)) for j in range(4)]
    heads = [(part(dq, j), keep_heads(j)) for j in range(3)]
    return [(part(d1, 0), owned(o1, ALL, ALL)), two[0], two[1], heads[0], two[2], two[3], heads[1], (part(do, 0), owned(oo, ALL, ALL)), heads[2]]


HEAD_UNITS = (3, 6, 8)
HG = 256
NB = 9
NA = 3

A_HEAD = ('P0', 'P1 D0', 'S0 P2', 'D1 F0', 'S1 P3', 'F1 D2 P4')
A_HALF = {0: 'P5 S2', 1: 'D3', 2: 'P6 F2', 3: 'D4', 4: 'P7 S3', 5: 'D5', 6: 'P8 S4 F3', 7: 'D6', 8: 'P9 S5 F4', 9: 'D7', 10: 'P10 S6 F5', 11: 'D8'}
A_MID = 'P11 S7 F6'
A_CHUNK = {0: 'D9 P12', 1: 'S8 F7', 2: 'D10 F8', 3: 'S9 D11', 4: 'F9 S10', 5: 'D12 F10', 6: 'S11', 7: 'F11', 8: 'S12', 9: 'F12'}
A_SCATTER = {3: "B0", 4: "P0", 6: "D0 B1", 7: "P1", 8: "L0", 9: "D1 B2", 10: "P2 F0", 11: "L1"}
A_TAIL = ("D2", "F1", "", "L2", "F2")
B_HALF = {0: "P0", 1: "P1", 3: "D0 P2", 4: "D1", 5: "P3", 6: "D2 L0", 7: "P4 L1", 8: "D3", 9: "P5 L2 F0", 10: "D4 F1", 11: "P6 L3 F2"}
B_TABLE = {0: "P7 D5", 6: "L4 F3", 8: "D6", 12: "P8", 16: "L5 F4 D7", 20: "L6"}
B_NORM = ("F5 D8", "L7 F6", "", "L8")
T_NORM = ((), (0,), (1,), (2,))
B_TAIL = "F7 F8"
V_TABLE = {6: 0, 18: 1}
V_NORM = ((2,), (), (3,), ())


def spread(base, k, part, per):
    rows = lax.broadcasted_iota(jnp.int32, (part.shape[0], D), 0)
    lanes = lax.broadcasted_iota(jnp.int32, (part.shape[0], D), 1)
    full = mm(part, jnp.where(base == k, 1.0, 0.0).astype(bf16))
    return lambda first: jnp.sum(jnp.where(rows == first + lanes // per, full, 0.0), axis=0, keepdims=True)


def bias_at(h):
    return pl.ds(pl.multiple_of(h // 3 * IP, 8), IP), pl.multiple_of(lax.rem(h, 3) * IL, IL)


def head_bias(h, tab, idxT, bias_s):
    rowi = lax.broadcasted_iota(jnp.int32, (IP, 128), 0)
    rows, first = bias_at(h)
    for l in range(2):
        idx = idxT[:, pl.ds(l * 128, 128)]
        lo, hi = jnp.bitwise_and(idx, 127), jnp.right_shift(idx, 7)
        acc = jnp.zeros((IP, 128), f32)
        for k in range(6):
            t = jnp.broadcast_to(tab[h, k:k + 1, :], (IP, 128))
            acc = jnp.where(hi == k, jnp.take_along_axis(t, lo, axis=1, mode="promise_in_bounds"), acc)
        bias_s[rows, pl.ds(first + l * 128, 128)] = jnp.where(rowi < PATCH, acc, NEG)


def forward_half(p, s, ids_ref, q_s, k_s, v_s, att_s, bias_s, put):
    cols = pl.ds(pl.multiple_of(p * 128, 128), 128)
    lane = lax.broadcasted_iota(jnp.int32, (1, 128), 1)
    at = lambda image, n: pl.ds(pl.multiple_of(image * IP, IP), n * IP)
    linked = ids_ref[2 * s * PATCH] == ids_ref[(2 * s + 1) * PATCH]
    mx = jnp.where(jnp.logical_and(lax.broadcasted_iota(jnp.int32, (IP, 1), 0) < PATCH, linked), 0.0, NEG)
    kk = k_s[at(2 * s, 2), cols]
    vT = v_s[at(2 * s, 2), cols].T
    for a in range(2):
        q = q_s[at(2 * s + a, 1), cols]
        ats = []
        for h in range(2):
            qm = jnp.where((lane < 64) if h == 0 else (lane >= 64), q, jnp.zeros_like(q))
            st = mmt(kk, qm)
            rows_b, first = bias_at(2 * p + h)
            b = bias_s[rows_b, pl.ds(first, IL)][:, 0:IP]
            s0, s1 = (st[:IP] + b, st[IP:] + mx) if a == 0 else (st[:IP] + mx, st[IP:] + b)
            m = jnp.maximum(jnp.max(s0, axis=0, keepdims=True), jnp.max(s1, axis=0, keepdims=True))
            e0, e1 = jnp.exp(s0 - m), jnp.exp(s1 - m)
            inv = 1.0 / (jnp.sum(e0, axis=0, keepdims=True) + jnp.sum(e1, axis=0, keepdims=True))
            p0, p1 = (e0 * inv).astype(bf16), (e1 * inv).astype(bf16)
            put(a, h, 0, p0)
            put(a, h, 1, p1)
            v_h = vT[h * 64:(h + 1) * 64]
            ats.append(mm(v_h[:, :IP], p0) + mm(v_h[:, IP:], p1))
        att_s[at(2 * s + a, 1), cols] = jnp.concatenate(ats, axis=0).T.astype(bf16)


def at_step(i, run, plan):
    for when, text in plan.items():
        @pl.when(i == when)
        def _(text=text):
            run(text)


def fused_a_kernel(ni, nf, ids_ref, tok_ref, g_ref, tab_ref, idx_ref, *refs):
    smalls, refs = refs[:NVEC + 1], refs[NVEC + 1:]
    fused_a_body(ni, nf, smalls, ids_ref, tok_ref, g_ref, tab_ref, idx_ref, *refs)


def fused_a_body(ni, nf, smalls, ids_ref, tok_ref, g_ref, tab_ref, idx_ref, wq_ref, wo_ref, w1_ref, w2_ref,
                   out_ref, x_out, q_s, k_s, v_s, dres_ref, datt_ref, idx_out, dvec_ref, db1_ref, dwo_ref, vec, o1_ref,
                   wq_out, p_out, dw1_out, dw2_out,
                   gs, gq, go, g1, g2, tab, square, att_s, act, actT, dmlp, res, n2, branch, mlp, r2,
                   p_st, w2_st, b1, g_b, p_sem, w_sem, q_sem, h_sem, small_ref, *rest):
    R = ni * IP
    dact, gp = dres_ref, datt_ref
    z, y, x, c = place()
    blocks = [pltpu.make_async_copy(wq_ref.at[:, pl.ds(t * D + j * HG, HG)], gq.at[z, y, x, c, :, pl.ds(j * UW + t * HG, HG)], h_sem.at[j, t])
              for j in range(3) for t in range(3)]
    for d in blocks:
        d.start()
    first = 0
    small_ref[...] = jnp.zeros_like(small_ref)
    for r in smalls:
        small_ref[0:1, first:first + r.shape[1]] = r[...].astype(f32)
        first += r.shape[1]
    greet()
    for d in blocks:
        d.wait()
    ga = Gather(gather_units((small_ref, wq_ref, wo_ref, w1_ref, w2_ref), (gs, gq, go, g1, g2)), *rest[:9])
    part_of = lambda j: lambda z, y, x, c: g_b.at[j, z, y, x, c]
    sc = Scatter([(part_of(j), owned(o1_ref, ALL, slice(j * UW, (j + 1) * UW))) for j in range(NA)], rest[9:15], rest[15:18])
    for a in range(len(ga.u)):
        ga.start(a)
    def padded(src, dst):
        res[pl.ds(0, ni * PATCH), :] = src[...].astype(f32)
        for i in range(ni):
            dst[pl.ds(i * IP, PATCH), :] = res[pl.ds(i * PATCH, PATCH), :].astype(bf16)
            dst[pl.ds(i * IP + PATCH, IP - PATCH), :] = jnp.zeros((IP - PATCH, D), bf16)
    def biases(first, last):
        def one(h, carry):
            head_bias(h, tab, idx_out, branch)
            return carry
        lax.fori_loop(first, last, one, 0)
    tab[...] = jnp.zeros_like(tab)
    for k in range(6):
        n = min(128, tab_ref.shape[1] - k * 128)
        piece = tab_ref[:, k * 128:k * 128 + n].astype(f32)
        for h in range(HEADS):
            tab[h, k:k + 1, 0:n] = piece[h:h + 1]
    square[...] = jnp.zeros_like(square)
    square[0:PATCH, 0:PATCH] = idx_ref[...].astype(f32)
    idx_out[...] = square[...].T[0:IP].astype(jnp.int32)
    padded(tok_ref, x_out)
    ga.run(A_HEAD[0])
    for i in range(ni):
        rows = pl.ds(i * IP, IP)
        n2[rows, :], _ = ln_parts(x_out[rows, :].astype(f32))
    biases(0, 2)
    ga.run(A_HEAD[1])
    biases(2, 4)
    ga.run(A_HEAD[2])
    biases(4, 6)
    ga.run(A_HEAD[3])
    n_small = NZ * NY * NX * NC
    flat = gs.reshape(n_small * 8, 384)
    part = jnp.concatenate([flat[8 * d:8 * d + 1, :] for d in range(n_small)], axis=0).astype(bf16)
    per = D // n_small
    base = lax.broadcasted_iota(jnp.int32, (384, D), 0) - lax.rem(lax.broadcasted_iota(jnp.int32, (384, D), 1), per)
    for k in range(NVEC):
        vec[k:k + 1, :] = spread(base, k * per, part, per)(0)
    V = lambda k: vec[k:k + 1, :]
    for i in range(ni):
        rows = pl.ds(i * IP, IP)
        act[rows, :] = (n2[rows, :] * V(LN1G) + V(LN1B)).astype(bf16)
    ga.run(A_HEAD[4])
    biases(6, 9)
    ga.run(A_HEAD[5])
    padded(g_ref, gp)
    base1 = lax.broadcasted_iota(jnp.int32, (384, D), 0) - lax.rem(lax.broadcasted_iota(jnp.int32, (384, D), 1), 4 * per)
    sp = spread(base1, NVEC * per, part, 4 * per)
    for j in range(nf * FC // D):
        line = sp(j * (D // (4 * per)))
        for i in range(D // FC):
            b1[j * (D // FC) + i, 0:1, :] = line[:, i * FC:(i + 1) * FC]

    biases(9, 12)

    ns = ni // 2

    def half(t, carry):
        p, sq = t // ns, lax.rem(t, ns)
        at_step(t, ga.run, A_HALF)

        @pl.when(lax.rem(t, 2 * ns) == 0)
        def _():
            j = p // 2
            w = gq[:, :, :, :, :, pl.ds(pl.multiple_of(j * UW, UW), UW)].reshape(D, UW)
            cols = pl.ds(pl.multiple_of(j * HG, HG), HG)
            qb, vb = vec[QB:QB + 1, cols], vec[VB:VB + 1, cols]
            for i in range(ni):
                rows = pl.ds(i * IP, IP)
                o = mm(act[rows, :], w)
                q_s[rows, cols] = ((o[:, :HG] + qb) * HEAD ** -0.5).astype(bf16)
                k_s[rows, cols] = o[:, HG:2 * HG].astype(bf16)
                v_s[rows, cols] = (o[:, 2 * HG:] + vb).astype(bf16)

        slot = lax.rem(t, 2)
        st = p_st.at[slot]
        cp = pltpu.make_async_copy(st, p_out.at[p, sq], p_sem.at[slot])

        @pl.when(t >= 2)
        def _():
            pltpu.make_async_copy(st, p_out.at[p, sq], p_sem.at[slot]).wait()

        def put(a, h, b, v):
            st[a, h, b, :, 0:IP] = v
        forward_half(p, sq, ids_ref, q_s, k_s, v_s, att_s, branch, put)
        cp.start()
        return carry
    lax.fori_loop(0, HEADS // 2 * ns, half, 0)
    keep = pltpu.make_async_copy(gq, wq_out, q_sem.at[0])
    keep.start()
    ga.run(A_MID)

    sb = jnp.zeros((1, D), f32)
    wo = go[...].reshape(D, D)
    for i in range(ni):
        rows = pl.ds(i * IP, IP)
        br = mm(att_s[rows, :], wo) + V(OUTB)
        branch[rows, :] = br
        rs = x_out[rows, :].astype(f32) + V(GAM1) * br
        res[rows, :] = rs
        n, r = ln_parts(rs)
        n2[rows, :] = n
        r2[rows, :] = jnp.broadcast_to(r, (IP, 128))
        act[rows, :] = (n * V(LN2G) + V(LN2B)).astype(bf16)
        dm = V(GAM2) * gp[rows, :].astype(f32)
        sb = sb + jnp.sum(dm, axis=0, keepdims=True)
        dmlp[rows, :] = dm.astype(bf16)
    actT[...] = act[...].T
    dvec_ref[0:1, :] = sb
    mlp[...] = jnp.zeros_like(mlp)
    dact[...] = jnp.zeros_like(dact)
    g2v = g2.reshape(nf * FC, D)

    def chunk(c, carry):
        slot = lax.rem(c, 2)
        at = pl.multiple_of(c * FC, FC)
        at_step(c, ga.run, A_CHUNK)
        at_step(c, sc.run, A_SCATTER)
        w1, w2 = g1[:, :, :, :, :, pl.ds(at, FC)].reshape(D, FC), g2v[pl.ds(at, FC), :]
        cp = pltpu.make_async_copy(w2_st.at[slot], dw2_out.at[pl.ds(at, FC), :], w_sem.at[slot])
        pre = mm(act[...], w1) + b1[c, 0:1, :]
        cdf, xpdf = gelu_parts(pre)
        hid = (pre * cdf).astype(bf16)
        dp = mmt(dmlp[...], w2) * (cdf + xpdf)
        db1_ref[c, 0:1, :] = jnp.sum(dp, axis=0, keepdims=True)
        dpb = dp.astype(bf16)
        mlp[...] += mm(hid, w2)
        dact[...] += mmt(dpb, w1)

        @pl.when(c >= 2)
        def _():
            pltpu.make_async_copy(w2_st.at[slot], dw2_out.at[pl.ds(at, FC), :], w_sem.at[slot]).wait()
        g_b[c // (D // FC), :, :, :, :, :, pl.ds(pl.multiple_of(lax.rem(c, D // FC) * FC, FC), FC)] = mm(actT[...], dpb).astype(bf16).reshape(NZ, NY, NX, NC, PR, FC)
        w2_st[slot] = mm(hid.T, dmlp[...]).astype(bf16)
        cp.start()
        return carry
    lax.fori_loop(0, nf, chunk, 0)
    last = pltpu.make_async_copy(g_b.at[NA], dw1_out, q_sem.at[1])
    last.start()

    wo = go[...].reshape(D, D)
    sums = [jnp.zeros((1, D), f32) for _ in range(5)]
    for i in range(ni):
        rows = pl.ds(i * IP, IP)
        g = gp[rows, :].astype(f32)
        ml = mlp[rows, :] + V(FC2B)
        mlp[pl.ds(i * PATCH, PATCH), :] = (res[rows, :] + V(GAM2) * ml)[:PATCH]
        e, n = dact[rows, :], n2[rows, :]
        dn = e * V(LN2G)
        dr = g + r2[rows, 0:1] * (dn - jnp.mean(dn, axis=-1, keepdims=True) - n * jnp.mean(dn * n, axis=-1, keepdims=True))
        dres_ref[rows, :] = dr
        db = V(GAM1) * dr
        for k, t in enumerate((g * ml, e * n, e, dr * branch[rows, :], db)):
            sums[k] = sums[k] + jnp.sum(t, axis=0, keepdims=True)
        dbb = db.astype(bf16)
        dmlp[rows, :] = dbb
        datt_ref[rows, :] = mmt(dbb, wo).astype(bf16)
        sc.run(A_TAIL[i % 4])
    for k in range(5):
        dvec_ref[k + 1:k + 2, :] = sums[k]
    out_ref[...] = mlp[pl.ds(0, ni * PATCH), :].astype(bf16)
    dwo_ref[...] = mm(att_s[...].T, dmlp[...]).astype(bf16)
    keep.wait()
    last.wait()
    sc.run(A_TAIL[4])
    for slot in range(2):
        pltpu.make_async_copy(p_st.at[slot], p_out.at[0, 0], p_sem.at[slot]).wait()
        pltpu.make_async_copy(w2_st.at[slot], dw2_out.at[pl.ds(0, FC), :], w_sem.at[slot]).wait()


def fused_a(ids, tok, g, tab, idx, smalls, wq, wo, w1, w2, ni):
    R, F, S = ni * IP, w1.shape[1], jax.ShapeDtypeStruct
    v, hbm = vm(), pl.BlockSpec(memory_space=pl.ANY)
    small = S((8, 384), f32)
    six = lambda a: pltpu.VMEM((NZ, NY, NX, NC) + a.shape, a.dtype)
    row = lambda t: pltpu.VMEM((R, D), t)
    nu = 13
    bufs, s_sems = Scatter.scratch(NA)
    return pl.pallas_call(
        functools.partial(fused_a_kernel, ni, F // FC),
        in_specs=[pl.BlockSpec(memory_space=pltpu.SMEM)] + [v] * (5 + NVEC) + [hbm] * 4,
        out_shape=[S((ni * PATCH, D), bf16)] + [S((R, D), bf16)] * 4 + [S((R, D), f32), S((R, D), bf16), S((IP, IL), jnp.int32), S((8, D), f32), S((F // FC, 8, FC), f32),
                   S((D, D), bf16), S((16, D), f32), S((PR, NA * UW), f32), S((NZ, NY, NX, NC) + wq.shape, bf16), S((6, ni // 2, 2, 2, 2, IP, IL), bf16), S((NZ, NY, NX, NC, PR, UW), bf16), S((F, D), bf16)],
        out_specs=[v] * 13 + [hbm] * 4,
        scratch_shapes=[six(a) for a in (small, wq, wo, w1, w2)] + [pltpu.VMEM((HEADS, 8, 128), f32), pltpu.VMEM((IL, IL), f32), row(bf16), row(bf16),
                        pltpu.VMEM((D, R), bf16), row(bf16)] + [row(f32)] * 4 + [pltpu.VMEM((R, 128), f32), pltpu.VMEM((2, 2, 2, 2, IP, IL), bf16),
                        pltpu.VMEM((2, FC, D), bf16), pltpu.VMEM((F // FC, 8, FC), f32), pltpu.VMEM((NA + 1, NZ, NY, NX, NC, PR, UW), bf16), DMA((2,)), DMA((2,)), DMA((2,)), DMA((3, 3)), pltpu.VMEM((8, 384), f32)] + Gather.scratch(nu) + bufs + s_sems,
        compiler_params=pltpu.CompilerParams(collective_id=2, has_side_effects=True, vmem_limit_bytes=62 << 20), name="forward_and_mlp",
    )(ids, tok, g, tab, idx, *smalls, wq, wo, w1, w2)


def backward_half(p, s, q_ref, k_ref, v_ref, da_ref, probs, dqkv, dimg, dvec):
    lane = lax.broadcasted_iota(jnp.int32, (1, 128), 1)
    cols = pl.ds(pl.multiple_of(p * 128, 128), 128)
    at = lambda image, n: pl.ds(pl.multiple_of(image * IP, IP), n * IP)
    srow = at(2 * s, 2)
    kk, vv = k_ref[srow, cols], v_ref[srow, cols]
    kT = kk.T
    sq = jnp.zeros((1, 128), f32)
    dv, dk = jnp.zeros((2 * IP, 128), f32), jnp.zeros((2 * IP, 128), f32)
    for a in range(2):
        rows = at(2 * s + a, 1)
        q, da = q_ref[rows, cols], da_ref[rows, cols]
        dqs = []
        for h in range(2):
            msk = (lane < 64) if h == 0 else (lane >= 64)
            qm, dam = jnp.where(msk, q, jnp.zeros_like(q)), jnp.where(msk, da, jnp.zeros_like(da))
            pb0, pb1 = probs(a, h, 0), probs(a, h, 1)
            dp = mmt(vv, dam)
            t0, t1 = pb0.astype(f32) * dp[:IP], pb1.astype(f32) * dp[IP:]
            dl = jnp.sum(t0, axis=0, keepdims=True) + jnp.sum(t1, axis=0, keepdims=True)
            d0, d1 = t0 - pb0.astype(f32) * dl, t1 - pb1.astype(f32) * dl
            dimg[2 * p + h, :, 0:IP] += d0 if a == 0 else d1
            ds = jnp.concatenate([d0.astype(bf16), d1.astype(bf16)], axis=0)
            dv = dv + mm(jnp.concatenate([pb0, pb1], axis=0), dam)
            dk = dk + mm(ds, qm)
            dqs.append(mm(kT[h * 64:(h + 1) * 64], ds))
        dq = jnp.concatenate(dqs, axis=0).T * HEAD ** -0.5
        sq = sq + jnp.sum(dq, axis=0, keepdims=True)
        dqkv[0][rows, cols] = dq.astype(bf16)
    dqkv[1][srow, cols] = dk.astype(bf16)
    dqkv[2][srow, cols] = dv.astype(bf16)
    dvec[QB:QB + 1, cols] += sq
    dvec[VB:VB + 1, cols] += jnp.sum(dv, axis=0, keepdims=True)


def table_step(t, dimg, idx_ref, acc):
    sub8 = lax.broadcasted_iota(jnp.int32, (8, IL), 0)
    sub128 = lax.broadcasted_iota(jnp.int32, (128, IL), 0)
    at = pl.multiple_of(t * 8, 8)
    ix = idx_ref[pl.ds(at, 8), :]
    lo, hi = jnp.bitwise_and(ix, 127), jnp.right_shift(ix, 7)
    ds = [dimg[h, pl.ds(at, 8), :] for h in range(HEADS)]
    left, right = [], []
    for j in range(8):
        right.append(jnp.where(sub128 == lo[j:j + 1], 1.0, 0.0).astype(bf16))
        hm = sub8 == hi[j:j + 1]
        left.append(jnp.concatenate([jnp.where(hm, jnp.broadcast_to(d[j:j + 1], (8, IL)), 0.0) for d in ds], axis=0))
    left = jnp.concatenate(left, axis=1)
    high = left.astype(bf16)
    low = (left - high.astype(f32)).astype(bf16)
    acc[...] += mmt(jnp.concatenate([high, low], axis=0), jnp.concatenate(right, axis=1))


def fused_b_kernel(ni, table_rows, dvec_a, db1, x_ref, dres, q_ref, k_ref, v_ref, da_ref, vec, idx_ref, wq_hbm, p_hbm, d1_hbm, d2_hbm, do_hbm,
                   dtok_ref, table_ref, own_vec, own_b1, oq, oo, o1, o2,
                   wq, dq, dk, dv, dimg, act, actT, dwq, acc, tot_t, tot_a, tot_b, p_st, p_sem, w_sem, *rest):
    bufs, sems, ta, tb, tt = rest[:6], rest[6:9], rest[9:12], rest[12:15], rest[15:18]
    greet([across()])
    sc = Scatter(scatter_units((dwq, do_hbm, d1_hbm, d2_hbm), (oq, oo, o1, o2)), bufs, sems)
    for a in range(NB):
        if a not in HEAD_UNITS:
            sc.start(a)
    load = pltpu.make_async_copy(wq_hbm, wq, w_sem)
    load.start()
    ns = ni // 2
    fetch = lambda t: pltpu.make_async_copy(p_hbm.at[t // ns, lax.rem(t, ns)], p_st.at[lax.rem(t, 2)], p_sem.at[lax.rem(t, 2)])
    fetch(0).start()
    tot_a[...] = jnp.zeros_like(tot_a)
    tot_b[...] = jnp.zeros_like(tot_b)
    for k, r in ((FC2B, 0), (GAM2, 1), (LN2G, 2), (LN2B, 3), (GAM1, 4), (OUTB, 5)):
        tot_a[k:k + 1, :] = dvec_a[r:r + 1, :]
    nb = NA + 1
    for j in range(nb):
        for i in range(D // FC):
            tot_a[NVEC + j:NVEC + j + 1, i * FC:(i + 1) * FC] = db1[j * (D // FC) + i, 0:1, :]
    dimg[...] = jnp.zeros_like(dimg)

    def half(t, carry):
        p, sq = t // ns, lax.rem(t, ns)
        fetch(t).wait()

        @pl.when(t + 1 < HEADS // 2 * ns)
        def _():
            fetch(t + 1).start()
        st = p_st.at[lax.rem(t, 2)]
        at_step(t, sc.run, B_HALF)
        backward_half(p, sq, q_ref, k_ref, v_ref, da_ref, lambda a, h, b: st[a, h, b, :, 0:IP], (dq, dk, dv), dimg, tot_a)

        @pl.when(lax.rem(t, 2 * ns) == 2 * ns - 1)
        def _():
            j = p // 2
            for n, d in enumerate((dq, dk, dv)):
                part = mm(actT[...], d[:, pl.ds(pl.multiple_of(j * HG, HG), HG)]).astype(bf16)
                dwq[:, :, :, :, :, pl.ds(pl.multiple_of(j * UW + n * HG, HG), HG)] = part.reshape(NZ, NY, NX, NC, PR, HG)
        at_step(t, sc.run, {(j + 1) * 2 * ns - 1: "B%d" % a for j, a in enumerate(HEAD_UNITS)})
        return carry
    V = lambda k: vec[k:k + 1, :]
    for i in range(ni):
        rows = pl.ds(i * IP, IP)
        n, _ = ln_parts(x_ref[rows, :].astype(f32))
        act[rows, :] = (n * V(LN1G) + V(LN1B)).astype(bf16)
    actT[...] = act[...].T
    lax.fori_loop(0, HEADS // 2 * ns, half, 0)
    t_a = Total(tot_a, Total.pairs(), *ta)
    t_a.start()
    acc[...] = jnp.zeros_like(acc)

    def table(t, carry):
        table_step(t, dimg, idx_ref, acc)
        at_step(t, sc.run, B_TABLE)
        at_step(t, t_a.step, V_TABLE)
        return carry
    lax.fori_loop(0, -(-PATCH // 8), table, 0)
    tot_t[...] = acc[0:96, :] + acc[96:192, :]
    t_t = Total(tot_t, Total.pairs(), *tt)
    t_t.start()
    load.wait()
    w = wq
    sg, sb = jnp.zeros((1, D), f32), jnp.zeros((1, D), f32)
    for i in range(ni):
        rows = pl.ds(i * IP, IP)
        e = jnp.zeros((IP, D), f32)
        for j in range(3):
            left = jnp.concatenate([d[rows, j * HG:(j + 1) * HG] for d in (dq, dk, dv)], axis=1)
            e = e + mmt(left, w[:, j * UW:(j + 1) * UW])
        n, r = ln_parts(x_ref[rows, :].astype(f32))
        dn = e * V(LN1G)
        dx = dres[rows, :] + r * (dn - jnp.mean(dn, axis=-1, keepdims=True) - n * jnp.mean(dn * n, axis=-1, keepdims=True))
        dres[pl.ds(i * PATCH, PATCH), :] = dx[:PATCH]
        sg = sg + jnp.sum(e * n, axis=0, keepdims=True)
        sb = sb + jnp.sum(e, axis=0, keepdims=True)
        sc.run(B_NORM[i % 4])
        for k in T_NORM[i % 4]:
            t_t.step(k)
        for k in V_NORM[i % 4]:
            t_a.step(k)
    tot_b[LN1G:LN1G + 1, :] = sg
    tot_b[LN1B:LN1B + 1, :] = sb
    t_b = Total(tot_b, Total.groups(), *tb)
    t_b.start()
    dtok_ref[...] = dres[pl.ds(0, ni * PATCH), :].astype(bf16)
    t_a.step(4)
    t_b.step(0)
    t_t.step(3)
    t_b.step(1)
    sc.run(B_TAIL)
    t_b.step(2)
    t_t.step(4)
    tot_a[LN1G:LN1B + 1, :] = tot_b[LN1G:LN1B + 1, :]

    z, y, x, c = place()
    me = ((z * NY + y) * NX + x) * NC + c
    per = D // (NZ * NY * NX * NC)
    def pick(rows, first, width):
        one = jnp.where(lax.broadcasted_iota(jnp.int32, (D, 128), 0) == first + lax.broadcasted_iota(jnp.int32, (D, 128), 1), 1.0, 0.0).astype(bf16)
        h = rows.astype(bf16)
        m = (rows - h.astype(f32)).astype(bf16)
        l = (rows - h.astype(f32) - m.astype(f32)).astype(bf16)
        return mm(h, one) + mm(m, one) + mm(l, one)
    own_vec[...] = pick(tot_a[0:16, :], me * per, per)
    wide = nb * per
    slab = me // (D // wide)
    part = pick(tot_a[8:16, :], lax.rem(me, D // wide) * wide, wide)
    rowi = lax.broadcasted_iota(jnp.int32, (8, 128), 0)
    own_b1[...] = jnp.broadcast_to(jnp.sum(jnp.where(rowi == slab + NVEC - 8, part, 0.0), axis=0, keepdims=True), (8, 128))
    for r in range(96):
        if r % 8 < 6:
            n = min(128, table_rows - r % 8 * 128)
            table_ref[r // 8:r // 8 + 1, (r % 8) * 128:(r % 8) * 128 + n] = tot_t[r:r + 1, 0:n]


def fused_b(dvec_a, db1, x, dres, q, k, v, da, vec, idx, wq6, p, d1, d2, do, table_rows, ni):
    R, S = ni * IP, jax.ShapeDtypeStruct
    vmem, hbm = vm(), pl.BlockSpec(memory_space=pl.ANY)
    split = lambda a: a.reshape((NZ, NY, NX, NC, -1, a.shape[-1]))
    d2, do = split(d2), split(do)
    own = lambda a: S(a.shape[-2:], f32)
    bufs, sems = Scatter.scratch(NB)
    row = lambda t: pltpu.VMEM((R, D), t)
    return pl.pallas_call(
        functools.partial(fused_b_kernel, ni, table_rows),
        in_specs=[vmem] * 10 + [hbm] * 5,
        out_shape=[S((ni * PATCH, D), bf16), S((HEADS, table_rows), f32), S((16, 128), f32), S((8, 128), f32), own(wq6), own(do), own(d1), own(d2)],
        out_specs=[vmem] * 8,
        scratch_shapes=[pltpu.VMEM((D, 3 * D), bf16)] + [row(bf16)] * 3 + [pltpu.VMEM((HEADS, IP, IL), f32), row(bf16), pltpu.VMEM((D, R), bf16), pltpu.VMEM(wq6.shape, bf16),
                        pltpu.VMEM((192, 128), f32), pltpu.VMEM((96, 128), f32), pltpu.VMEM((16, D), f32), pltpu.VMEM((2, D), f32),
                        pltpu.VMEM((2, 2, 2, 2, IP, IL), bf16), DMA((2,)), DMA] + bufs + sems + Total.scratch(5, 16, D) + Total.scratch(7, 2, D) + Total.scratch(5, 96, 128),
        compiler_params=pltpu.CompilerParams(collective_id=3, has_side_effects=True, vmem_limit_bytes=62 << 20), name="attention_backward",
    )(dvec_a, db1, x, dres, q, k, v, da, vec, idx, wq6.reshape(D, 3 * D), p, d1, d2, do)


def place_kernel(per, wide, out, dtok, table, vecs, b1, oq, oo, o1a, o1b, o2, *outs):
    for a, b in ((out, outs[0]), (dtok, outs[1]), (table, outs[2]), (oq, outs[3]), (oo, outs[4]), (o2, outs[6])):
        b[...] = a[...]
    outs[5][:, 0:o1a.shape[1]] = o1a[...]
    outs[5][:, o1a.shape[1]:] = o1b[...]
    outs[7][...] = b1[0:1, 0:wide]
    for k in range(NVEC):
        outs[8 + k][...] = vecs[k:k + 1, 0:per]


def place_outputs(out, dtok, table, vecs, b1, oq, oo, o1a, o1b, o2, per, wide):
    S = jax.ShapeDtypeStruct
    like = lambda a: S(a.shape, a.dtype)
    return pl.pallas_call(
        functools.partial(place_kernel, per, wide),
        in_specs=[vm()] * 10,
        out_shape=[like(out), like(dtok), like(table), like(oq), like(oo), S((PR, o1a.shape[1] + o1b.shape[1]), f32), like(o2), S((1, wide), f32)] + [S((1, per), f32)] * NVEC,
        out_specs=[vm()] * (8 + NVEC),
        compiler_params=pltpu.CompilerParams(vmem_limit_bytes=60 << 20), name="place_outputs",
    )(out, dtok, table, vecs, b1, oq, oo, o1a, o1b, o2)


def pad_rows(a, ni):
    return jnp.pad(a.reshape(ni, PATCH, D), ((0, 0), (0, IP - PATCH), (0, 0))).reshape(ni * IP, D)


def unpad_rows(a, ni):
    return a.reshape(ni, IP, D)[:, :PATCH].reshape(ni * PATCH, D)


def local(tokens, image_ids, rel_index, rel_table, ln1_gain, ln1_bias, w_qkv, q_bias, v_bias, w_out, out_bias, gamma1,
          ln2_gain, ln2_bias, w_fc1, fc1_bias, w_fc2, fc2_bias, gamma2, out_grad):
    ni = tokens.shape[0] // PATCH
    per = ln1_gain.shape[0]
    n_dev = D // per
    small = jnp.concatenate([ln1_gain, ln1_bias, q_bias, v_bias, out_bias, gamma1, ln2_gain, ln2_bias, fc2_bias, gamma2, fc1_bias])
    me = lax.axis_index("gx") * lax.axis_size("gy") + lax.axis_index("gy")
    if (lax.axis_size("gx"), lax.axis_size("gy"), per) == (NZ * NY, NX * NC, PR):
        smalls = [a.reshape(1, -1) for a in (ln1_gain, ln1_bias, q_bias, v_bias, out_bias, gamma1, ln2_gain, ln2_bias, fc2_bias, gamma2, fc1_bias)]
        res = fused_a(image_ids, tokens, out_grad, rel_table.T, rel_index, smalls, w_qkv, w_out, w_fc1, w_fc2, ni)
        out, x, q, k, v, dres, datt, idx, dvec, db1, dwo, vec, g1, wq6, p, dw1, dw2 = res
        dtok, table_grad, own_vec, own_b1, gq, go, g1b, g2 = fused_b(dvec, db1, x, dres, q, k, v, datt, vec, idx, wq6, p, dw1, dw2, dwo, rel_table.shape[0], ni)
        res = place_outputs(out, dtok, table_grad, own_vec, own_b1, gq, go, g1, g1b, g2, per, fc1_bias.shape[0])
        out, dtok, table_grad, gq, go, g1, g2, b1 = res[:8]
        sl = [a.reshape(-1) for a in res[8:]]
        return (out, dtok, table_grad.T, sl[LN1G], sl[LN1B], gq, sl[QB], sl[VB], go, sl[OUTB], sl[GAM1], sl[LN2G], sl[LN2B], g1,
                b1.reshape(-1), g2, sl[FC2B], sl[GAM2])
    gather = lambda a: lax.all_gather(a, AXES, axis=0, tiled=True)
    wq, wo, w1, w2 = gather(w_qkv), gather(w_out), gather(w_fc1), gather(w_fc2)
    small = lax.all_gather(small, AXES, axis=0, tiled=False).reshape(n_dev, -1).astype(f32)
    vec = jnp.pad(jnp.transpose(small[:, : NVEC * per].reshape(n_dev, NVEC, per), (1, 0, 2)).reshape(NVEC, D), ((0, 16 - NVEC), (0, 0)))
    b1 = small[:, NVEC * per :].reshape(1, -1)

    x = pad_rows(tokens, ni)
    g = pad_rows(out_grad, ni)
    ids = image_ids.reshape(ni, PATCH)[:, 0]
    table_rows = rel_table.shape[0]
    tab = jnp.pad(rel_table.astype(f32).T, ((0, 0), (0, 768 - table_rows))).reshape(6, 2, 6, 128)
    idx = jnp.pad(rel_index.T, ((0, IP - PATCH), (0, IL - PATCH)))

    att, q, k, v, p = front(ids, x, wq, tab, idx, vec, ni)
    out, dres, datt, dw1, dw2, dwo, db1, dvec = mlp(x, att, g, wo, vec, w1, w2, b1, ni)
    dq, dk, dv, dimg, dvec2 = attb(q, k, v, datt, p, ni)
    dtok, dwq, dvec3, dtab = qkvb(x, dres, dq, dk, dv, wq, vec, dimg, idx, ni)

    scatter = lambda a: lax.psum_scatter(a.astype(f32), AXES, scatter_dimension=0, tiled=True)
    rows = jnp.concatenate([dvec3[0:2], dvec2[0:2], dvec[5:6], dvec[4:5], dvec[2:4], dvec[0:1], dvec[1:2], db1.reshape(-1, D), dtab.reshape(-1, D)])
    total = lax.psum(rows, AXES)
    sl = [lax.dynamic_slice(total[i], (me * per,), (per,)) for i in range(NVEC)]
    nb = db1.shape[1] // D
    db1_own = lax.dynamic_slice(total[NVEC : NVEC + nb].reshape(-1), (me * per * nb,), (per * nb,))
    table_grad = total[NVEC + nb :].reshape(HEADS, 1024)[:, :table_rows].T
    return (unpad_rows(out, ni), unpad_rows(dtok, ni), table_grad, sl[LN1G], sl[LN1B], scatter(dwq), sl[QB], sl[VB], scatter(dwo),
            sl[OUTB], sl[GAM1], sl[LN2G], sl[LN2B], scatter(dw1), db1_own, scatter(dw2), sl[FC2B], sl[GAM2])


def solution(mesh):
    rows, vecs, none = P(AXES, None), P(AXES), P()
    return jax.shard_map(
        local,
        mesh=mesh,
        in_specs=(rows, vecs, none, none, vecs, vecs, rows, vecs, vecs, rows, vecs, vecs, vecs, vecs, rows, vecs, rows, vecs, vecs, rows),
        out_specs=(rows, rows, none, vecs, vecs, rows, vecs, vecs, rows, vecs, vecs, vecs, vecs, rows, vecs, rows, vecs, vecs),
        check_vma=False,
    )
```

```python
import functools

import jax
import jax.numpy as jnp
from jax import lax
from jax.experimental import pallas as pl
from jax.experimental.pallas import tpu as pltpu
from jax.sharding import PartitionSpec as P

D=768; HEADS=12; HEAD=64; PATCH=197; IP=208; IL=256
f32=jnp.float32; bf16=jnp.bfloat16
NEG=-1e30
def mm(a,b): return jnp.dot(a,b,preferred_element_type=f32)
def mmt(a,b): return lax.dot_general(a,b,(((1,),(1,)),((),())),preferred_element_type=f32)
def vm(): return pl.BlockSpec(memory_space=pltpu.VMEM)

def ln_parts(x):
    c=x-jnp.mean(x,axis=-1,keepdims=True)
    r=lax.rsqrt(jnp.mean(c*c,axis=-1,keepdims=True)+1e-6)
    return c*r,r

def front_kernel(ni, ids_ref, x_ref, wq_ref, tab_ref, idx_ref, vec_ref, att_ref, q_out, k_out, v_out, p_ref, bias_ref):
    pid=pl.program_id(0)
    R=ni*IP
    @pl.when(pid==0)
    def _():
        for i in range(ni):
            rows=pl.ds(i*IP,IP)
            n,_=ln_parts(x_ref[rows,:].astype(f32))
            a=(n*vec_ref[0:1,:]+vec_ref[1:2,:]).astype(bf16)
            for j in range(3):
                sl=pl.ds(j*D,D)
                o=mm(a,wq_ref[:,sl])
                if j==0: q_out[rows,:]=((o+vec_ref[2:3,:])*0.125).astype(bf16)
                if j==1: k_out[rows,:]=o.astype(bf16)
                if j==2: v_out[rows,:]=(o+vec_ref[3:4,:]).astype(bf16)
    rowi=lax.broadcasted_iota(jnp.int32,(IP,128),0)
    for h in range(2):
        for l in range(2):
            idx=idx_ref[:,pl.ds(l*128,128)]
            lo=jnp.bitwise_and(idx,127); hi=jnp.right_shift(idx,7)
            acc=jnp.zeros((IP,128),f32)
            for k in range(6):
                t=jnp.broadcast_to(tab_ref[0,h,k:k+1,:],(IP,128))
                gth=jnp.take_along_axis(t,lo,axis=1,mode="promise_in_bounds")
                acc=jnp.where(hi==k,gth,acc)
            bias_ref[h,:,pl.ds(l*128,128)]=jnp.where(rowi<PATCH,acc,NEG)
    cols=pl.ds(pl.multiple_of(pid*128,128),128)
    lane=lax.broadcasted_iota(jnp.int32,(1,128),1)
    for s in range(ni//2):
        linked=ids_ref[2*s]==ids_ref[2*s+1]
        mx=jnp.where(jnp.logical_and(lax.broadcasted_iota(jnp.int32,(IP,1),0)<PATCH,linked),0.0,NEG)
        kk=k_out[pl.ds(2*s*IP,2*IP),cols]
        vT=v_out[pl.ds(2*s*IP,2*IP),cols].T
        for a in range(2):
            rows=pl.ds((2*s+a)*IP,IP)
            q=q_out[rows,cols]
            ats=[]
            for h in range(2):
                qm=jnp.where((lane<64) if h==0 else (lane>=64),q,jnp.zeros_like(q))
                st=mmt(kk,qm)
                b=bias_ref[h,:,0:IP]
                if a==0: s0=st[:IP]+b; s1=st[IP:]+mx
                else: s0=st[:IP]+mx; s1=st[IP:]+b
                m=jnp.maximum(jnp.max(s0,axis=0,keepdims=True),jnp.max(s1,axis=0,keepdims=True))
                e0=jnp.exp(s0-m); e1=jnp.exp(s1-m)
                inv=1.0/(jnp.sum(e0,axis=0,keepdims=True)+jnp.sum(e1,axis=0,keepdims=True))
                p0=(e0*inv).astype(bf16); p1=(e1*inv).astype(bf16)
                p_ref[0,s,a,h,0,:,0:IP]=p0
                p_ref[0,s,a,h,1,:,0:IP]=p1
                v_h=vT[h*64:(h+1)*64]
                ats.append(mm(v_h[:,:IP],p0)+mm(v_h[:,IP:],p1))
            att_ref[rows,cols]=jnp.concatenate(ats,axis=0).T.astype(bf16)

def front(ids,x,wq,tab,idx,vec,ni):
    R=ni*IP
    full=lambda *s: pl.BlockSpec(s,lambda p:(0,)*len(s))
    return pl.pallas_call(functools.partial(front_kernel,ni),
        grid=(6,),
        out_shape=[jax.ShapeDtypeStruct((R,D),bf16)]*4+[jax.ShapeDtypeStruct((6,ni//2,2,2,2,IP,IL),bf16)],
        in_specs=[pl.BlockSpec(memory_space=pltpu.SMEM),full(R,D),full(D,3*D),pl.BlockSpec((1,2,6,128),lambda p:(p,0,0,0)),full(IP,IL),full(16,D)],
        out_specs=[full(R,D)]*4+[pl.BlockSpec((1,ni//2,2,2,2,IP,IL),lambda p:(p,0,0,0,0,0,0))],
        scratch_shapes=[pltpu.VMEM((2,IP,IL),f32)],
        compiler_params=pltpu.CompilerParams(vmem_limit_bytes=56<<20),name="front",
    )(ids,x,wq,tab,idx,vec)

def gelu_parts(x):
    z=x*0.7071067811865476
    e=lax.erf(z)
    cdf=0.5+0.5*e
    pdf=jnp.exp(-z*z)*0.3989422804014327
    return cdf, x*pdf

FC=256
def mlp_kernel(ni, nf, x_ref, att_ref, g_ref, wo_ref, vec_ref, w1_ref, w2_ref, b1_ref,
               out_ref, dres_ref, datt_ref, dw1_ref, dw2_ref, dwo_ref, db1_ref, dvec_ref,
               res, n2, r2, branch, act2, act2T, dmlp, mlp, dact):
    pid=pl.program_id(0)
    V=lambda k: vec_ref[k:k+1,:]
    @pl.when(pid==0)
    def _():
        sb=jnp.zeros((1,D),f32)
        for i in range(ni):
            rows=pl.ds(i*IP,IP)
            br=mm(att_ref[rows,:],wo_ref[...])+V(OUTB)
            branch[rows,:]=br
            rs=x_ref[rows,:].astype(f32)+V(GAM1)*br
            res[rows,:]=rs
            n,r=ln_parts(rs)
            n2[rows,:]=n
            r2[rows,:]=jnp.broadcast_to(r,(IP,128))
            act2[rows,:]=(n*V(LN2G)+V(LN2B)).astype(bf16)
            dm=V(GAM2)*g_ref[rows,:].astype(f32)
            sb=sb+jnp.sum(dm,axis=0,keepdims=True)
            dmlp[rows,:]=dm.astype(bf16)
        act2T[...]=act2[...].T
        dvec_ref[0:1,:]=sb
        mlp[...]=jnp.zeros_like(mlp)
        dact[...]=jnp.zeros_like(dact)
    w1=w1_ref[...]; w2=w2_ref[...]
    pre=mm(act2[...],w1)+b1_ref[...]
    cdf,xpdf=gelu_parts(pre)
    hid=(pre*cdf).astype(bf16)
    dh=mmt(dmlp[...],w2)
    dp=dh*(cdf+xpdf)
    db1_ref[...]=jnp.sum(dp,axis=0,keepdims=True)
    dpb=dp.astype(bf16)
    mlp[...]+=mm(hid,w2)
    dact[...]+=mmt(dpb,w1)
    dw1_ref[...]=mm(act2T[...],dpb).astype(bf16)
    dw2_ref[...]=mm(hid.T,dmlp[...]).astype(bf16)
    @pl.when(pid==nf-1)
    def _():
        sums=[jnp.zeros((1,D),f32) for _ in range(5)]
        for i in range(ni):
            rows=pl.ds(i*IP,IP)
            g=g_ref[rows,:].astype(f32)
            ml=mlp[rows,:]+V(FC2B)
            out_ref[rows,:]=(res[rows,:]+V(GAM2)*ml).astype(bf16)
            e=dact[rows,:]; n=n2[rows,:]
            dn=e*V(LN2G)
            dr=g+r2[rows,0:1]*(dn-jnp.mean(dn,axis=-1,keepdims=True)-n*jnp.mean(dn*n,axis=-1,keepdims=True))
            dres_ref[rows,:]=dr
            db=V(GAM1)*dr
            for k,t in enumerate((g*ml,e*n,e,dr*branch[rows,:],db)):
                sums[k]=sums[k]+jnp.sum(t,axis=0,keepdims=True)
            dbb=db.astype(bf16)
            dmlp[rows,:]=dbb
            datt_ref[rows,:]=mmt(dbb,wo_ref[...]).astype(bf16)
        for k in range(5): dvec_ref[k+1:k+2,:]=sums[k]
        dwo_ref[...]=mm(att_ref[...].T,dmlp[...]).astype(bf16)

def mlp(x,att,g,wo,vec,w1,w2,b1,ni):
    R=ni*IP; F=w1.shape[1]; nf=F//FC
    full=lambda *s: pl.BlockSpec(s,lambda p:(0,)*len(s),pipeline_mode=pl.Buffered(1))
    S=jax.ShapeDtypeStruct
    return pl.pallas_call(functools.partial(mlp_kernel,ni,nf),grid=(nf,),
        in_specs=[full(R,D)]*3+[full(D,D),full(16,D),pl.BlockSpec((D,FC),lambda p:(0,p)),pl.BlockSpec((FC,D),lambda p:(p,0)),pl.BlockSpec((1,FC),lambda p:(0,p))],
        out_shape=[S((R,D),bf16),S((R,D),f32),S((R,D),bf16),S((D,F),bf16),S((F,D),bf16),S((D,D),bf16),S((1,F),f32),S((8,D),f32)],
        out_specs=[full(R,D)]*3+[pl.BlockSpec((D,FC),lambda p:(0,p)),pl.BlockSpec((FC,D),lambda p:(p,0)),full(D,D),pl.BlockSpec((1,FC),lambda p:(0,p)),full(8,D)],
        scratch_shapes=[pltpu.VMEM((R,D),f32)]*2+[pltpu.VMEM((R,128),f32),pltpu.VMEM((R,D),f32),pltpu.VMEM((R,D),bf16),pltpu.VMEM((D,R),bf16),pltpu.VMEM((R,D),bf16)]+[pltpu.VMEM((R,D),f32)]*2,
        compiler_params=pltpu.CompilerParams(vmem_limit_bytes=60<<20),name="mlp",
    )(x,att,g,wo,vec,w1,w2,b1)

def attb_kernel(ni, q_ref,k_ref,v_ref,da_ref,p_ref, dq_ref,dk_ref,dv_ref,dimg_ref,dvec_ref):
    lane=lax.broadcasted_iota(jnp.int32,(1,128),1)
    sq=jnp.zeros((1,128),f32); sv=jnp.zeros((1,128),f32)
    for s in range(ni//2):
        srow=pl.ds(2*s*IP,2*IP)
        kk=k_ref[srow,:]; vv=v_ref[srow,:]
        kT=kk.T
        dv=jnp.zeros((2*IP,128),f32); dk=jnp.zeros((2*IP,128),f32)
        for a in range(2):
            rows=pl.ds((2*s+a)*IP,IP)
            q=q_ref[rows,:]; da=da_ref[rows,:]
            dqs=[]
            for h in range(2):
                msk=(lane<64) if h==0 else (lane>=64)
                qm=jnp.where(msk,q,jnp.zeros_like(q)); dam=jnp.where(msk,da,jnp.zeros_like(da))
                pb0=p_ref[0,s,a,h,0,:,0:IP]; pb1=p_ref[0,s,a,h,1,:,0:IP]
                dp=mmt(vv,dam)
                t0=pb0.astype(f32)*dp[:IP]; t1=pb1.astype(f32)*dp[IP:]
                dl=jnp.sum(t0,axis=0,keepdims=True)+jnp.sum(t1,axis=0,keepdims=True)
                d0=t0-pb0.astype(f32)*dl; d1=t1-pb1.astype(f32)*dl
                same=d0 if a==0 else d1
                if s==0 and a==0: dimg_ref[0,h,:,0:IP]=same
                else: dimg_ref[0,h,:,0:IP]+=same
                ds=jnp.concatenate([d0.astype(bf16),d1.astype(bf16)],axis=0)
                pb=jnp.concatenate([pb0,pb1],axis=0)
                dv=dv+mm(pb,dam)
                dk=dk+mm(ds,qm)
                dqs.append(mm(kT[h*64:(h+1)*64],ds))
            dq=jnp.concatenate(dqs,axis=0).T*0.125
            sq=sq+jnp.sum(dq,axis=0,keepdims=True)
            dq_ref[rows,:]=dq.astype(bf16)
        sv=sv+jnp.sum(dv,axis=0,keepdims=True)
        dk_ref[srow,:]=dk.astype(bf16); dv_ref[srow,:]=dv.astype(bf16)
    dimg_ref[0,:,:,IP:]=jnp.zeros((2,IP,IL-IP),f32)
    dvec_ref[0:1,:]=sq; dvec_ref[1:2,:]=sv

def attb(q,k,v,da,p,ni):
    R=ni*IP; S=jax.ShapeDtypeStruct
    col=pl.BlockSpec((R,128),lambda i:(0,i))
    return pl.pallas_call(functools.partial(attb_kernel,ni),grid=(6,),
        in_specs=[col]*4+[pl.BlockSpec((1,ni//2,2,2,2,IP,IL),lambda p:(p,0,0,0,0,0,0))],
        out_shape=[S((R,D),bf16)]*3+[S((6,2,IP,IL),f32),S((8,D),f32)],
        out_specs=[col]*3+[pl.BlockSpec((1,2,IP,IL),lambda i:(i,0,0,0)),pl.BlockSpec((8,128),lambda i:(0,i))],
        compiler_params=pltpu.CompilerParams(vmem_limit_bytes=56<<20),name="attb",
    )(q,k,v,da,p)

def qkvb_kernel(ni,x_ref,dres_ref,dq_ref,dk_ref,dv_ref,wq_ref,vec_ref,dimg_ref,idx_ref,
                dtok_ref,dw_ref,dvec_ref,dtab_ref,a1T,act1,acc):
    for i in range(ni):
        rows=pl.ds(i*IP,IP)
        n,r=ln_parts(x_ref[rows,:].astype(f32))
        act1[rows,:]=(n*vec_ref[0:1,:]+vec_ref[1:2,:]).astype(bf16)
    a1T[...]=act1[...].T
    for j,r_ in enumerate((dq_ref,dk_ref,dv_ref)):
        dw_ref[:,pl.ds(j*D,D)]=mm(a1T[...],r_[...]).astype(bf16)
    sg=jnp.zeros((1,D),f32); sb=jnp.zeros((1,D),f32)
    for i in range(ni):
        rows=pl.ds(i*IP,IP)
        e=mmt(dq_ref[rows,:],wq_ref[:,0:D])+mmt(dk_ref[rows,:],wq_ref[:,D:2*D])+mmt(dv_ref[rows,:],wq_ref[:,2*D:])
        n,r=ln_parts(x_ref[rows,:].astype(f32))
        dn=e*vec_ref[0:1,:]
        dx=dres_ref[rows,:]+r*(dn-jnp.mean(dn,axis=-1,keepdims=True)-n*jnp.mean(dn*n,axis=-1,keepdims=True))
        dtok_ref[rows,:]=dx.astype(bf16)
        sg=sg+jnp.sum(e*n,axis=0,keepdims=True); sb=sb+jnp.sum(e,axis=0,keepdims=True)
    dvec_ref[0:1,:]=sg; dvec_ref[1:2,:]=sb
    acc[...]=jnp.zeros_like(acc)
    sub8=lax.broadcasted_iota(jnp.int32,(8,IL),0)
    sub128=lax.broadcasted_iota(jnp.int32,(128,IL),0)
    def body(j,_):
        ix=idx_ref[pl.ds(j,1),:]
        lo=jnp.bitwise_and(ix,127); hi=jnp.right_shift(ix,7)
        oh=jnp.where(sub128==lo,1.0,0.0).astype(bf16)
        hm=sub8==hi
        As=[]
        for h in range(HEADS):
            d=dimg_ref[h//2,h%2,pl.ds(j,1),:]
            As.append(jnp.where(hm,jnp.broadcast_to(d,(8,IL)),0.0))
        A=jnp.concatenate(As,axis=0)
        Ah=A.astype(bf16); Al=(A-Ah.astype(f32)).astype(bf16)
        acc[...]+=mmt(Ah,oh)+mmt(Al,oh)
        return 0
    lax.fori_loop(0,PATCH,body,0)
    dtab_ref[...]=acc[...]

def qkvb(x,dres,dq,dk,dv,wq,vec,dimg,idx,ni):
    R=ni*IP; S=jax.ShapeDtypeStruct
    return pl.pallas_call(functools.partial(qkvb_kernel,ni),
        in_specs=[vm()]*9,
        out_shape=[S((R,D),bf16),S((D,3*D),bf16),S((8,D),f32),S((96,128),f32)],
        out_specs=[vm()]*4,
        scratch_shapes=[pltpu.VMEM((D,R),bf16),pltpu.VMEM((R,D),bf16),pltpu.VMEM((96,128),f32)],
        compiler_params=pltpu.CompilerParams(vmem_limit_bytes=56<<20),name="qkvb",
    )(x,dres,dq,dk,dv,wq,vec,dimg,idx)


AXES = ("gx", "gy")
NVEC = 10
(LN1G, LN1B, QB, VB, OUTB, GAM1, LN2G, LN2B, FC2B, GAM2) = range(NVEC)

MESH = pl.DeviceIdType.MESH
NZ, NY, NX, NC = 4, 2, 2, 2
PR, UW = 24, 768
DMA = pltpu.SemaphoreType.DMA
ALL = slice(None)


def place():
    gx, gy = lax.axis_index("gx"), lax.axis_index("gy")
    return gx // NY, lax.rem(gx, NY), gy // NC, lax.rem(gy, NC)


def at_place(z, y, x, c):
    return (z * NY + y, x * NC + c)


def neighbours():
    z, y, x, c = place()
    line = [at_place(lax.rem(z + k, NZ), y, x, c) for k in (1, 2, 3)]
    return line, at_place(z, y, 1 - x, c), at_place(z, 1 - y, x, c), at_place(z, y, x, 1 - c)


def across():
    z, y, x, c = place()
    return at_place(z, y, 1 - x, 1 - c)


def greet(also=()):
    line, nx, ny, nc = neighbours()
    peers = line + [nx, ny, nc] + list(also)
    barrier = pltpu.get_barrier_semaphore()
    for t in peers:
        pl.semaphore_signal(barrier, inc=1, device_id=t, device_id_type=MESH)
    return lambda: pl.semaphore_wait(barrier, len(peers))


def remote(src, dst, send, recv, to):
    return pltpu.make_async_remote_copy(src_ref=src, dst_ref=dst, send_sem=send, recv_sem=recv, device_id=to, device_id_type=MESH)


class Gather:
    def __init__(self, units, local, z_s, z_r, p_s, p_r, d_s, d_r, c_s, c_r):
        self.u = units
        self.local, self.z_s, self.z_r, self.p_s, self.p_r, self.d_s, self.d_r, self.c_s, self.c_r = local, z_s, z_r, p_s, p_r, d_s, d_r, c_s, c_r
        self.pos = place()
        self.line, self.nx, self.ny, self.nc = neighbours()

    @staticmethod
    def scratch(n):
        return [DMA((n,)), DMA((n, 3)), DMA((n, 3)), DMA((n, 2)), DMA((n, 2)), DMA((n, 2)), DMA((n, 2)), DMA((n, 4)), DMA((n, 4))]

    def first(self, a):
        z, y, x, c = self.pos
        src, view, plane = self.u[a]
        to = view(z if plane is None else plane, y, x, c)
        mine = [] if src is None else [pltpu.make_async_copy(src, to, self.local.at[a])]
        src = to if src is None else src
        return mine + [remote(src, to, self.z_s.at[a, k], self.z_r.at[a, k if plane is None else 0], self.line[k]) for k in range(3)]

    def start(self, a):
        plane = self.u[a][2]
        if plane is None:
            for d in self.first(a):
                d.start()
        else:
            @pl.when(self.pos[0] == plane)
            def _():
                for d in self.first(a):
                    d.start()

    def arrive(self, a):
        plane = self.u[a][2]
        if plane is None:
            for d in self.first(a):
                d.wait()
        else:
            @pl.when(self.pos[0] == plane)
            def _():
                mine, *sent = self.first(a)
                mine.wait()
                for d in sent:
                    d.wait_send()

            @pl.when(self.pos[0] != plane)
            def _():
                z, y, x, c = self.pos
                src, view, plane = self.u[a]
                remote(src, view(plane, y, x, c), self.z_s.at[a, 0], self.z_r.at[a, 0], self.line[0]).wait_recv()

    def to_plane(self, a):
        z, y, x, c = self.pos
        _, view, plane = self.u[a]
        v = view(ALL if plane is None else plane, y, x, c)
        return (remote(v, v, self.p_s.at[a, 0], self.p_r.at[a, 0], self.nx), remote(v, v, self.p_s.at[a, 1], self.p_r.at[a, 1], self.ny))

    def to_diagonal(self, a):
        z, y, x, c = self.pos
        _, view, plane = self.u[a]
        if plane is None:
            vx, vy = view(slice(0, 2), y, 1 - x, c), view(slice(2, 4), 1 - y, x, c)
        else:
            vx, vy = view(plane, y, 1 - x, c), view(plane, 1 - y, x, c)
            half = vx.shape[0] // 2
            vx, vy = vx.at[pl.ds(0, half)], vy.at[pl.ds(half, half)]
        return (remote(vx, vx, self.d_s.at[a, 0], self.d_r.at[a, 0], self.ny), remote(vy, vy, self.d_s.at[a, 1], self.d_r.at[a, 1], self.nx))

    def to_sibling(self, a, k):
        z, y, x, c = self.pos
        _, view, plane = self.u[a]
        v = view(ALL if plane is None else plane, (y, y, 1 - y, 1 - y)[k], (x, 1 - x, x, 1 - x)[k], c)
        return remote(v, v, self.c_s.at[a, k], self.c_r.at[a, k], self.nc)

    def plane(self, a):
        self.arrive(a)
        for d in self.to_plane(a):
            d.start()
        self.to_sibling(a, 0).start()

    def diagonal(self, a):
        for d in self.to_plane(a):
            d.wait()
        for d in self.to_diagonal(a):
            d.start()
        self.to_sibling(a, 1).start()
        self.to_sibling(a, 2).start()

    def sibling(self, a):
        for d in self.to_diagonal(a):
            d.wait()
        self.to_sibling(a, 3).start()

    def finish(self, a):
        for k in range(4):
            self.to_sibling(a, k).wait()

    def run(self, text):
        for word in text.split():
            {"P": self.plane, "D": self.diagonal, "S": self.sibling, "F": self.finish}[word[0]](int(word[1:]))


class Scatter:
    def __init__(self, units, bufs, sems):
        self.u = units
        self.own, self.rc, self.rx, self.ry, self.r3, self.rz = bufs
        self.sems = sems
        self.pos = place()
        self.line, self.nx, self.ny, self.nc = neighbours()
        self.line_z = [lax.rem(self.pos[0] + k, NZ) for k in (1, 2, 3)]

    @staticmethod
    def scratch(n):
        v = lambda *s: pltpu.VMEM((n,) + s + (PR, UW), bf16)
        return [v(NZ, NY, NX), v(NZ, NY, NX), v(2, NY), v(2, NX), v(NZ), v(3)], [DMA((n,)), DMA((n, 8)), DMA((n, 8))]

    def copy(self, a, k, src, dst, to):
        return remote(src, dst, self.sems[1].at[a, k], self.sems[2].at[a, k], to)

    def one(self, a):
        c = self.pos[3]
        view = self.u[a][0]
        mine = pltpu.make_async_copy(view(ALL, ALL, ALL, c), self.own.at[a], self.sems[0].at[a])
        return mine, self.copy(a, 0, view(ALL, ALL, ALL, 1 - c), self.rc.at[a], self.nc)

    def two(self, a):
        z, y, x, c = self.pos
        own = self.own.at[a]
        return (self.copy(a, 1, own.at[0:2, :, 1 - x], self.rx.at[a], self.nx), self.copy(a, 2, own.at[2:4, 1 - y, :], self.ry.at[a], self.ny))

    def three(self, a):
        z, y, x, c = self.pos
        own, r3 = self.own.at[a], self.r3.at[a]
        return (self.copy(a, 3, own.at[0:2, 1 - y, x], r3.at[0:2], self.ny), self.copy(a, 4, own.at[2:4, y, 1 - x], r3.at[2:4], self.nx))

    def four(self, a):
        z, y, x, c = self.pos
        own = self.own.at[a]
        return [self.copy(a, 5 + k, own.at[self.line_z[k], y, x], self.rz.at[a, k], self.line[k]) for k in range(3)]

    def start(self, a):
        for d in self.one(a):
            d.start()

    def plane(self, a):
        for d in self.one(a):
            d.wait()
        own, rc = self.own.at[a], self.rc.at[a]

        @pl.loop(0, NZ)
        def _(i):
            own[i] = own[i] + rc[i]
        for d in self.two(a):
            d.start()

    def diagonal(self, a):
        z, y, x, c = self.pos
        for d in self.two(a):
            d.wait()
        own, rx, ry = self.own.at[a], self.rx.at[a], self.ry.at[a]
        for i in range(2):
            for j in range(2):
                own[i, j, x] = own[i, j, x] + rx[i, j]
                own[2 + i, y, j] = own[2 + i, y, j] + ry[i, j]
        for d in self.three(a):
            d.start()

    def along(self, a):
        z, y, x, c = self.pos
        for d in self.three(a):
            d.wait()
        own, r3 = self.own.at[a], self.r3.at[a]
        for i in range(NZ):
            own[i, y, x] = own[i, y, x] + r3[i]
        for d in self.four(a):
            d.start()

    def finish(self, a):
        z, y, x, c = self.pos
        for d in self.four(a):
            d.wait()
        own, rz = self.own.at[a], self.rz.at[a]
        total = own[z, y, x].astype(f32)
        for k in range(3):
            total = total + rz[k].astype(f32)
        self.u[a][1](total)

    def run(self, text):
        for word in text.split():
            {"B": self.start, "P": self.plane, "D": self.diagonal, "L": self.along, "F": self.finish}[word[0]](int(word[1:]))


class Total:
    def __init__(self, ref, hops, bufs, s_s, s_r):
        self.ref, self.hops, self.bufs, self.s, self.r = ref, hops, bufs, s_s, s_r

    @staticmethod
    def pairs():
        z, y, x, c = place()
        near = z + 1 - 2 * lax.rem(z, 2)
        _, nx, ny, nc = neighbours()
        return [[nc], [nx], [ny], [at_place(near, y, x, c)], [at_place(lax.rem(z + 2, NZ), y, x, c)]]

    @staticmethod
    def groups():
        line, nx, ny, nc = neighbours()
        return [[nc, nx, across()], [ny], line]

    @staticmethod
    def scratch(n, *shape):
        return [pltpu.VMEM((n,) + shape, f32), DMA((n,)), DMA((n,))]

    def copies(self, k):
        first = sum(len(h) for h in self.hops[:k])
        return [remote(self.ref, self.bufs.at[first + i], self.s.at[first + i], self.r.at[first + i], to) for i, to in enumerate(self.hops[k])]

    def start(self):
        for d in self.copies(0):
            d.start()

    def step(self, k):
        for d in self.copies(k):
            d.wait()
        first = sum(len(h) for h in self.hops[:k])
        for i in range(len(self.hops[k])):
            self.ref[...] = self.ref[...] + self.bufs[first + i]
        if k + 1 < len(self.hops):
            for d in self.copies(k + 1):
                d.start()


def columns(src, j):
    return src.at[:, pl.ds(j * UW, UW)]


def gather_units(shards, gathered):
    (small, wq, wo, w1, w2), (gsmall, gq, go, g1, g2) = shards, gathered
    cols = lambda src, dst, j: (columns(src, j), lambda z, y, x, c: dst.at[z, y, x, c, :, pl.ds(j * UW, UW)], None)
    units = [(small, lambda z, y, x, c: gsmall.at[z, y, x, c], None)]
    units += [(None, lambda z, y, x, c, j=j: gq.at[z, y, x, c, :, pl.ds(j * UW, UW)], None) for j in range(3)] + [cols(wo, go, 0)]
    for j in range(NZ):
        units += [(w2, lambda z, y, x, c: g2.at[z, y, x, c], j), cols(w1, g1, j)]
    return units


def owned(out, rows, cols):
    def store(total):
        out[rows, cols] = total
    return store


def scatter_units(grads, outs):
    (dq, do, d1, d2), (oq, oo, o1, o2) = grads, outs

    def keep_heads(j):
        def store(total):
            for t in range(3):
                oq[:, t * D + j * HG:t * D + (j + 1) * HG] = total[:, t * HG:(t + 1) * HG]
        return store
    part = lambda src, j: lambda z, y, x, c: src.at[z, y, x, c, :, pl.ds(j * UW, UW)]
    two = [(lambda z, y, x, c, j=j: d2.at[z, y, x, c, pl.ds(j * PR, PR), :], owned(o2, slice(j * PR, (j + 1) * PR), ALL)) for j in range(4)]
    heads = [(part(dq, j), keep_heads(j)) for j in range(3)]
    return [(part(d1, 0), owned(o1, ALL, ALL)), two[0], two[1], heads[0], two[2], two[3], heads[1], (part(do, 0), owned(oo, ALL, ALL)), heads[2]]


HEAD_UNITS = (3, 6, 8)
HG = 256
NB = 9
NA = 3

A_HEAD = ('P0', 'P1 D0', 'S0 P2', 'D1 F0', 'S1 P3', 'F1 D2 P4')
A_HALF = {0: 'P5 S2', 1: 'D3', 2: 'P6 F2', 3: 'D4', 4: 'P7 S3', 5: 'D5', 6: 'P8 S4 F3', 7: 'D6', 8: 'P9 S5 F4', 9: 'D7', 10: 'P10 S6 F5', 11: 'D8'}
A_MID = 'P11 S7 F6'
A_CHUNK = {0: 'D9 P12', 1: 'S8 F7', 2: 'D10 F8', 3: 'S9 D11', 4: 'F9 S10', 5: 'D12 F10', 6: 'S11', 7: 'F11', 8: 'S12', 9: 'F12'}
A_SCATTER = {3: "B0", 4: "P0", 6: "D0 B1", 7: "P1", 8: "L0", 9: "B2 D1", 10: "P2", 11: "L1 F0"}
A_TAIL = ("D2", "F1", "L2", "", "F2")
B_HALF = {0: "P0", 1: "P1", 3: "D0 P2", 4: "D1", 5: "P3", 6: "D2 L0", 7: "P4 L1", 8: "D3", 9: "P5 L2 F0", 10: "D4 F1", 11: "P6 L3 F2"}
B_TABLE = {0: "P7 D5", 6: "L4 F3", 8: "D6", 12: "P8", 16: "L5 F4 D7", 20: "L6"}
B_NORM = ("F5 D8", "L7 F6", "", "L8")
T_NORM = ((), (0,), (1,), (2,))
B_TAIL = "F7 F8"
V_TABLE = {6: 0, 18: 1}
V_NORM = ((2,), (), (3,), ())


def spread(base, k, part, per):
    rows = lax.broadcasted_iota(jnp.int32, (part.shape[0], D), 0)
    lanes = lax.broadcasted_iota(jnp.int32, (part.shape[0], D), 1)
    full = mm(part, jnp.where(base == k, 1.0, 0.0).astype(bf16))
    return lambda first: jnp.sum(jnp.where(rows == first + lanes // per, full, 0.0), axis=0, keepdims=True)


def bias_at(h):
    return pl.ds(pl.multiple_of(h // 3 * IP, 8), IP), pl.multiple_of(lax.rem(h, 3) * IL, IL)


def head_bias(h, tab, idxT, bias_s):
    rowi = lax.broadcasted_iota(jnp.int32, (IP, 128), 0)
    rows, first = bias_at(h)
    for l in range(2):
        idx = idxT[:, pl.ds(l * 128, 128)]
        lo, hi = jnp.bitwise_and(idx, 127), jnp.right_shift(idx, 7)
        acc = jnp.zeros((IP, 128), f32)
        for k in range(6):
            t = jnp.broadcast_to(tab[h, k:k + 1, :], (IP, 128))
            acc = jnp.where(hi == k, jnp.take_along_axis(t, lo, axis=1, mode="promise_in_bounds"), acc)
        bias_s[rows, pl.ds(first + l * 128, 128)] = jnp.where(rowi < PATCH, acc, NEG)


def forward_half(p, s, ids_ref, q_s, k_s, v_s, att_s, bias_s, put):
    cols = pl.ds(pl.multiple_of(p * 128, 128), 128)
    lane = lax.broadcasted_iota(jnp.int32, (1, 128), 1)
    at = lambda image, n: pl.ds(pl.multiple_of(image * IP, IP), n * IP)
    linked = ids_ref[2 * s * PATCH] == ids_ref[(2 * s + 1) * PATCH]
    mx = jnp.where(jnp.logical_and(lax.broadcasted_iota(jnp.int32, (IP, 1), 0) < PATCH, linked), 0.0, NEG)
    kk = k_s[at(2 * s, 2), cols]
    vT = v_s[at(2 * s, 2), cols].T
    for a in range(2):
        q = q_s[at(2 * s + a, 1), cols]
        ats = []
        for h in range(2):
            qm = jnp.where((lane < 64) if h == 0 else (lane >= 64), q, jnp.zeros_like(q))
            st = mmt(kk, qm)
            rows_b, first = bias_at(2 * p + h)
            b = bias_s[rows_b, pl.ds(first, IL)][:, 0:IP]
            s0, s1 = (st[:IP] + b, st[IP:] + mx) if a == 0 else (st[:IP] + mx, st[IP:] + b)
            m = jnp.maximum(jnp.max(s0, axis=0, keepdims=True), jnp.max(s1, axis=0, keepdims=True))
            e0, e1 = jnp.exp(s0 - m), jnp.exp(s1 - m)
            inv = 1.0 / (jnp.sum(e0, axis=0, keepdims=True) + jnp.sum(e1, axis=0, keepdims=True))
            p0, p1 = (e0 * inv).astype(bf16), (e1 * inv).astype(bf16)
            put(a, h, 0, p0)
            put(a, h, 1, p1)
            v_h = vT[h * 64:(h + 1) * 64]
            ats.append(mm(v_h[:, :IP], p0) + mm(v_h[:, IP:], p1))
        att_s[at(2 * s + a, 1), cols] = jnp.concatenate(ats, axis=0).T.astype(bf16)


def at_step(i, run, plan):
    for when, text in plan.items():
        @pl.when(i == when)
        def _(text=text):
            run(text)


def fused_a_kernel(ni, nf, ids_ref, tok_ref, g_ref, tab_ref, idx_ref, *refs):
    smalls, refs = refs[:NVEC + 1], refs[NVEC + 1:]
    fused_a_body(ni, nf, smalls, ids_ref, tok_ref, g_ref, tab_ref, idx_ref, *refs)


def fused_a_body(ni, nf, smalls, ids_ref, tok_ref, g_ref, tab_ref, idx_ref, wq_ref, wo_ref, w1_ref, w2_ref,
                   out_ref, x_out, q_s, k_s, v_s, dres_ref, datt_ref, idx_out, dvec_ref, db1_ref, dwo_ref, vec, o1_ref,
                   wq_out, p_out, dw1_out, dw2_out,
                   gs, gq, go, g1, g2, tab, square, att_s, act, actT, dmlp, res, n2, branch, mlp, r2,
                   p_st, w2_st, b1, g_b, p_sem, w_sem, q_sem, h_sem, small_ref, *rest):
    R = ni * IP
    dact, gp = dres_ref, datt_ref
    z, y, x, c = place()
    blocks = [pltpu.make_async_copy(wq_ref.at[:, pl.ds(t * D + j * HG, HG)], gq.at[z, y, x, c, :, pl.ds(j * UW + t * HG, HG)], h_sem.at[j, t])
              for j in range(3) for t in range(3)]
    for d in blocks:
        d.start()
    met = greet()
    first = 0
    small_ref[...] = jnp.zeros_like(small_ref)
    for r in smalls:
        small_ref[0:1, first:first + r.shape[1]] = r[...].astype(f32)
        first += r.shape[1]
    tab[...] = jnp.zeros_like(tab)
    for k in range(6):
        n = min(128, tab_ref.shape[1] - k * 128)
        piece = tab_ref[:, k * 128:k * 128 + n].astype(f32)
        for h in range(HEADS):
            tab[h, k:k + 1, 0:n] = piece[h:h + 1]
    square[...] = jnp.zeros_like(square)
    square[0:PATCH, 0:PATCH] = idx_ref[...].astype(f32)
    idx_out[...] = square[...].T[0:IP].astype(jnp.int32)
    met()
    for d in blocks:
        d.wait()
    ga = Gather(gather_units((small_ref, wq_ref, wo_ref, w1_ref, w2_ref), (gs, gq, go, g1, g2)), *rest[:9])
    part_of = lambda j: lambda z, y, x, c: g_b.at[j, z, y, x, c]
    sc = Scatter([(part_of(j), owned(o1_ref, ALL, slice(j * UW, (j + 1) * UW))) for j in range(NA)], rest[9:15], rest[15:18])
    for a in range(len(ga.u)):
        ga.start(a)
    def padded(src, dst):
        res[pl.ds(0, ni * PATCH), :] = src[...].astype(f32)
        for i in range(ni):
            dst[pl.ds(i * IP, PATCH), :] = res[pl.ds(i * PATCH, PATCH), :].astype(bf16)
            dst[pl.ds(i * IP + PATCH, IP - PATCH), :] = jnp.zeros((IP - PATCH, D), bf16)
    def biases(first, last):
        def one(h, carry):
            head_bias(h, tab, idx_out, branch)
            return carry
        lax.fori_loop(first, last, one, 0)
    padded(tok_ref, x_out)
    ga.run(A_HEAD[0])
    for i in range(ni):
        rows = pl.ds(i * IP, IP)
        n2[rows, :], _ = ln_parts(x_out[rows, :].astype(f32))
    biases(0, 2)
    ga.run(A_HEAD[1])
    biases(2, 4)
    ga.run(A_HEAD[2])
    biases(4, 6)
    ga.run(A_HEAD[3])
    n_small = NZ * NY * NX * NC
    flat = gs.reshape(n_small * 8, 384)
    part = jnp.concatenate([flat[8 * d:8 * d + 1, :] for d in range(n_small)], axis=0).astype(bf16)
    per = D // n_small
    base = lax.broadcasted_iota(jnp.int32, (384, D), 0) - lax.rem(lax.broadcasted_iota(jnp.int32, (384, D), 1), per)
    for k in range(NVEC):
        vec[k:k + 1, :] = spread(base, k * per, part, per)(0)
    V = lambda k: vec[k:k + 1, :]
    for i in range(ni):
        rows = pl.ds(i * IP, IP)
        act[rows, :] = (n2[rows, :] * V(LN1G) + V(LN1B)).astype(bf16)
    ga.run(A_HEAD[4])
    biases(6, 9)
    ga.run(A_HEAD[5])
    padded(g_ref, gp)
    base1 = lax.broadcasted_iota(jnp.int32, (384, D), 0) - lax.rem(lax.broadcasted_iota(jnp.int32, (384, D), 1), 4 * per)
    sp = spread(base1, NVEC * per, part, 4 * per)
    for j in range(nf * FC // D):
        line = sp(j * (D // (4 * per)))
        for i in range(D // FC):
            b1[j * (D // FC) + i, 0:1, :] = line[:, i * FC:(i + 1) * FC]

    biases(9, 12)

    ns = ni // 2

    def half(t, carry):
        p, sq = t // ns, lax.rem(t, ns)
        at_step(t, ga.run, A_HALF)

        @pl.when(lax.rem(t, 2 * ns) == 0)
        def _():
            j = p // 2
            w = gq[:, :, :, :, :, pl.ds(pl.multiple_of(j * UW, UW), UW)].reshape(D, UW)
            cols = pl.ds(pl.multiple_of(j * HG, HG), HG)
            qb, vb = vec[QB:QB + 1, cols], vec[VB:VB + 1, cols]
            for i in range(ni):
                rows = pl.ds(i * IP, IP)
                o = mm(act[rows, :], w)
                q_s[rows, cols] = ((o[:, :HG] + qb) * HEAD ** -0.5).astype(bf16)
                k_s[rows, cols] = o[:, HG:2 * HG].astype(bf16)
                v_s[rows, cols] = (o[:, 2 * HG:] + vb).astype(bf16)

        slot = lax.rem(t, 2)
        st = p_st.at[slot]
        cp = pltpu.make_async_copy(st, p_out.at[p, sq], p_sem.at[slot])

        @pl.when(t >= 2)
        def _():
            pltpu.make_async_copy(st, p_out.at[p, sq], p_sem.at[slot]).wait()

        def put(a, h, b, v):
            st[a, h, b, :, 0:IP] = v
        forward_half(p, sq, ids_ref, q_s, k_s, v_s, att_s, branch, put)
        cp.start()
        return carry
    lax.fori_loop(0, HEADS // 2 * ns, half, 0)
    keep = pltpu.make_async_copy(gq, wq_out, q_sem.at[0])
    keep.start()
    ga.run(A_MID)

    sb = jnp.zeros((1, D), f32)
    wo = go[...].reshape(D, D)
    for i in range(ni):
        rows = pl.ds(i * IP, IP)
        br = mm(att_s[rows, :], wo) + V(OUTB)
        branch[rows, :] = br
        rs = x_out[rows, :].astype(f32) + V(GAM1) * br
        res[rows, :] = rs
        n, r = ln_parts(rs)
        n2[rows, :] = n
        r2[rows, :] = jnp.broadcast_to(r, (IP, 128))
        act[rows, :] = (n * V(LN2G) + V(LN2B)).astype(bf16)
        dm = V(GAM2) * gp[rows, :].astype(f32)
        sb = sb + jnp.sum(dm, axis=0, keepdims=True)
        dmlp[rows, :] = dm.astype(bf16)
    actT[...] = act[...].T
    dvec_ref[0:1, :] = sb
    mlp[...] = jnp.zeros_like(mlp)
    dact[...] = jnp.zeros_like(dact)
    g2v = g2.reshape(nf * FC, D)

    def chunk(c, carry):
        slot = lax.rem(c, 2)
        at = pl.multiple_of(c * FC, FC)
        at_step(c, ga.run, A_CHUNK)
        at_step(c, sc.run, A_SCATTER)
        w1, w2 = g1[:, :, :, :, :, pl.ds(at, FC)].reshape(D, FC), g2v[pl.ds(at, FC), :]
        cp = pltpu.make_async_copy(w2_st.at[slot], dw2_out.at[pl.ds(at, FC), :], w_sem.at[slot])
        pre = mm(act[...], w1) + b1[c, 0:1, :]
        cdf, xpdf = gelu_parts(pre)
        hid = (pre * cdf).astype(bf16)
        dp = mmt(dmlp[...], w2) * (cdf + xpdf)
        db1_ref[c, 0:1, :] = jnp.sum(dp, axis=0, keepdims=True)
        dpb = dp.astype(bf16)
        mlp[...] += mm(hid, w2)
        dact[...] += mmt(dpb, w1)

        @pl.when(c >= 2)
        def _():
            pltpu.make_async_copy(w2_st.at[slot], dw2_out.at[pl.ds(at, FC), :], w_sem.at[slot]).wait()
        g_b[c // (D // FC), :, :, :, :, :, pl.ds(pl.multiple_of(lax.rem(c, D // FC) * FC, FC), FC)] = mm(actT[...], dpb).astype(bf16).reshape(NZ, NY, NX, NC, PR, FC)
        w2_st[slot] = mm(hid.T, dmlp[...]).astype(bf16)
        cp.start()
        return carry
    lax.fori_loop(0, nf, chunk, 0)
    last = pltpu.make_async_copy(g_b.at[NA], dw1_out, q_sem.at[1])
    last.start()

    wo = go[...].reshape(D, D)
    sums = [jnp.zeros((1, D), f32) for _ in range(5)]
    for i in range(ni):
        rows = pl.ds(i * IP, IP)
        g = gp[rows, :].astype(f32)
        ml = mlp[rows, :] + V(FC2B)
        mlp[pl.ds(i * PATCH, PATCH), :] = (res[rows, :] + V(GAM2) * ml)[:PATCH]
        e, n = dact[rows, :], n2[rows, :]
        dn = e * V(LN2G)
        dr = g + r2[rows, 0:1] * (dn - jnp.mean(dn, axis=-1, keepdims=True) - n * jnp.mean(dn * n, axis=-1, keepdims=True))
        dres_ref[rows, :] = dr
        db = V(GAM1) * dr
        for k, t in enumerate((g * ml, e * n, e, dr * branch[rows, :], db)):
            sums[k] = sums[k] + jnp.sum(t, axis=0, keepdims=True)
        dbb = db.astype(bf16)
        dmlp[rows, :] = dbb
        datt_ref[rows, :] = mmt(dbb, wo).astype(bf16)
        sc.run(A_TAIL[i % 4])
    for k in range(5):
        dvec_ref[k + 1:k + 2, :] = sums[k]
    out_ref[...] = mlp[pl.ds(0, ni * PATCH), :].astype(bf16)
    dwo_ref[...] = mm(att_s[...].T, dmlp[...]).astype(bf16)
    keep.wait()
    last.wait()
    sc.run(A_TAIL[4])
    for slot in range(2):
        pltpu.make_async_copy(p_st.at[slot], p_out.at[0, 0], p_sem.at[slot]).wait()
        pltpu.make_async_copy(w2_st.at[slot], dw2_out.at[pl.ds(0, FC), :], w_sem.at[slot]).wait()


def fused_a(ids, tok, g, tab, idx, smalls, wq, wo, w1, w2, ni):
    R, F, S = ni * IP, w1.shape[1], jax.ShapeDtypeStruct
    v, hbm = vm(), pl.BlockSpec(memory_space=pl.ANY)
    small = S((8, 384), f32)
    six = lambda a: pltpu.VMEM((NZ, NY, NX, NC) + a.shape, a.dtype)
    row = lambda t: pltpu.VMEM((R, D), t)
    nu = 13
    bufs, s_sems = Scatter.scratch(NA)
    return pl.pallas_call(
        functools.partial(fused_a_kernel, ni, F // FC),
        in_specs=[pl.BlockSpec(memory_space=pltpu.SMEM)] + [v] * (5 + NVEC) + [hbm] * 4,
        out_shape=[S((ni * PATCH, D), bf16)] + [S((R, D), bf16)] * 4 + [S((R, D), f32), S((R, D), bf16), S((IP, IL), jnp.int32), S((8, D), f32), S((F // FC, 8, FC), f32),
                   S((D, D), bf16), S((16, D), f32), S((PR, NA * UW), f32), S((NZ, NY, NX, NC) + wq.shape, bf16), S((6, ni // 2, 2, 2, 2, IP, IL), bf16), S((NZ, NY, NX, NC, PR, UW), bf16), S((F, D), bf16)],
        out_specs=[v] * 13 + [hbm] * 4,
        scratch_shapes=[six(a) for a in (small, wq, wo, w1, w2)] + [pltpu.VMEM((HEADS, 8, 128), f32), pltpu.VMEM((IL, IL), f32), row(bf16), row(bf16),
                        pltpu.VMEM((D, R), bf16), row(bf16)] + [row(f32)] * 4 + [pltpu.VMEM((R, 128), f32), pltpu.VMEM((2, 2, 2, 2, IP, IL), bf16),
                        pltpu.VMEM((2, FC, D), bf16), pltpu.VMEM((F // FC, 8, FC), f32), pltpu.VMEM((NA + 1, NZ, NY, NX, NC, PR, UW), bf16), DMA((2,)), DMA((2,)), DMA((2,)), DMA((3, 3)), pltpu.VMEM((8, 384), f32)] + Gather.scratch(nu) + bufs + s_sems,
        compiler_params=pltpu.CompilerParams(collective_id=2, has_side_effects=True, vmem_limit_bytes=62 << 20), name="forward_and_mlp",
    )(ids, tok, g, tab, idx, *smalls, wq, wo, w1, w2)


def backward_half(p, s, q_ref, k_ref, v_ref, da_ref, probs, dqkv, dimg, dvec):
    lane = lax.broadcasted_iota(jnp.int32, (1, 128), 1)
    cols = pl.ds(pl.multiple_of(p * 128, 128), 128)
    at = lambda image, n: pl.ds(pl.multiple_of(image * IP, IP), n * IP)
    srow = at(2 * s, 2)
    kk, vv = k_ref[srow, cols], v_ref[srow, cols]
    kT = kk.T
    sq = jnp.zeros((1, 128), f32)
    dv, dk = jnp.zeros((2 * IP, 128), f32), jnp.zeros((2 * IP, 128), f32)
    for a in range(2):
        rows = at(2 * s + a, 1)
        q, da = q_ref[rows, cols], da_ref[rows, cols]
        dqs = []
        for h in range(2):
            msk = (lane < 64) if h == 0 else (lane >= 64)
            qm, dam = jnp.where(msk, q, jnp.zeros_like(q)), jnp.where(msk, da, jnp.zeros_like(da))
            pb0, pb1 = probs(a, h, 0), probs(a, h, 1)
            dp = mmt(vv, dam)
            t0, t1 = pb0.astype(f32) * dp[:IP], pb1.astype(f32) * dp[IP:]
            dl = jnp.sum(t0, axis=0, keepdims=True) + jnp.sum(t1, axis=0, keepdims=True)
            d0, d1 = t0 - pb0.astype(f32) * dl, t1 - pb1.astype(f32) * dl
            dimg[2 * p + h, :, 0:IP] += d0 if a == 0 else d1
            ds = jnp.concatenate([d0.astype(bf16), d1.astype(bf16)], axis=0)
            dv = dv + mm(jnp.concatenate([pb0, pb1], axis=0), dam)
            dk = dk + mm(ds, qm)
            dqs.append(mm(kT[h * 64:(h + 1) * 64], ds))
        dq = jnp.concatenate(dqs, axis=0).T * HEAD ** -0.5
        sq = sq + jnp.sum(dq, axis=0, keepdims=True)
        dqkv[0][rows, cols] = dq.astype(bf16)
    dqkv[1][srow, cols] = dk.astype(bf16)
    dqkv[2][srow, cols] = dv.astype(bf16)
    dvec[QB:QB + 1, cols] += sq
    dvec[VB:VB + 1, cols] += jnp.sum(dv, axis=0, keepdims=True)


def table_step(t, dimg, idx_ref, acc):
    sub8 = lax.broadcasted_iota(jnp.int32, (8, IL), 0)
    sub128 = lax.broadcasted_iota(jnp.int32, (128, IL), 0)
    at = pl.multiple_of(t * 8, 8)
    ix = idx_ref[pl.ds(at, 8), :]
    lo, hi = jnp.bitwise_and(ix, 127), jnp.right_shift(ix, 7)
    ds = [dimg[h, pl.ds(at, 8), :] for h in range(HEADS)]
    left, right = [], []
    for j in range(8):
        right.append(jnp.where(sub128 == lo[j:j + 1], 1.0, 0.0).astype(bf16))
        hm = sub8 == hi[j:j + 1]
        left.append(jnp.concatenate([jnp.where(hm, jnp.broadcast_to(d[j:j + 1], (8, IL)), 0.0) for d in ds], axis=0))
    left = jnp.concatenate(left, axis=1)
    high = left.astype(bf16)
    low = (left - high.astype(f32)).astype(bf16)
    acc[...] += mmt(jnp.concatenate([high, low], axis=0), jnp.concatenate(right, axis=1))


def fused_b_kernel(ni, table_rows, dvec_a, db1, x_ref, dres, q_ref, k_ref, v_ref, da_ref, vec, idx_ref, wq_hbm, p_hbm, d1_hbm, d2_hbm, do_hbm,
                   dtok_ref, table_ref, own_vec, own_b1, oq, oo, o1, o2,
                   wq, dq, dk, dv, dimg, act, actT, dwq, acc, tot_t, tot_a, tot_b, p_st, p_sem, w_sem, *rest):
    bufs, sems, ta, tb, tt = rest[:6], rest[6:9], rest[9:12], rest[12:15], rest[15:18]
    met = greet([across()])
    V = lambda k: vec[k:k + 1, :]
    for i in range(ni):
        rows = pl.ds(i * IP, IP)
        n, _ = ln_parts(x_ref[rows, :].astype(f32))
        act[rows, :] = (n * V(LN1G) + V(LN1B)).astype(bf16)
    actT[...] = act[...].T
    met()
    sc = Scatter(scatter_units((dwq, do_hbm, d1_hbm, d2_hbm), (oq, oo, o1, o2)), bufs, sems)
    for a in range(NB):
        if a not in HEAD_UNITS:
            sc.start(a)
    load = pltpu.make_async_copy(wq_hbm, wq, w_sem)
    load.start()
    ns = ni // 2
    fetch = lambda t: pltpu.make_async_copy(p_hbm.at[t // ns, lax.rem(t, ns)], p_st.at[lax.rem(t, 2)], p_sem.at[lax.rem(t, 2)])
    fetch(0).start()
    tot_a[...] = jnp.zeros_like(tot_a)
    tot_b[...] = jnp.zeros_like(tot_b)
    for k, r in ((FC2B, 0), (GAM2, 1), (LN2G, 2), (LN2B, 3), (GAM1, 4), (OUTB, 5)):
        tot_a[k:k + 1, :] = dvec_a[r:r + 1, :]
    nb = NA + 1
    for j in range(nb):
        for i in range(D // FC):
            tot_a[NVEC + j:NVEC + j + 1, i * FC:(i + 1) * FC] = db1[j * (D // FC) + i, 0:1, :]
    dimg[...] = jnp.zeros_like(dimg)

    def half(t, carry):
        p, sq = t // ns, lax.rem(t, ns)
        fetch(t).wait()

        @pl.when(t + 1 < HEADS // 2 * ns)
        def _():
            fetch(t + 1).start()
        st = p_st.at[lax.rem(t, 2)]
        at_step(t, sc.run, B_HALF)
        backward_half(p, sq, q_ref, k_ref, v_ref, da_ref, lambda a, h, b: st[a, h, b, :, 0:IP], (dq, dk, dv), dimg, tot_a)

        @pl.when(lax.rem(t, 2 * ns) == 2 * ns - 1)
        def _():
            j = p // 2
            for n, d in enumerate((dq, dk, dv)):
                part = mm(actT[...], d[:, pl.ds(pl.multiple_of(j * HG, HG), HG)]).astype(bf16)
                dwq[:, :, :, :, :, pl.ds(pl.multiple_of(j * UW + n * HG, HG), HG)] = part.reshape(NZ, NY, NX, NC, PR, HG)
        at_step(t, sc.run, {(j + 1) * 2 * ns - 1: "B%d" % a for j, a in enumerate(HEAD_UNITS)})
        return carry
    lax.fori_loop(0, HEADS // 2 * ns, half, 0)
    t_a = Total(tot_a, Total.pairs(), *ta)
    t_a.start()
    acc[...] = jnp.zeros_like(acc)

    def table(t, carry):
        table_step(t, dimg, idx_ref, acc)
        at_step(t, sc.run, B_TABLE)
        at_step(t, t_a.step, V_TABLE)
        return carry
    lax.fori_loop(0, -(-PATCH // 8), table, 0)
    tot_t[...] = acc[0:96, :] + acc[96:192, :]
    t_t = Total(tot_t, Total.pairs(), *tt)
    t_t.start()
    load.wait()
    w = wq
    sg, sb = jnp.zeros((1, D), f32), jnp.zeros((1, D), f32)
    for i in range(ni):
        rows = pl.ds(i * IP, IP)
        e = jnp.zeros((IP, D), f32)
        for j in range(3):
            left = jnp.concatenate([d[rows, j * HG:(j + 1) * HG] for d in (dq, dk, dv)], axis=1)
            e = e + mmt(left, w[:, j * UW:(j + 1) * UW])
        n, r = ln_parts(x_ref[rows, :].astype(f32))
        dn = e * V(LN1G)
        dx = dres[rows, :] + r * (dn - jnp.mean(dn, axis=-1, keepdims=True) - n * jnp.mean(dn * n, axis=-1, keepdims=True))
        dres[pl.ds(i * PATCH, PATCH), :] = dx[:PATCH]
        sg = sg + jnp.sum(e * n, axis=0, keepdims=True)
        sb = sb + jnp.sum(e, axis=0, keepdims=True)
        sc.run(B_NORM[i % 4])
        for k in T_NORM[i % 4]:
            t_t.step(k)
        for k in V_NORM[i % 4]:
            t_a.step(k)
    tot_b[LN1G:LN1G + 1, :] = sg
    tot_b[LN1B:LN1B + 1, :] = sb
    t_b = Total(tot_b, Total.groups(), *tb)
    t_b.start()
    dtok_ref[...] = dres[pl.ds(0, ni * PATCH), :].astype(bf16)
    t_a.step(4)
    t_b.step(0)
    t_t.step(3)
    t_b.step(1)
    sc.run(B_TAIL)
    t_b.step(2)
    t_t.step(4)
    tot_a[LN1G:LN1B + 1, :] = tot_b[LN1G:LN1B + 1, :]

    z, y, x, c = place()
    me = ((z * NY + y) * NX + x) * NC + c
    per = D // (NZ * NY * NX * NC)
    def pick(rows, first, width):
        one = jnp.where(lax.broadcasted_iota(jnp.int32, (D, 128), 0) == first + lax.broadcasted_iota(jnp.int32, (D, 128), 1), 1.0, 0.0).astype(bf16)
        h = rows.astype(bf16)
        m = (rows - h.astype(f32)).astype(bf16)
        l = (rows - h.astype(f32) - m.astype(f32)).astype(bf16)
        return mm(h, one) + mm(m, one) + mm(l, one)
    own_vec[...] = pick(tot_a[0:16, :], me * per, per)
    wide = nb * per
    slab = me // (D // wide)
    part = pick(tot_a[8:16, :], lax.rem(me, D // wide) * wide, wide)
    rowi = lax.broadcasted_iota(jnp.int32, (8, 128), 0)
    own_b1[...] = jnp.broadcast_to(jnp.sum(jnp.where(rowi == slab + NVEC - 8, part, 0.0), axis=0, keepdims=True), (8, 128))
    for r in range(96):
        if r % 8 < 6:
            n = min(128, table_rows - r % 8 * 128)
            table_ref[r // 8:r // 8 + 1, (r % 8) * 128:(r % 8) * 128 + n] = tot_t[r:r + 1, 0:n]


def fused_b(dvec_a, db1, x, dres, q, k, v, da, vec, idx, wq6, p, d1, d2, do, table_rows, ni):
    R, S = ni * IP, jax.ShapeDtypeStruct
    vmem, hbm = vm(), pl.BlockSpec(memory_space=pl.ANY)
    split = lambda a: a.reshape((NZ, NY, NX, NC, -1, a.shape[-1]))
    d2, do = split(d2), split(do)
    own = lambda a: S(a.shape[-2:], f32)
    bufs, sems = Scatter.scratch(NB)
    row = lambda t: pltpu.VMEM((R, D), t)
    return pl.pallas_call(
        functools.partial(fused_b_kernel, ni, table_rows),
        in_specs=[vmem] * 10 + [hbm] * 5,
        out_shape=[S((ni * PATCH, D), bf16), S((HEADS, table_rows), f32), S((16, 128), f32), S((8, 128), f32), own(wq6), own(do), own(d1), own(d2)],
        out_specs=[vmem] * 8,
        scratch_shapes=[pltpu.VMEM((D, 3 * D), bf16)] + [row(bf16)] * 3 + [pltpu.VMEM((HEADS, IP, IL), f32), row(bf16), pltpu.VMEM((D, R), bf16), pltpu.VMEM(wq6.shape, bf16),
                        pltpu.VMEM((192, 128), f32), pltpu.VMEM((96, 128), f32), pltpu.VMEM((16, D), f32), pltpu.VMEM((2, D), f32),
                        pltpu.VMEM((2, 2, 2, 2, IP, IL), bf16), DMA((2,)), DMA] + bufs + sems + Total.scratch(5, 16, D) + Total.scratch(7, 2, D) + Total.scratch(5, 96, 128),
        compiler_params=pltpu.CompilerParams(collective_id=3, has_side_effects=True, vmem_limit_bytes=62 << 20), name="attention_backward",
    )(dvec_a, db1, x, dres, q, k, v, da, vec, idx, wq6.reshape(D, 3 * D), p, d1, d2, do)


def place_kernel(per, wide, out, dtok, table, vecs, b1, oq, oo, o1a, o1b, o2, *outs):
    for a, b in ((out, outs[0]), (dtok, outs[1]), (table, outs[2]), (oq, outs[3]), (oo, outs[4]), (o2, outs[6])):
        b[...] = a[...]
    outs[5][:, 0:o1a.shape[1]] = o1a[...]
    outs[5][:, o1a.shape[1]:] = o1b[...]
    outs[7][...] = b1[0:1, 0:wide]
    for k in range(NVEC):
        outs[8 + k][...] = vecs[k:k + 1, 0:per]


def place_outputs(out, dtok, table, vecs, b1, oq, oo, o1a, o1b, o2, per, wide):
    S = jax.ShapeDtypeStruct
    like = lambda a: S(a.shape, a.dtype)
    return pl.pallas_call(
        functools.partial(place_kernel, per, wide),
        in_specs=[vm()] * 10,
        out_shape=[like(out), like(dtok), like(table), like(oq), like(oo), S((PR, o1a.shape[1] + o1b.shape[1]), f32), like(o2), S((1, wide), f32)] + [S((1, per), f32)] * NVEC,
        out_specs=[vm()] * (8 + NVEC),
        compiler_params=pltpu.CompilerParams(vmem_limit_bytes=60 << 20), name="place_outputs",
    )(out, dtok, table, vecs, b1, oq, oo, o1a, o1b, o2)


def pad_rows(a, ni):
    return jnp.pad(a.reshape(ni, PATCH, D), ((0, 0), (0, IP - PATCH), (0, 0))).reshape(ni * IP, D)


def unpad_rows(a, ni):
    return a.reshape(ni, IP, D)[:, :PATCH].reshape(ni * PATCH, D)


def local(tokens, image_ids, rel_index, rel_table, ln1_gain, ln1_bias, w_qkv, q_bias, v_bias, w_out, out_bias, gamma1,
          ln2_gain, ln2_bias, w_fc1, fc1_bias, w_fc2, fc2_bias, gamma2, out_grad):
    ni = tokens.shape[0] // PATCH
    per = ln1_gain.shape[0]
    n_dev = D // per
    small = jnp.concatenate([ln1_gain, ln1_bias, q_bias, v_bias, out_bias, gamma1, ln2_gain, ln2_bias, fc2_bias, gamma2, fc1_bias])
    me = lax.axis_index("gx") * lax.axis_size("gy") + lax.axis_index("gy")
    if (lax.axis_size("gx"), lax.axis_size("gy"), per) == (NZ * NY, NX * NC, PR):
        smalls = [a.reshape(1, -1) for a in (ln1_gain, ln1_bias, q_bias, v_bias, out_bias, gamma1, ln2_gain, ln2_bias, fc2_bias, gamma2, fc1_bias)]
        res = fused_a(image_ids, tokens, out_grad, rel_table.T, rel_index, smalls, w_qkv, w_out, w_fc1, w_fc2, ni)
        out, x, q, k, v, dres, datt, idx, dvec, db1, dwo, vec, g1, wq6, p, dw1, dw2 = res
        dtok, table_grad, own_vec, own_b1, gq, go, g1b, g2 = fused_b(dvec, db1, x, dres, q, k, v, datt, vec, idx, wq6, p, dw1, dw2, dwo, rel_table.shape[0], ni)
        res = place_outputs(out, dtok, table_grad, own_vec, own_b1, gq, go, g1, g1b, g2, per, fc1_bias.shape[0])
        out, dtok, table_grad, gq, go, g1, g2, b1 = res[:8]
        sl = [a.reshape(-1) for a in res[8:]]
        return (out, dtok, table_grad.T, sl[LN1G], sl[LN1B], gq, sl[QB], sl[VB], go, sl[OUTB], sl[GAM1], sl[LN2G], sl[LN2B], g1,
                b1.reshape(-1), g2, sl[FC2B], sl[GAM2])
    gather = lambda a: lax.all_gather(a, AXES, axis=0, tiled=True)
    wq, wo, w1, w2 = gather(w_qkv), gather(w_out), gather(w_fc1), gather(w_fc2)
    small = lax.all_gather(small, AXES, axis=0, tiled=False).reshape(n_dev, -1).astype(f32)
    vec = jnp.pad(jnp.transpose(small[:, : NVEC * per].reshape(n_dev, NVEC, per), (1, 0, 2)).reshape(NVEC, D), ((0, 16 - NVEC), (0, 0)))
    b1 = small[:, NVEC * per :].reshape(1, -1)

    x = pad_rows(tokens, ni)
    g = pad_rows(out_grad, ni)
    ids = image_ids.reshape(ni, PATCH)[:, 0]
    table_rows = rel_table.shape[0]
    tab = jnp.pad(rel_table.astype(f32).T, ((0, 0), (0, 768 - table_rows))).reshape(6, 2, 6, 128)
    idx = jnp.pad(rel_index.T, ((0, IP - PATCH), (0, IL - PATCH)))

    att, q, k, v, p = front(ids, x, wq, tab, idx, vec, ni)
    out, dres, datt, dw1, dw2, dwo, db1, dvec = mlp(x, att, g, wo, vec, w1, w2, b1, ni)
    dq, dk, dv, dimg, dvec2 = attb(q, k, v, datt, p, ni)
    dtok, dwq, dvec3, dtab = qkvb(x, dres, dq, dk, dv, wq, vec, dimg, idx, ni)

    scatter = lambda a: lax.psum_scatter(a.astype(f32), AXES, scatter_dimension=0, tiled=True)
    rows = jnp.concatenate([dvec3[0:2], dvec2[0:2], dvec[5:6], dvec[4:5], dvec[2:4], dvec[0:1], dvec[1:2], db1.reshape(-1, D), dtab.reshape(-1, D)])
    total = lax.psum(rows, AXES)
    sl = [lax.dynamic_slice(total[i], (me * per,), (per,)) for i in range(NVEC)]
    nb = db1.shape[1] // D
    db1_own = lax.dynamic_slice(total[NVEC : NVEC + nb].reshape(-1), (me * per * nb,), (per * nb,))
    table_grad = total[NVEC + nb :].reshape(HEADS, 1024)[:, :table_rows].T
    return (unpad_rows(out, ni), unpad_rows(dtok, ni), table_grad, sl[LN1G], sl[LN1B], scatter(dwq), sl[QB], sl[VB], scatter(dwo),
            sl[OUTB], sl[GAM1], sl[LN2G], sl[LN2B], scatter(dw1), db1_own, scatter(dw2), sl[FC2B], sl[GAM2])


def solution(mesh):
    rows, vecs, none = P(AXES, None), P(AXES), P()
    return jax.shard_map(
        local,
        mesh=mesh,
        in_specs=(rows, vecs, none, none, vecs, vecs, rows, vecs, vecs, rows, vecs, vecs, vecs, vecs, rows, vecs, rows, vecs, vecs, rows),
        out_specs=(rows, rows, none, vecs, vecs, rows, vecs, vecs, rows, vecs, vecs, vecs, vecs, rows, vecs, rows, vecs, vecs),
        check_vma=False,
    )
```
